128 devices in a mesh: lat: 8 (over y_hi, z), lon: 16 (over x, y_lo, core).
Axes of the slice: x: 4, y: 4 (y_hi: 2, y_lo: 2; y = y_hi * 2 + y_lo), z: 4, core: 2. Of those that a mesh axis runs over, the one named last changes fastest.
Arguments:
- tokens: bfloat16 [192, 768, 512], P('lat', 'lon'), may hold values from -8 to 8
- lat_band: int32 [192], replicated, may hold values from 0 to 15, as said below
- gain_attn: float32 [512], replicated, may hold values from 0.1 to 1.9
- w_qkv: bfloat16 [512, 1536], replicated, may hold values from -1.5 to 1.5
- w_out: bfloat16 [512, 512], replicated, may hold values from -0.25 to 0.25
- gain_merge: float32 [2048], replicated, may hold values from 0.1 to 1.9
- w_merge: bfloat16 [2048, 1024], replicated, may hold values from -0.125 to 0.125
- grad_merged: bfloat16 [96, 384, 1024], P('lat', 'lon'), may hold values from -6 to 6
Outputs:
- merged: bfloat16 [96, 384, 1024], P('lat', 'lon')
- grad_tokens: float32 [192, 768, 512], P('lat', 'lon')
- grad_gain_attn: float32 [512], replicated
- grad_w_qkv: float32 [512, 1536], replicated
- grad_w_out: float32 [512, 512], replicated
- grad_gain_merge: float32 [2048], replicated
- grad_w_merge: float32 [2048, 1024], replicated
The draws below stay inside these ranges and needn't reach their ends.
Inputs may be any that keep to these rules, and one draw needn't show every extreme that they name: `lat_band`: band number of each latitude row; it never falls from one row to the next, and every band holds at least one row.
All inputs are finite; a program needn't handle non-finite values.
Results may differ from the reference program's by a relative error of at most 0.025.
Values may be sent and summed in bfloat16 or wider, within the bound.
A program may use at most 192 MiB of HBM per device.

```python
import jax
import jax.numpy as jnp
from jax import lax

C1 = 512
C2 = 1024
HEADS = 8
WLAT = 6
WLON = 12
NLAT = 192
NLON = 768


def draw_lat_band(key, part):
    band_total = max(2, NLAT // 12)
    order = jax.random.permutation(jax.random.fold_in(key, 31), NLAT - 1).astype(jnp.int32) + 1
    cut_rows = order[:band_total - 1]
    row_ids = jnp.arange(NLAT, dtype=jnp.int32)
    above = (row_ids[:, None] >= cut_rows[None, :]).astype(jnp.int32)
    return jnp.sum(above, axis=1).astype(jnp.int32)


def draw_tokens(key, part):
    values = jnp.clip(jax.random.normal(jax.random.fold_in(key, 11), (NLAT, NLON, C1), jnp.float32), -6.0, 6.0)
    return values.astype(jnp.bfloat16)


def draw_w_qkv(key, part):
    scale = C1 ** (-0.5)
    values = jnp.clip(jax.random.normal(jax.random.fold_in(key, 21), (C1, 3 * C1), jnp.float32), -6.0, 6.0) * scale
    return values.astype(jnp.bfloat16)


def level_of(rng, extent, pieces, smallest, top_value):
    factor_of, own = 1.0, jax.random.fold_in(rng, 6)
    for dim, parts in pieces:
        draws = jnp.exp(jax.random.uniform(jax.random.fold_in(own, dim), (parts,), jnp.float32, smallest / len(pieces), top_value / len(pieces)))
        factor_of = factor_of * jnp.repeat(draws, extent[dim] // parts).reshape([-1 if axis == dim else 1 for axis in range(len(extent))])
    return factor_of


def centred(key, dims, scale, most, shards=(), kind=jnp.bfloat16):
    values = scale * jax.random.normal(key, dims, jnp.float32)
    if shards:
        values = values * level_of(key, dims, shards, -0.22, 0.18)
    return jnp.clip(values, -most, most).astype(kind)


def setup_inputs(seed: int = 0) -> dict:
    keys = jax.random.split(jax.random.key(seed), 9)
    tokens = draw_tokens(jax.random.fold_in(keys[8], 71), 0)
    lat_band = draw_lat_band(jax.random.fold_in(keys[8], 71), 0)
    gain_attn = jnp.clip(1.0 + 0.18 * jax.random.normal(keys[2], (C1,), jnp.float32), 0.1, 1.9)
    w_qkv = draw_w_qkv(jax.random.fold_in(keys[8], 71), 0)
    w_out = centred(keys[4], (C1, C1), C1 ** -0.5, 0.25)
    gain_merge = jnp.clip(1.0 + 0.18 * jax.random.normal(keys[5], (4 * C1,), jnp.float32), 0.1, 1.9)
    w_merge = centred(keys[6], (4 * C1, C2), (4 * C1) ** -0.5, 0.125)
    grad_merged = centred(keys[7], (NLAT // 2, NLON // 2, C2), 1.0, 6.0, ((0, 8), (1, 16)))
    return dict(tokens=tokens, lat_band=lat_band, gain_attn=gain_attn, w_qkv=w_qkv, w_out=w_out, gain_merge=gain_merge, w_merge=w_merge, grad_merged=grad_merged)


EPSILON = 1e-05

def normalize(values, gain_vec):
    average = lax.optimization_barrier(jnp.mean(values, axis=-1, keepdims=True))
    centered = values - average
    variance = lax.optimization_barrier(jnp.mean(centered * centered, axis=-1, keepdims=True))
    return centered * lax.rsqrt(variance + EPSILON) * gain_vec

def windows_attend(qkv_grid, band_rows, head_count):
    grid_rows, grid_cols, triple = qkv_grid.shape
    features = triple // 3
    head_size = features // head_count
    count_a = grid_rows // WLAT
    count_b = grid_cols // WLON
    window_size = WLAT * WLON
    blocks = qkv_grid.reshape(count_a, WLAT, count_b, WLON, 3, head_count, head_size)
    blocks = blocks.transpose(4, 0, 2, 5, 1, 3, 6).reshape(3, count_a, count_b, head_count, window_size, head_size)
    queries = blocks[0].astype(jnp.float32)
    key_rows = blocks[1].astype(jnp.float32)
    value_rows = blocks[2].astype(jnp.float32)
    scores = jnp.einsum('abhqd,abhkd->abhqk', queries, key_rows) * head_size ** (-0.5)
    labels = jnp.repeat(band_rows.reshape(count_a, WLAT), WLON, axis=1)
    allowed = labels[:, :, None] == labels[:, None, :]
    scores = jnp.where(allowed[:, None, None, :, :], scores, -1e+30)
    attn_weights = jax.nn.softmax(scores, axis=-1).astype(jnp.bfloat16)
    attn_out = jnp.einsum('abhqk,abhkd->abhqd', attn_weights.astype(jnp.float32), value_rows).astype(jnp.bfloat16)
    attn_out = attn_out.reshape(count_a, count_b, head_count, WLAT, WLON, head_size)
    return attn_out.transpose(0, 3, 1, 4, 2, 5).reshape(grid_rows, grid_cols, features)

def merge_groups(mixed_tokens):
    grid_rows, grid_cols, features = mixed_tokens.shape
    grouped = mixed_tokens.reshape(grid_rows // 2, 2, grid_cols // 2, 2, features).transpose(0, 2, 3, 1, 4)
    return grouped.reshape(grid_rows // 2, grid_cols // 2, 4 * features)

def reference(tokens, lat_band, gain_attn, w_qkv, w_out, gain_merge, w_merge, grad_merged):
    features = tokens.shape[2]
    half_lat = WLAT // 2
    half_lon = WLON // 2
    inputs = tokens.astype(jnp.float32)

    def section_one(values, gain_vec):
        return normalize(values, gain_vec).astype(jnp.bfloat16)
    normed, first_back = jax.vjp(section_one, inputs, gain_attn)
    flat_normed = normed.reshape(-1, features)
    qkv_grid = jnp.dot(flat_normed, w_qkv, preferred_element_type=jnp.float32).astype(jnp.bfloat16)
    qkv_grid = qkv_grid.reshape(NLAT, NLON, 3 * features)
    rolled = jnp.roll(qkv_grid, (-half_lat, -half_lon), (0, 1))
    band_rows = jnp.roll(lat_band, -half_lat)

    def section_two(values):
        return windows_attend(values, band_rows, HEADS)
    attended, second_back = jax.vjp(section_two, rolled)
    attended = jnp.roll(attended, (half_lat, half_lon), (0, 1))
    flat_att = attended.reshape(-1, features)
    projected = jnp.dot(flat_att, w_out, preferred_element_type=jnp.float32).reshape(NLAT, NLON, features)
    mixed_tokens = (inputs + projected).astype(jnp.bfloat16)

    def section_three(values, gain_vec):
        return normalize(merge_groups(values).astype(jnp.float32), gain_vec).astype(jnp.bfloat16)
    merged_in, third_back = jax.vjp(section_three, mixed_tokens, gain_merge)
    flat_in = merged_in.reshape(-1, 4 * features)
    flat_grad = grad_merged.reshape(-1, grad_merged.shape[2])
    merged = jnp.dot(flat_in, w_merge, preferred_element_type=jnp.float32).astype(jnp.bfloat16).reshape(grad_merged.shape)
    grad_w_merge = jnp.dot(flat_in.T, flat_grad, preferred_element_type=jnp.float32)
    grad_in = jnp.dot(flat_grad, w_merge.T, preferred_element_type=jnp.float32).astype(jnp.bfloat16).reshape(merged_in.shape)
    grad_mixed, grad_gain_merge = third_back(grad_in)
    flat_mixed = grad_mixed.reshape(-1, features)
    grad_w_out = jnp.dot(flat_att.T, flat_mixed, preferred_element_type=jnp.float32)
    grad_att = jnp.dot(flat_mixed, w_out.T, preferred_element_type=jnp.float32).astype(jnp.bfloat16)
    grad_att = grad_att.reshape(NLAT, NLON, features)
    grad_rolled, = second_back(jnp.roll(grad_att, (-half_lat, -half_lon), (0, 1)))
    grad_qkv = jnp.roll(grad_rolled, (half_lat, half_lon), (0, 1)).reshape(-1, 3 * features)
    grad_w_qkv = jnp.dot(flat_normed.T, grad_qkv, preferred_element_type=jnp.float32)
    grad_normed = jnp.dot(grad_qkv, w_qkv.T, preferred_element_type=jnp.float32).astype(jnp.bfloat16)
    grad_inputs, grad_gain_attn = first_back(grad_normed.reshape(NLAT, NLON, features))
    grad_tokens = grad_inputs + grad_mixed.astype(jnp.float32)
    return (merged, grad_tokens, grad_gain_attn, grad_w_qkv, grad_w_out, grad_gain_merge, grad_w_merge)
```

```python
import functools
import jax
import jax.numpy as jnp
from jax import lax
from jax.experimental import pallas as pl
from jax.experimental.pallas import tpu as pltpu
from jax.sharding import PartitionSpec as P

HEADS = 8
WLAT = 6
WLON = 12
EPSILON = 1e-05
F32 = jnp.float32
BF = jnp.bfloat16
ROWS = 24
COLS = 48
C = 512
WIN = 72
NW = COLS // WLON
PAIRS = HEADS // 2
MIB = 1 << 20


def dot(a, b, ca, cb):
    return lax.dot_general(a, b, (((ca,), (cb,)), ((), ())), preferred_element_type=F32)


def head_masks(scale):
    lane = lax.broadcasted_iota(jnp.int32, (1, 128), 1)
    low = jnp.where(lane < 64, scale, 0.0).astype(F32)
    high = jnp.where(lane < 64, 0.0, scale).astype(F32)
    return low, high


def stacked(value, masks):
    return jnp.concatenate([value * masks[0], value * masks[1]], axis=0).astype(BF)


def merged_heads(value):
    lane = lax.broadcasted_iota(jnp.int32, (WIN, 128), 1)
    return jnp.where(lane < 64, value[:WIN], value[WIN:])


def to_windows(src, dst):
    for v in range(NW):
        for r in range(WLAT):
            dst[v, WLON * r : WLON * (r + 1), :] = src[r, WLON * v : WLON * (v + 1), :]


def to_grid(src, dst):
    for v in range(NW):
        for r in range(WLAT):
            dst[r, WLON * v : WLON * (v + 1), :] = src[v, WLON * r : WLON * (r + 1), :]


def moments(x):
    mean = jnp.mean(x, axis=-1, keepdims=True)
    centered = x - mean
    var = jnp.mean(centered * centered, axis=-1, keepdims=True)
    rstd = lax.rsqrt(var + EPSILON)
    return centered * rstd, rstd


def attend_fwd(tok_ref, bias_ref, gain_ref, w_ref, att_ref, qkv_ref, prob_ref, normed_ref, s1, s2, qf):
    xhat, _ = moments(tok_ref[...].astype(F32))
    s1[...] = xhat * gain_ref[...].reshape(1, 1, C)
    to_windows(s1, s2)
    normed = s2[...].reshape(NW * WIN, C).astype(BF)
    normed_ref[...] = normed
    for t in range(3):
        part = dot(normed, w_ref[:, C * t : C * (t + 1)], 1, 0).reshape(NW, WIN, C)
        if t == 0:
            qf[...] = part
        qkv_ref[:, :, C * t : C * (t + 1)] = part.astype(BF)
    bias = bias_ref[0]

    def window(v, carry):
        masks = head_masks(0.125)
        for p in range(PAIRS):
            lanes = slice(128 * p, 128 * (p + 1))
            qs = stacked(qf[v, :, lanes].astype(BF).astype(F32), masks)
            k = qkv_ref[v, :, C + 128 * p : C + 128 * (p + 1)]
            val = qkv_ref[v, :, 2 * C + 128 * p : 2 * C + 128 * (p + 1)]
            s = dot(k, qs, 1, 1) + bias
            e = jnp.exp(s - jnp.max(s, axis=0, keepdims=True))
            prob = (e * (1.0 / jnp.sum(e, axis=0, keepdims=True))).astype(BF)
            prob_ref[v, p] = prob
            s2[v, :, lanes] = merged_heads(dot(prob, val, 0, 0))
        return carry

    lax.fori_loop(0, NW, window, 0)
    to_grid(s2, s1)
    att_ref[...] = s1[...].astype(BF)


def attention_forward(tokens, bias, gain, w_qkv):
    steps = ROWS // WLAT
    return pl.pallas_call(
        attend_fwd,
        grid=(steps,),
        in_specs=[
            pl.BlockSpec((WLAT, COLS, C), lambda i: (i, 0, 0)),
            pl.BlockSpec((1, WIN, 2 * WIN), lambda i: (i, 0, 0)),
            pl.BlockSpec((1, C), lambda i: (0, 0)),
            pl.BlockSpec((C, 3 * C), lambda i: (0, 0)),
        ],
        out_specs=[
            pl.BlockSpec((WLAT, COLS, C), lambda i: (i, 0, 0)),
            pl.BlockSpec((NW, WIN, 3 * C), lambda i: (i, 0, 0)),
            pl.BlockSpec((NW, PAIRS, WIN, 2 * WIN), lambda i: (i, 0, 0, 0)),
            pl.BlockSpec((NW * WIN, C), lambda i: (i, 0)),
        ],
        out_shape=[
            jax.ShapeDtypeStruct((ROWS, COLS, C), BF),
            jax.ShapeDtypeStruct((steps * NW, WIN, 3 * C), BF),
            jax.ShapeDtypeStruct((steps * NW, PAIRS, WIN, 2 * WIN), BF),
            jax.ShapeDtypeStruct((ROWS * COLS, C), BF),
        ],
        scratch_shapes=[
            pltpu.VMEM((WLAT, COLS, C), F32),
            pltpu.VMEM((NW, WIN, C), F32),
            pltpu.VMEM((NW, WIN, C), F32),
        ],
        compiler_params=pltpu.CompilerParams(vmem_limit_bytes=40 * MIB),
        name="attend_fwd",
    )(tokens, bias, gain, w_qkv)


def attend_bwd(tok_ref, gatt_ref, qkv_ref, prob_ref, normed_ref, gain_ref, w_ref,
               gin_ref, gw_ref, ggain_ref, s1, s2, dq, dall):
    step = pl.program_id(0)
    s1[...] = gatt_ref[...].astype(F32)
    to_windows(s1, s2)

    def window(v, carry):
        masks = head_masks(1.0)
        scaled = head_masks(0.125)
        for p in range(PAIRS):
            lanes = slice(128 * p, 128 * (p + 1))
            q = qkv_ref[v, :, lanes].astype(F32)
            k = qkv_ref[v, :, C + 128 * p : C + 128 * (p + 1)]
            val = qkv_ref[v, :, 2 * C + 128 * p : 2 * C + 128 * (p + 1)]
            qs = stacked(q, scaled)
            gs = stacked(s2[v, :, lanes], masks)
            prob = prob_ref[v, p]
            pf = prob.astype(F32)
            dp = dot(val, gs, 1, 1)
            delta = jnp.sum(pf * dp, axis=0, keepdims=True)
            ds = (pf * (dp - delta)).astype(BF)
            dq[v, :, lanes] = merged_heads(dot(ds, k, 0, 0)) * 0.125
            dq[v, :, C + 128 * p : C + 128 * (p + 1)] = dot(ds, qs, 1, 0)
            dq[v, :, 2 * C + 128 * p : 2 * C + 128 * (p + 1)] = dot(prob, gs, 1, 0)
        return carry

    lax.fori_loop(0, NW, window, 0)
    dqkv = dq[...].reshape(NW * WIN, 3 * C).astype(BF)
    dall[pl.ds(pl.multiple_of(step * (NW * WIN), NW * WIN), NW * WIN), :] = dqkv
    s2[...] = dot(dqkv, w_ref[...], 1, 1).astype(BF).astype(F32).reshape(NW, WIN, C)
    to_grid(s2, s1)
    xhat, rstd = moments(tok_ref[...].astype(F32))
    g = s1[...]
    part = jnp.sum(g * xhat, axis=(0, 1)).reshape(1, C)

    @pl.when(step == 0)
    def _():
        ggain_ref[...] = part

    @pl.when(step > 0)
    def _():
        ggain_ref[...] += part

    dx = g * gain_ref[...].reshape(1, 1, C)
    m1 = jnp.mean(dx, axis=-1, keepdims=True)
    m2 = jnp.mean(dx * xhat, axis=-1, keepdims=True)
    gin_ref[...] = rstd * (dx - m1 - xhat * m2)

    @pl.when(step == pl.num_programs(0) - 1)
    def _():
        for t in range(6):
            cols = slice(256 * t, 256 * (t + 1))
            gw_ref[:, cols] = dot(normed_ref[...], dall[:, cols], 0, 0).astype(BF)


def attention_backward(tokens, grad_att, qkv, prob, normed, gain, w_qkv):
    steps = ROWS // WLAT
    return pl.pallas_call(
        attend_bwd,
        grid=(steps,),
        in_specs=[
            pl.BlockSpec((WLAT, COLS, C), lambda i: (i, 0, 0)),
            pl.BlockSpec((WLAT, COLS, C), lambda i: (i, 0, 0)),
            pl.BlockSpec((NW, WIN, 3 * C), lambda i: (i, 0, 0)),
            pl.BlockSpec((NW, PAIRS, WIN, 2 * WIN), lambda i: (i, 0, 0, 0)),
            pl.BlockSpec((ROWS * COLS, C), lambda i: (0, 0)),
            pl.BlockSpec((1, C), lambda i: (0, 0)),
            pl.BlockSpec((C, 3 * C), lambda i: (0, 0)),
        ],
        out_specs=[
            pl.BlockSpec((WLAT, COLS, C), lambda i: (i, 0, 0)),
            pl.BlockSpec((C, 3 * C), lambda i: (0, 0)),
            pl.BlockSpec((1, C), lambda i: (0, 0)),
        ],
        out_shape=[
            jax.ShapeDtypeStruct((ROWS, COLS, C), F32),
            jax.ShapeDtypeStruct((C, 3 * C), BF),
            jax.ShapeDtypeStruct((1, C), F32),
        ],
        scratch_shapes=[
            pltpu.VMEM((WLAT, COLS, C), F32),
            pltpu.VMEM((NW, WIN, C), F32),
            pltpu.VMEM((NW, WIN, 3 * C), F32),
            pltpu.VMEM((ROWS * COLS, 3 * C), BF),
        ],
        compiler_params=pltpu.CompilerParams(vmem_limit_bytes=48 * MIB),
        name="attend_bwd",
    )(tokens, grad_att, qkv, prob, normed, gain, w_qkv)


CH = 4
NCH = ROWS // CH
MT = (CH // 2) * (COLS // 2)
MALL = NCH * MT
C4 = 4 * C
C2 = 1024


def merge_body(att_ref, tok_ref, gm_ref, wout_ref, wm_hbm, gain_ref,
               merged_ref, gatt_ref, gmix_ref, gwm_ref, gwo_ref, ggain_ref,
               wm_ref, sem, s1, xh, rs, mi, gi):
    load = pltpu.make_async_copy(wm_hbm, wm_ref, sem)
    load.start()
    gain = gain_ref[...]

    def forward(c, carry):
        rows = pl.ds(c * CH, CH)
        att = att_ref[rows].reshape(CH * COLS, C)
        proj = dot(att, wout_ref[...], 1, 0).reshape(CH, COLS, C)
        mixed = (tok_ref[rows].astype(F32) + proj).astype(BF).astype(F32)
        for q in range(4):
            s1[q] = mixed[:, :, 128 * q : 128 * (q + 1)]
        parts = []
        for b in range(2):
            for a in range(2):
                for q in range(4):
                    piece = [s1[q, 2 * i + a, pl.ds(b, COLS // 2, stride=2), :] for i in range(CH // 2)]
                    parts.append(jnp.concatenate(piece, axis=0))
        x = jnp.concatenate(parts, axis=1)
        xhat, rstd = moments(x)
        here = pl.ds(pl.multiple_of(c * MT, MT), MT)
        xh[here, :] = xhat
        rs[here, :] = rstd
        mi[here, :] = (xhat * gain).astype(BF)
        return carry

    lax.fori_loop(0, NCH, forward, 0)
    load.wait()
    gm = gm_ref[...].astype(F32).reshape(MALL, C2).astype(BF)

    def merged_tile(n, carry):
        cols = pl.ds(pl.multiple_of(n * 256, 256), 256)
        merged_ref[:, :, cols] = dot(mi[...], wm_ref[:, cols], 1, 0).reshape(ROWS // 2, COLS // 2, 256).astype(BF)
        return carry

    lax.fori_loop(0, C2 // 256, merged_tile, 0)

    def wide_tile(n, carry):
        cols = pl.ds(pl.multiple_of(n * 256, 256), 256)
        gwm_ref[cols, :] = dot(mi[:, cols], gm, 0, 0).astype(BF)
        gi[:, cols] = dot(gm, wm_ref[cols, :], 1, 1).astype(BF)
        return carry

    lax.fori_loop(0, C4 // 256, wide_tile, 0)
    ggain_ref[...] = jnp.zeros_like(ggain_ref)

    def backward(c, carry):
        rows = pl.ds(c * CH, CH)
        here = pl.ds(pl.multiple_of(c * MT, MT), MT)
        xhat = xh[here, :]
        g = gi[here, :].astype(F32)
        ggain_ref[...] += jnp.sum(g * xhat, axis=0, keepdims=True)
        dx = g * gain
        m1 = jnp.mean(dx, axis=-1, keepdims=True)
        m2 = jnp.mean(dx * xhat, axis=-1, keepdims=True)
        dx = rs[here, :] * (dx - m1 - xhat * m2)
        for b in range(2):
            for a in range(2):
                for q in range(4):
                    start = C * (2 * b + a) + 128 * q
                    for i in range(CH // 2):
                        s1[q, 2 * i + a, pl.ds(b, COLS // 2, stride=2), :] = dx[
                            (COLS // 2) * i : (COLS // 2) * (i + 1), start : start + 128
                        ]
        mixed = jnp.concatenate([s1[q] for q in range(4)], axis=-1).astype(BF)
        gmix_ref[rows] = mixed
        gatt_ref[rows] = dot(mixed.reshape(CH * COLS, C), wout_ref[...], 1, 1).reshape(CH, COLS, C).astype(BF)
        return carry

    lax.fori_loop(0, NCH, backward, 0)
    gmix = gmix_ref[...].reshape(ROWS * COLS, C)
    att = att_ref[...].reshape(ROWS * COLS, C)
    for t in range(2):
        cols = slice(256 * t, 256 * (t + 1))
        gwo_ref[cols, :] = dot(att[:, cols], gmix, 0, 0).astype(BF)


def merge_block(att, tokens, grad_merged, w_out, w_merge, gain):
    vmem = pl.BlockSpec(memory_space=pltpu.VMEM)
    return pl.pallas_call(
        merge_body,
        in_specs=[vmem] * 4 + [pl.BlockSpec(memory_space=pl.ANY), vmem],
        out_specs=[vmem] * 6,
        out_shape=[
            jax.ShapeDtypeStruct((ROWS // 2, COLS // 2, C2), BF),
            jax.ShapeDtypeStruct((ROWS, COLS, C), BF),
            jax.ShapeDtypeStruct((ROWS, COLS, C), BF),
            jax.ShapeDtypeStruct((C4, C2), BF),
            jax.ShapeDtypeStruct((C, C), BF),
            jax.ShapeDtypeStruct((1, C4), F32),
        ],
        scratch_shapes=[
            pltpu.VMEM((C4, C2), BF),
            pltpu.SemaphoreType.DMA(()),
            pltpu.VMEM((4, CH, COLS, 128), F32),
            pltpu.VMEM((MALL, C4), F32),
            pltpu.VMEM((MALL, 1), F32),
            pltpu.VMEM((MALL, C4), BF),
            pltpu.VMEM((MALL, C4), BF),
        ],
        compiler_params=pltpu.CompilerParams(vmem_limit_bytes=52 * MIB),
        name="merge_block",
    )(att, tokens, grad_merged, w_out, w_merge, gain)


def shifted_2(value, axis, steps):
    count = lax.axis_size(axis)
    pairs = [(source, (source + steps) % count) for source in range(count)]
    return lax.ppermute(value, axis, pairs)


def on_device(tokens, lat_band, gain_attn, w_qkv, w_out, gain_merge, w_merge, grad_merged):
    tile_rows, tile_cols, features = tokens.shape
    half_lat = WLAT // 2
    half_lon = WLON // 2
    west_cols = shifted_2(tokens[:, tile_cols - half_lon :], "lon", 1)
    shifted = jnp.concatenate([west_cols, tokens[:, : tile_cols - half_lon]], axis=1)
    south_rows = shifted_2(shifted[tile_rows - half_lat :], "lat", 1)
    shifted = jnp.concatenate([south_rows, shifted[: tile_rows - half_lat]], axis=0)
    band_count = lat_band.shape[0]
    extended = jnp.concatenate([lat_band[band_count - half_lat :], lat_band])
    band_rows = lax.dynamic_slice_in_dim(extended, lax.axis_index("lat") * tile_rows, tile_rows)
    labels = jnp.repeat(band_rows.reshape(-1, WLAT), WLON, axis=1)
    bias = jnp.where(labels[:, :, None] == jnp.tile(labels, (1, 2))[:, None, :], 0.0, -1e30).astype(F32)
    gain_a = gain_attn.reshape(1, C)
    attended, qkv, prob, normed = attention_forward(shifted, bias, gain_a, w_qkv)
    north_rows = shifted_2(attended[:half_lat], "lat", -1)
    back_frame = jnp.concatenate([attended[half_lat:], north_rows], axis=0)
    east_cols = shifted_2(back_frame[:, :half_lon], "lon", -1)
    own_att = jnp.concatenate([back_frame[:, half_lon:], east_cols], axis=1)
    merged, grad_att, grad_mixed, gw_merge, gw_out, gg_merge = merge_block(
        own_att, tokens, grad_merged, w_out, w_merge, gain_merge.reshape(1, C4)
    )
    to_east = shifted_2(grad_att[:, tile_cols - half_lon :], "lon", 1)
    grad_back = jnp.concatenate([to_east, grad_att[:, : tile_cols - half_lon]], axis=1)
    to_north = shifted_2(grad_back[tile_rows - half_lat :], "lat", 1)
    grad_shifted = jnp.concatenate([to_north, grad_back[: tile_rows - half_lat]], axis=0)
    grad_inputs, gw_qkv, gg_attn = attention_backward(
        shifted, grad_shifted, qkv, prob, normed, gain_a, w_qkv
    )
    upper_rows = shifted_2(grad_inputs[:half_lat].astype(BF), "lat", -1).astype(F32)
    own_frame = jnp.concatenate([grad_inputs[half_lat:], upper_rows], axis=0)
    right_cols = shifted_2(own_frame[:, :half_lon].astype(BF), "lon", -1).astype(F32)
    own_frame = jnp.concatenate([own_frame[:, half_lon:], right_cols], axis=1)
    grad_tokens = own_frame + grad_mixed.astype(F32)
    gg_attn, gg_merge, gw_qkv, gw_out, gw_merge = lax.psum(
        (gg_attn, gg_merge, gw_qkv, gw_out, gw_merge), ("lat", "lon")
    )
    return (
        merged,
        grad_tokens,
        gg_attn.reshape(C),
        gw_qkv.astype(F32),
        gw_out.astype(F32),
        gg_merge.reshape(C4),
        gw_merge.astype(F32),
    )


def solution(mesh):
    return jax.shard_map(
        on_device,
        mesh=mesh,
        in_specs=(P("lat", "lon", None), P(), P(), P(), P(), P(), P(), P("lat", "lon", None)),
        out_specs=(P("lat", "lon", None), P("lat", "lon", None), P(), P(), P(), P(), P()),
        check_vma=False,
    )
```

```python
import functools
import jax
import jax.numpy as jnp
from jax import lax
from jax.experimental import pallas as pl
from jax.experimental.pallas import tpu as pltpu
from jax.sharding import PartitionSpec as P

HEADS = 8
WLAT = 6
WLON = 12
EPSILON = 1e-05
F32 = jnp.float32
BF = jnp.bfloat16
ROWS = 24
COLS = 48
C = 512
WIN = 72
NW = COLS // WLON
PAIRS = HEADS // 2
MIB = 1 << 20


def dot(a, b, ca, cb):
    return lax.dot_general(a, b, (((ca,), (cb,)), ((), ())), preferred_element_type=F32)


def head_masks(scale):
    lane = lax.broadcasted_iota(jnp.int32, (1, 128), 1)
    low = jnp.where(lane < 64, scale, 0.0).astype(F32)
    high = jnp.where(lane < 64, 0.0, scale).astype(F32)
    return low, high


def stacked(value, masks):
    return jnp.concatenate([value * masks[0], value * masks[1]], axis=0).astype(BF)


def merged_heads(value):
    lane = lax.broadcasted_iota(jnp.int32, (WIN, 128), 1)
    return jnp.where(lane < 64, value[:WIN], value[WIN:])


def to_windows(src, dst):
    for v in range(NW):
        for r in range(WLAT):
            dst[v, WLON * r : WLON * (r + 1), :] = src[r, WLON * v : WLON * (v + 1), :]


def to_grid(src, dst):
    for v in range(NW):
        for r in range(WLAT):
            dst[r, WLON * v : WLON * (v + 1), :] = src[v, WLON * r : WLON * (r + 1), :]


def moments(x):
    mean = jnp.mean(x, axis=-1, keepdims=True)
    centered = x - mean
    var = jnp.mean(centered * centered, axis=-1, keepdims=True)
    rstd = lax.rsqrt(var + EPSILON)
    return centered * rstd, rstd


def attend_fwd(tok_ref, bias_ref, gain_ref, w_ref, att_ref, qkv_ref, prob_ref, normed_ref, s1, s2, qf):
    xhat, _ = moments(tok_ref[...].astype(F32))
    s1[...] = xhat * gain_ref[...].reshape(1, 1, C)
    to_windows(s1, s2)
    normed = s2[...].reshape(NW * WIN, C).astype(BF)
    normed_ref[...] = normed
    for t in range(3):
        part = dot(normed, w_ref[:, C * t : C * (t + 1)], 1, 0).reshape(NW, WIN, C)
        if t == 0:
            qf[...] = part
        qkv_ref[:, :, C * t : C * (t + 1)] = part.astype(BF)
    bias = bias_ref[0]

    def window(v, carry):
        masks = head_masks(0.125)
        for p in range(PAIRS):
            lanes = slice(128 * p, 128 * (p + 1))
            qs = stacked(qf[v, :, lanes].astype(BF).astype(F32), masks)
            k = qkv_ref[v, :, C + 128 * p : C + 128 * (p + 1)]
            val = qkv_ref[v, :, 2 * C + 128 * p : 2 * C + 128 * (p + 1)]
            s = dot(k, qs, 1, 1) + bias
            e = jnp.exp(s - jnp.max(s, axis=0, keepdims=True))
            prob = (e * (1.0 / jnp.sum(e, axis=0, keepdims=True))).astype(BF)
            prob_ref[v, p] = prob
            s2[v, :, lanes] = merged_heads(dot(prob, val, 0, 0))
        return carry

    lax.fori_loop(0, NW, window, 0)
    to_grid(s2, s1)
    att_ref[...] = s1[...].astype(BF)


def attention_forward(tokens, bias, gain, w_qkv):
    steps = ROWS // WLAT
    return pl.pallas_call(
        attend_fwd,
        grid=(steps,),
        in_specs=[
            pl.BlockSpec((WLAT, COLS, C), lambda i: (i, 0, 0)),
            pl.BlockSpec((1, WIN, 2 * WIN), lambda i: (i, 0, 0)),
            pl.BlockSpec((1, C), lambda i: (0, 0)),
            pl.BlockSpec((C, 3 * C), lambda i: (0, 0)),
        ],
        out_specs=[
            pl.BlockSpec((WLAT, COLS, C), lambda i: (i, 0, 0)),
            pl.BlockSpec((NW, WIN, 3 * C), lambda i: (i, 0, 0)),
            pl.BlockSpec((NW, PAIRS, WIN, 2 * WIN), lambda i: (i, 0, 0, 0)),
            pl.BlockSpec((NW * WIN, C), lambda i: (i, 0)),
        ],
        out_shape=[
            jax.ShapeDtypeStruct((ROWS, COLS, C), BF),
            jax.ShapeDtypeStruct((steps * NW, WIN, 3 * C), BF),
            jax.ShapeDtypeStruct((steps * NW, PAIRS, WIN, 2 * WIN), BF),
            jax.ShapeDtypeStruct((ROWS * COLS, C), BF),
        ],
        scratch_shapes=[
            pltpu.VMEM((WLAT, COLS, C), F32),
            pltpu.VMEM((NW, WIN, C), F32),
            pltpu.VMEM((NW, WIN, C), F32),
        ],
        compiler_params=pltpu.CompilerParams(vmem_limit_bytes=40 * MIB),
        name="attend_fwd",
    )(tokens, bias, gain, w_qkv)


def attend_bwd(tok_ref, gatt_ref, qkv_ref, prob_ref, normed_ref, gain_ref, w_ref,
               gin_ref, gw_ref, ggain_ref, s1, s2, dq, dall):
    step = pl.program_id(0)
    s1[...] = gatt_ref[...].astype(F32)
    to_windows(s1, s2)

    def window(v, carry):
        masks = head_masks(1.0)
        scaled = head_masks(0.125)
        for p in range(PAIRS):
            lanes = slice(128 * p, 128 * (p + 1))
            q = qkv_ref[v, :, lanes].astype(F32)
            k = qkv_ref[v, :, C + 128 * p : C + 128 * (p + 1)]
            val = qkv_ref[v, :, 2 * C + 128 * p : 2 * C + 128 * (p + 1)]
            qs = stacked(q, scaled)
            gs = stacked(s2[v, :, lanes], masks)
            prob = prob_ref[v, p]
            pf = prob.astype(F32)
            dp = dot(val, gs, 1, 1)
            delta = jnp.sum(pf * dp, axis=0, keepdims=True)
            ds = (pf * (dp - delta)).astype(BF)
            dq[v, :, lanes] = merged_heads(dot(ds, k, 0, 0)) * 0.125
            dq[v, :, C + 128 * p : C + 128 * (p + 1)] = dot(ds, qs, 1, 0)
            dq[v, :, 2 * C + 128 * p : 2 * C + 128 * (p + 1)] = dot(prob, gs, 1, 0)
        return carry

    lax.fori_loop(0, NW, window, 0)
    dqkv = dq[...].reshape(NW * WIN, 3 * C).astype(BF)
    dall[pl.ds(pl.multiple_of(step * (NW * WIN), NW * WIN), NW * WIN), :] = dqkv
    s2[...] = dot(dqkv, w_ref[...], 1, 1).astype(BF).astype(F32).reshape(NW, WIN, C)
    to_grid(s2, s1)
    xhat, rstd = moments(tok_ref[...].astype(F32))
    g = s1[...]
    part = jnp.sum(g * xhat, axis=(0, 1)).reshape(1, C)

    @pl.when(step == 0)
    def _():
        ggain_ref[...] = part

    @pl.when(step > 0)
    def _():
        ggain_ref[...] += part

    dx = g * gain_ref[...].reshape(1, 1, C)
    m1 = jnp.mean(dx, axis=-1, keepdims=True)
    m2 = jnp.mean(dx * xhat, axis=-1, keepdims=True)
    gin_ref[...] = rstd * (dx - m1 - xhat * m2)

    @pl.when(step == pl.num_programs(0) - 1)
    def _():
        for t in range(6):
            cols = slice(256 * t, 256 * (t + 1))
            gw_ref[:, cols] = dot(normed_ref[...], dall[:, cols], 0, 0).astype(BF)


def attention_backward(tokens, grad_att, qkv, prob, normed, gain, w_qkv):
    steps = ROWS // WLAT
    return pl.pallas_call(
        attend_bwd,
        grid=(steps,),
        in_specs=[
            pl.BlockSpec((WLAT, COLS, C), lambda i: (i, 0, 0)),
            pl.BlockSpec((WLAT, COLS, C), lambda i: (i, 0, 0)),
            pl.BlockSpec((NW, WIN, 3 * C), lambda i: (i, 0, 0)),
            pl.BlockSpec((NW, PAIRS, WIN, 2 * WIN), lambda i: (i, 0, 0, 0)),
            pl.BlockSpec((ROWS * COLS, C), lambda i: (0, 0)),
            pl.BlockSpec((1, C), lambda i: (0, 0)),
            pl.BlockSpec((C, 3 * C), lambda i: (0, 0)),
        ],
        out_specs=[
            pl.BlockSpec((WLAT, COLS, C), lambda i: (i, 0, 0)),
            pl.BlockSpec((C, 3 * C), lambda i: (0, 0)),
            pl.BlockSpec((1, C), lambda i: (0, 0)),
        ],
        out_shape=[
            jax.ShapeDtypeStruct((ROWS, COLS, C), F32),
            jax.ShapeDtypeStruct((C, 3 * C), BF),
            jax.ShapeDtypeStruct((1, C), F32),
        ],
        scratch_shapes=[
            pltpu.VMEM((WLAT, COLS, C), F32),
            pltpu.VMEM((NW, WIN, C), F32),
            pltpu.VMEM((NW, WIN, 3 * C), F32),
            pltpu.VMEM((ROWS * COLS, 3 * C), BF),
        ],
        compiler_params=pltpu.CompilerParams(vmem_limit_bytes=48 * MIB),
        name="attend_bwd",
    )(tokens, grad_att, qkv, prob, normed, gain, w_qkv)


CH = 4
NCH = ROWS // CH
MT = (CH // 2) * (COLS // 2)
MALL = NCH * MT
C4 = 4 * C
C2 = 1024


def merge_body(att_ref, tok_ref, gm_ref, wout_ref, wm_hbm, gain_ref,
               merged_ref, gatt_ref, gmix_ref, gwm_ref, gwo_ref, ggain_ref,
               wm_ref, sem, s1, xh, rs, mi, gi):
    load = pltpu.make_async_copy(wm_hbm, wm_ref, sem)
    load.start()
    gain = gain_ref[...]

    def forward(c, carry):
        rows = pl.ds(c * CH, CH)
        att = att_ref[rows].reshape(CH * COLS, C)
        proj = dot(att, wout_ref[...], 1, 0).reshape(CH, COLS, C)
        mixed = (tok_ref[rows].astype(F32) + proj).astype(BF).astype(F32)
        for q in range(4):
            s1[q] = mixed[:, :, 128 * q : 128 * (q + 1)]
        parts = []
        for b in range(2):
            for a in range(2):
                for q in range(4):
                    piece = [s1[q, 2 * i + a, pl.ds(b, COLS // 2, stride=2), :] for i in range(CH // 2)]
                    parts.append(jnp.concatenate(piece, axis=0))
        x = jnp.concatenate(parts, axis=1)
        xhat, rstd = moments(x)
        here = pl.ds(pl.multiple_of(c * MT, MT), MT)
        xh[here, :] = xhat
        rs[here, :] = rstd
        mi[here, :] = (xhat * gain).astype(BF)
        return carry

    lax.fori_loop(0, NCH, forward, 0)
    load.wait()
    gm = gm_ref[...].astype(F32).reshape(MALL, C2).astype(BF)

    def merged_tile(n, carry):
        cols = pl.ds(pl.multiple_of(n * 256, 256), 256)
        merged_ref[:, :, cols] = dot(mi[...], wm_ref[:, cols], 1, 0).reshape(ROWS // 2, COLS // 2, 256).astype(BF)
        return carry

    lax.fori_loop(0, C2 // 256, merged_tile, 0)

    def wide_tile(n, carry):
        cols = pl.ds(pl.multiple_of(n * 256, 256), 256)
        gwm_ref[cols, :] = dot(mi[:, cols], gm, 0, 0).astype(BF)
        gi[:, cols] = dot(gm, wm_ref[cols, :], 1, 1).astype(BF)
        return carry

    lax.fori_loop(0, C4 // 256, wide_tile, 0)
    ggain_ref[...] = jnp.zeros_like(ggain_ref)

    def backward(c, carry):
        rows = pl.ds(c * CH, CH)
        here = pl.ds(pl.multiple_of(c * MT, MT), MT)
        xhat = xh[here, :]
        g = gi[here, :].astype(F32)
        ggain_ref[...] += jnp.sum(g * xhat, axis=0, keepdims=True)
        dx = g * gain
        m1 = jnp.mean(dx, axis=-1, keepdims=True)
        m2 = jnp.mean(dx * xhat, axis=-1, keepdims=True)
        dx = rs[here, :] * (dx - m1 - xhat * m2)
        for b in range(2):
            for a in range(2):
                for q in range(4):
                    start = C * (2 * b + a) + 128 * q
                    for i in range(CH // 2):
                        s1[q, 2 * i + a, pl.ds(b, COLS // 2, stride=2), :] = dx[
                            (COLS // 2) * i : (COLS // 2) * (i + 1), start : start + 128
                        ]
        mixed = jnp.concatenate([s1[q] for q in range(4)], axis=-1).astype(BF)
        gmix_ref[rows] = mixed
        gatt_ref[rows] = dot(mixed.reshape(CH * COLS, C), wout_ref[...], 1, 1).reshape(CH, COLS, C).astype(BF)
        return carry

    lax.fori_loop(0, NCH, backward, 0)
    gmix = gmix_ref[...].reshape(ROWS * COLS, C)
    att = att_ref[...].reshape(ROWS * COLS, C)
    for t in range(2):
        cols = slice(256 * t, 256 * (t + 1))
        gwo_ref[cols, :] = dot(att[:, cols], gmix, 0, 0).astype(BF)


def merge_block(att, tokens, grad_merged, w_out, w_merge, gain):
    vmem = pl.BlockSpec(memory_space=pltpu.VMEM)
    return pl.pallas_call(
        merge_body,
        in_specs=[vmem] * 4 + [pl.BlockSpec(memory_space=pl.ANY), vmem],
        out_specs=[vmem] * 6,
        out_shape=[
            jax.ShapeDtypeStruct((ROWS // 2, COLS // 2, C2), BF),
            jax.ShapeDtypeStruct((ROWS, COLS, C), BF),
            jax.ShapeDtypeStruct((ROWS, COLS, C), BF),
            jax.ShapeDtypeStruct((C4, C2), BF),
            jax.ShapeDtypeStruct((C, C), BF),
            jax.ShapeDtypeStruct((1, C4), F32),
        ],
        scratch_shapes=[
            pltpu.VMEM((C4, C2), BF),
            pltpu.SemaphoreType.DMA(()),
            pltpu.VMEM((4, CH, COLS, 128), F32),
            pltpu.VMEM((MALL, C4), F32),
            pltpu.VMEM((MALL, 1), F32),
            pltpu.VMEM((MALL, C4), BF),
            pltpu.VMEM((MALL, C4), BF),
        ],
        compiler_params=pltpu.CompilerParams(vmem_limit_bytes=52 * MIB),
        name="merge_block",
    )(att, tokens, grad_merged, w_out, w_merge, gain)


AXES = ("x", "y", "z")


def coordinates():
    lat = lax.axis_index("lat")
    lon = lax.axis_index("lon")
    return {"x": lon // 4, "y": (lat // 4) * 2 + (lon // 2) % 2, "z": lat % 4, "core": lon % 2}


def device(at):
    return ((at["y"] // 2) * 4 + at["z"], at["x"] * 4 + (at["y"] % 2) * 2 + at["core"])


def peer(at, axis, step):
    size = 2 if axis == "core" else 4
    return device({**at, axis: (at[axis] + step) % size})


def remote(src, dst, send, recv, target):
    return pltpu.make_async_remote_copy(
        src_ref=src, dst_ref=dst, send_sem=send, recv_sem=recv,
        device_id=target, device_id_type=pl.DeviceIdType.MESH,
    )


def greet(at):
    barrier = pltpu.get_barrier_semaphore()
    for axis, count in (("core", 2), ("x", 4), ("y", 4), ("z", 4)):
        for step in range(1, count):
            pl.semaphore_signal(
                barrier, inc=1, device_id=peer(at, axis, step), device_id_type=pl.DeviceIdType.MESH
            )
    pl.semaphore_wait(barrier, 10)


def add_rows(dst, terms, rows, chunk):
    chunk = min(rows, chunk)

    def body(i, carry):
        total = None
        for ref, first in terms:
            piece = ref[pl.ds(pl.multiple_of(first + i * chunk, 16), chunk), :].astype(F32)
            total = piece if total is None else total + piece
        dst[pl.ds(pl.multiple_of(i * chunk, 16), chunk), :] = total.astype(dst.dtype)
        return carry

    if rows == chunk:
        body(0, 0)
    else:
        lax.fori_loop(0, rows // chunk, body, 0)


class Sum:
    def __init__(self, at, src, out, order, bufs, send, recv):
        self.at, self.src, self.out, self.order = at, src, out, order
        self.recv0, self.acc0, self.recvs, self.accs = bufs
        self.send, self.recv = send, recv
        self.rows = src.shape[0]
        self.sent = []

    def start(self, src, dst, index, target):
        copy = remote(src, dst, self.send.at[index], self.recv.at[index], target)
        copy.start()
        self.sent.append(copy)
        return copy

    def begin(self):
        half = self.rows // 2
        theirs = pl.ds(pl.multiple_of((1 - self.at["core"]) * half, 16), half)
        self.last = [self.start(self.src.at[theirs, :], self.recv0, 0, peer(self.at, "core", 1))]

    def core_sum(self):
        half = self.rows // 2
        self.last[0].wait_recv()
        add_rows(self.acc0, [(self.src, self.at["core"] * half), (self.recv0, 0)], half, 64)
        self.scatter(0, self.acc0)

    def scatter(self, level, acc):
        axis = self.order[level]
        block = self.rows // 2 // 4 ** (level + 1)
        self.last = []
        for step in range(1, 4):
            first = pl.multiple_of((self.at[axis] + step) % 4 * block, 16)
            self.last.append(
                self.start(
                    acc.at[pl.ds(first, block), :], self.recvs[level].at[step - 1],
                    1 + 3 * level + step - 1, peer(self.at, axis, step),
                )
            )

    def combine(self, level):
        axis = self.order[level]
        block = self.rows // 2 // 4 ** (level + 1)
        for copy in self.last:
            copy.wait_recv()
        acc = self.acc0 if level == 0 else self.accs[level - 1]
        terms = [(acc, self.at[axis] * block)] + [(self.recvs[level].at[s], 0) for s in range(3)]
        if level < 2:
            add_rows(self.accs[level], terms, block, 64)
            self.scatter(level + 1, self.accs[level])
        else:
            add_rows(self.out.at[pl.ds(self.first(3), block), :], terms, block, 64)
            self.gather(2)

    def first(self, levels):
        first = self.at["core"] * (self.rows // 2)
        for level in range(levels):
            first = first + self.at[self.order[level]] * (self.rows // 2 // 4 ** (level + 1))
        return pl.multiple_of(first, 16)

    def gather(self, level):
        axis = self.order[level]
        block = self.rows // 2 // 4 ** (level + 1)
        mine = self.out.at[pl.ds(self.first(level + 1), block), :]
        self.last = [
            self.start(mine, mine, 10 + 3 * level + step - 1, peer(self.at, axis, step)) for step in range(1, 4)
        ]

    def gathered(self, level):
        for copy in self.last:
            copy.wait_recv()
        if level:
            self.gather(level - 1)
        else:
            mine = self.out.at[pl.ds(self.first(0), self.rows // 2), :]
            self.last = [self.start(mine, mine, 19, peer(self.at, "core", 1))]

    def finish(self):
        self.last[0].wait_recv()
        for copy in self.sent:
            copy.wait_send()

    def steps(self):
        return [
            self.begin,
            self.core_sum,
            lambda: self.combine(0),
            lambda: self.combine(1),
            lambda: self.combine(2),
            lambda: self.gathered(2),
            lambda: self.gathered(1),
            lambda: self.gathered(0),
            self.finish,
        ]


SUM_COPIES = 20


def sum_scratch(rows, lanes):
    half = rows // 2
    return [
        pltpu.VMEM((half, lanes), BF),
        pltpu.VMEM((half, lanes), BF),
        pltpu.VMEM((3, half // 4, lanes), BF),
        pltpu.VMEM((3, half // 16, lanes), BF),
        pltpu.VMEM((3, half // 64, lanes), BF),
        pltpu.VMEM((half // 4, lanes), BF),
        pltpu.VMEM((half // 16, lanes), BF),
    ]


def pack_scratch(refs):
    return refs[0], refs[1], refs[2:5], refs[5:7]


class SmallSum:
    def __init__(self, at, block, slots, send, recv):
        self.at, self.block, self.slots, self.send, self.recv = at, block, slots, send, recv
        self.sent = []

    def begin(self, level):
        axis, count = (("core", 2), ("x", 4), ("y", 4), ("z", 4))[level]
        base = 0 if level == 0 else 3 * level - 2
        self.last = []
        for step in range(1, count):
            i = base + step - 1
            copy = remote(self.block.at[level], self.slots.at[i], self.send.at[i], self.recv.at[i],
                          peer(self.at, axis, step))
            copy.start()
            self.last.append((copy, i))
            self.sent.append(copy)

    def end(self, level):
        total = self.block[level]
        for copy, i in self.last:
            copy.wait_recv()
            total = total + self.slots[i]
        self.block[level + 1] = total

    def finish(self):
        for copy in self.sent:
            copy.wait_send()


def sum_body(gwm_ref, gwq_ref, gwo_ref, ga_ref, gg_ref, outm_ref, outq_ref, outs_ref, *scratch):
    qo, small, slots, send, recv, ssend, srecv = scratch[:7]
    at = coordinates()
    greet(at)
    for t in range(3):
        qo[C * t : C * (t + 1), :] = gwq_ref[:, C * t : C * (t + 1)]
    qo[3 * C : 4 * C, :] = gwo_ref[...]
    small[0] = jnp.zeros_like(small[0])
    small[0, 0:1, :] = ga_ref[...]
    for t in range(4):
        small[0, 1 + t : 2 + t, :] = gg_ref[:, C * t : C * (t + 1)]
    pieces = [
        (gwm_ref.at[:, 0:C], outm_ref.at[:, 0:C]),
        (gwm_ref.at[:, C : 2 * C], outm_ref.at[:, C : 2 * C]),
        (qo, outq_ref),
    ]
    sums = []
    for t, (src, out) in enumerate(pieces):
        order = AXES[t:] + AXES[:t]
        bufs = pack_scratch(scratch[7 + 7 * t : 14 + 7 * t])
        sums.append(Sum(at, src, out, order, bufs, send.at[t], recv.at[t]).steps())
    gains = SmallSum(at, small, slots, ssend, srecv)
    for n in range(len(sums[0])):
        for steps in sums:
            steps[n]()
        if n < 4:
            gains.begin(n)
            gains.end(n)
    gains.finish()
    outs_ref[...] = small[4]


def sum_all(gw_merge, gw_qkv, gw_out, gg_attn, gg_merge):
    vmem = pl.BlockSpec(memory_space=pltpu.VMEM)
    return pl.pallas_call(
        sum_body,
        in_specs=[vmem] * 5,
        out_specs=[vmem] * 3,
        out_shape=[
            jax.ShapeDtypeStruct((C4, C2), BF),
            jax.ShapeDtypeStruct((4 * C, C), BF),
            jax.ShapeDtypeStruct((8, C), F32),
        ],
        scratch_shapes=[
            pltpu.VMEM((4 * C, C), BF),
            pltpu.VMEM((5, 8, C), F32),
            pltpu.VMEM((10, 8, C), F32),
            pltpu.SemaphoreType.DMA((3, SUM_COPIES)),
            pltpu.SemaphoreType.DMA((3, SUM_COPIES)),
            pltpu.SemaphoreType.DMA((10,)),
            pltpu.SemaphoreType.DMA((10,)),
        ]
        + sum_scratch(4 * C, C) * 3,
        compiler_params=pltpu.CompilerParams(
            vmem_limit_bytes=52 * MIB, collective_id=0, has_side_effects=True
        ),
        name="sum_all",
    )(gw_merge, gw_qkv, gw_out, gg_attn, gg_merge)


def shifted_2(value, axis, steps):
    count = lax.axis_size(axis)
    pairs = [(source, (source + steps) % count) for source in range(count)]
    return lax.ppermute(value, axis, pairs)


def on_device(tokens, lat_band, gain_attn, w_qkv, w_out, gain_merge, w_merge, grad_merged):
    tile_rows, tile_cols, features = tokens.shape
    half_lat = WLAT // 2
    half_lon = WLON // 2
    west_cols = shifted_2(tokens[:, tile_cols - half_lon :], "lon", 1)
    shifted = jnp.concatenate([west_cols, tokens[:, : tile_cols - half_lon]], axis=1)
    south_rows = shifted_2(shifted[tile_rows - half_lat :], "lat", 1)
    shifted = jnp.concatenate([south_rows, shifted[: tile_rows - half_lat]], axis=0)
    band_count = lat_band.shape[0]
    extended = jnp.concatenate([lat_band[band_count - half_lat :], lat_band])
    band_rows = lax.dynamic_slice_in_dim(extended, lax.axis_index("lat") * tile_rows, tile_rows)
    labels = jnp.repeat(band_rows.reshape(-1, WLAT), WLON, axis=1)
    bias = jnp.where(labels[:, :, None] == jnp.tile(labels, (1, 2))[:, None, :], 0.0, -1e30).astype(F32)
    gain_a = gain_attn.reshape(1, C)
    attended, qkv, prob, normed = attention_forward(shifted, bias, gain_a, w_qkv)
    north_rows = shifted_2(attended[:half_lat], "lat", -1)
    back_frame = jnp.concatenate([attended[half_lat:], north_rows], axis=0)
    east_cols = shifted_2(back_frame[:, :half_lon], "lon", -1)
    own_att = jnp.concatenate([back_frame[:, half_lon:], east_cols], axis=1)
    merged, grad_att, grad_mixed, gw_merge, gw_out, gg_merge = merge_block(
        own_att, tokens, grad_merged, w_out, w_merge, gain_merge.reshape(1, C4)
    )
    to_east = shifted_2(grad_att[:, tile_cols - half_lon :], "lon", 1)
    grad_back = jnp.concatenate([to_east, grad_att[:, : tile_cols - half_lon]], axis=1)
    to_north = shifted_2(grad_back[tile_rows - half_lat :], "lat", 1)
    grad_shifted = jnp.concatenate([to_north, grad_back[: tile_rows - half_lat]], axis=0)
    grad_inputs, gw_qkv, gg_attn = attention_backward(
        shifted, grad_shifted, qkv, prob, normed, gain_a, w_qkv
    )
    upper_rows = shifted_2(grad_inputs[:half_lat].astype(BF), "lat", -1).astype(F32)
    own_frame = jnp.concatenate([grad_inputs[half_lat:], upper_rows], axis=0)
    right_cols = shifted_2(own_frame[:, :half_lon].astype(BF), "lon", -1).astype(F32)
    own_frame = jnp.concatenate([own_frame[:, half_lon:], right_cols], axis=1)
    grad_tokens = own_frame + grad_mixed.astype(F32)
    sum_merge, sum_qo, sum_gain = sum_all(gw_merge, gw_qkv, gw_out, gg_attn, gg_merge)
    gw_qkv = jnp.concatenate([sum_qo[C * t : C * (t + 1)] for t in range(3)], axis=1)
    return (
        merged,
        grad_tokens,
        sum_gain[0],
        gw_qkv.astype(F32),
        sum_qo[3 * C :].astype(F32),
        sum_gain[1:5].reshape(C4),
        sum_merge.astype(F32),
    )


def solution(mesh):
    return jax.shard_map(
        on_device,
        mesh=mesh,
        in_specs=(P("lat", "lon", None), P(), P(), P(), P(), P(), P(), P("lat", "lon", None)),
        out_specs=(P("lat", "lon", None), P("lat", "lon", None), P(), P(), P(), P(), P()),
        check_vma=False,
    )
```

```python
import functools
import jax
import jax.numpy as jnp
from jax import lax
from jax.experimental import pallas as pl
from jax.experimental.pallas import tpu as pltpu
from jax.sharding import PartitionSpec as P

HEADS = 8
WLAT = 6
WLON = 12
EPSILON = 1e-05
F32 = jnp.float32
BF = jnp.bfloat16
ROWS = 24
COLS = 48
C = 512
WIN = 72
NW = COLS // WLON
PAIRS = HEADS // 2
MIB = 1 << 20


def dot(a, b, ca, cb):
    return lax.dot_general(a, b, (((ca,), (cb,)), ((), ())), preferred_element_type=F32)


def head_masks(scale):
    lane = lax.broadcasted_iota(jnp.int32, (1, 128), 1)
    low = jnp.where(lane < 64, scale, 0.0).astype(F32)
    high = jnp.where(lane < 64, 0.0, scale).astype(F32)
    return low, high


def stacked(value, masks):
    return jnp.concatenate([value * masks[0], value * masks[1]], axis=0).astype(BF)


def merged_heads(value):
    lane = lax.broadcasted_iota(jnp.int32, (WIN, 128), 1)
    return jnp.where(lane < 64, value[:WIN], value[WIN:])


def moments(x):
    mean = jnp.mean(x, axis=-1, keepdims=True)
    centered = x - mean
    var = jnp.mean(centered * centered, axis=-1, keepdims=True)
    rstd = lax.rsqrt(var + EPSILON)
    return centered * rstd, rstd


AXES = ("x", "y", "z")


def coordinates():
    lat = lax.axis_index("lat")
    lon = lax.axis_index("lon")
    return {"x": lon // 4, "y": (lat // 4) * 2 + (lon // 2) % 2, "z": lat % 4, "core": lon % 2}


def device(at):
    return ((at["y"] // 2) * 4 + at["z"], at["x"] * 4 + (at["y"] % 2) * 2 + at["core"])


def peer(at, axis, step):
    size = 2 if axis == "core" else 4
    return device({**at, axis: (at[axis] + step) % size})


def remote(src, dst, send, recv, target):
    return pltpu.make_async_remote_copy(
        src_ref=src, dst_ref=dst, send_sem=send, recv_sem=recv,
        device_id=target, device_id_type=pl.DeviceIdType.MESH,
    )


def neighbour(rows, cols):
    lat = lax.axis_index("lat")
    lon = lax.axis_index("lon")
    return ((lat + rows) % 8, (lon + cols) % 16)


EDGES = ((0, 1), (1, 0), (1, 1))


def greet(at):
    barrier = pltpu.get_barrier_semaphore()
    targets = [
        peer(at, axis, step)
        for axis, count in (("core", 2), ("x", 4), ("y", 4), ("z", 4))
        for step in range(1, count)
    ]
    targets += [neighbour(sign * r, sign * c) for sign in (1, -1) for r, c in EDGES]
    for target in targets:
        pl.semaphore_signal(barrier, inc=1, device_id=target, device_id_type=pl.DeviceIdType.MESH)
    pl.semaphore_wait(barrier, len(targets))


def add_rows(dst, start, terms, rows):
    chunk = min(rows, 64)

    def body(i, carry):
        total = None
        for ref, first in terms:
            piece = ref[pl.ds(pl.multiple_of(first + i * chunk, 16), chunk), :].astype(F32)
            total = piece if total is None else total + piece
        dst[pl.ds(pl.multiple_of(start + i * chunk, 16), chunk), :] = total.astype(dst.dtype)
        return carry

    lax.fori_loop(0, rows // chunk, body, 0)


class Sum:
    def __init__(self, at, src, out, order, recvs, send, recv):
        self.at, self.src, self.out, self.order = at, src, out, order
        self.recvs, self.send, self.recv = recvs, send, recv
        self.rows = src.shape[0]
        self.sent = []

    def start(self, src, dst, index, target):
        copy = remote(src, dst, self.send.at[index], self.recv.at[index], target)
        copy.start()
        self.sent.append(copy)
        return copy

    def block(self, level):
        return self.rows // 2 // 4**level

    def first(self, levels):
        first = self.at["core"] * (self.rows // 2)
        for level in range(levels):
            first = first + self.at[self.order[level]] * self.block(level + 1)
        return pl.multiple_of(first, 16)

    def begin(self):
        half = self.rows // 2
        theirs = pl.ds(pl.multiple_of((1 - self.at["core"]) * half, 16), half)
        self.last = [self.start(self.src.at[theirs, :], self.recvs[0].at[0], 0, peer(self.at, "core", 1))]

    def combine(self, level):
        for copy in self.last:
            copy.wait_recv()
        count = self.block(level)
        first = self.first(level)
        terms = [(self.src, first)] + [(self.recvs[level].at[s], 0) for s in range(1 if level == 0 else 3)]
        if level == 3:
            add_rows(self.out, first, terms, count)
            self.gather(3)
            return
        add_rows(self.src, first, terms, count)
        axis = self.order[level]
        block = self.block(level + 1)
        self.last = []
        for step in range(1, 4):
            there = pl.multiple_of(first + (self.at[axis] + step) % 4 * block, 16)
            self.last.append(
                self.start(
                    self.src.at[pl.ds(there, block), :], self.recvs[level + 1].at[step - 1],
                    3 * level + step, peer(self.at, axis, step),
                )
            )

    def gather(self, level):
        mine = self.out.at[pl.ds(self.first(level), self.block(level)), :]
        if level == 0:
            self.last = [self.start(mine, mine, 19, peer(self.at, "core", 1))]
            return
        axis = self.order[level - 1]
        self.last = [
            self.start(mine, mine, 10 + 3 * (level - 1) + step - 1, peer(self.at, axis, step)) for step in range(1, 4)
        ]

    def gathered(self, level):
        for copy in self.last:
            copy.wait_recv()
        self.gather(level - 1)

    def finish(self):
        self.last[0].wait_recv()
        for copy in self.sent:
            copy.wait_send()

    def step(self, n):
        if n == 0:
            self.begin()
        elif n < 5:
            self.combine(n - 1)
        elif n < 8:
            self.gathered(8 - n)
        else:
            self.finish()


SUM_COPIES = 20


def sum_scratch(rows, lanes):
    half = rows // 2
    return [pltpu.VMEM((1, half, lanes), BF)] + [pltpu.VMEM((3, half // 4**n, lanes), BF) for n in (1, 2, 3)]


class SmallSum:
    def __init__(self, at, block, slots, send, recv):
        self.at, self.block, self.slots, self.send, self.recv = at, block, slots, send, recv
        self.sent = []

    def begin(self, level):
        axis, count = (("core", 2), ("x", 4), ("y", 4), ("z", 4))[level]
        base = 0 if level == 0 else 3 * level - 2
        self.last = []
        for step in range(1, count):
            i = base + step - 1
            copy = remote(self.block.at[level], self.slots.at[i], self.send.at[i], self.recv.at[i],
                          peer(self.at, axis, step))
            copy.start()
            self.last.append((copy, i))
            self.sent.append(copy)

    def end(self, level):
        total = self.block[level]
        for copy, i in self.last:
            copy.wait_recv()
            total = total + self.slots[i]
        self.block[level + 1] = total

    def finish(self):
        for copy in self.sent:
            copy.wait_send()

CH = 4
NCH = ROWS // CH
MT = (CH // 2) * (COLS // 2)
MALL = NCH * MT
C4 = 4 * C
C2 = 1024
WROWS = ROWS // WLAT
NWT = NW * WIN
FR = COLS + 8
TALL = 4 * C


class Halo:
    def __init__(self, sign, send, recv):
        self.sign, self.send, self.recv = sign, send, recv

    def start(self, sources, targets):
        self.copies = []
        for n, (r, c) in enumerate(EDGES):
            copy = remote(sources[n], targets[n], self.send.at[n], self.recv.at[n],
                          neighbour(self.sign * r, self.sign * c))
            copy.start()
            self.copies.append(copy)

    def arrived(self):
        for copy in self.copies:
            copy.wait_recv()

    def left(self):
        for copy in self.copies:
            copy.wait_send()


def pair_half(ref, pair, half):
    return ref[pair].astype(F32)[8 * half : 8 * half + 8]


def load_frame(fr, w, rows_ref, edge_ref):
    for r in range(WLAT):
        fr[r, 8:FR, :] = rows_ref[WLAT * w + r].astype(F32)
        fr[r, 0:8, :] = pair_half(edge_ref, 3 * w + (r + 1) // 2, (r + 1) % 2)


def to_windows(fr, dst):
    for v in range(NW):
        for r in range(WLAT):
            dst[v, WLON * r : WLON * (r + 1), :] = fr[r, WLON * v + 2 : WLON * v + 14, :]


def to_frame(src, fr):
    for v in range(NW):
        for r in range(WLAT):
            fr[r, WLON * v + 2 : WLON * v + 14, :] = src[v, WLON * r : WLON * (r + 1), :]


def pack_rows(fr, edge_ref, w):
    for r in range(0, WLAT, 2):
        edge_ref[3 * w + r // 2] = jnp.concatenate([fr[r, 0:8, :], fr[r + 1, 0:8, :]], axis=0).astype(BF)


def step_body(tok_hbm, bias_ref, ga_ref, wq_hbm, wo_hbm, gm_hbm, wm_hbm, gmg_ref,
              merged_ref, gtok_ref, outm_ref, outq_ref, outs_ref,
              text, hw, pk, wq, wo, gmb, wm, qkv, prob, nrm, qf, s2, fr, attx, he, bw,
              s1, xh, rs, mi, gwm, qo, gmix, gext, gw, pkg, dq, dall, bn2, bw2, hs2, he2,
              small, slots, ggm, gga, lsem, hsend, hrecv, send, recv, ssend, srecv, *sums):
    loads = [
        pltpu.make_async_copy(src, dst, lsem.at[n])
        for n, (src, dst) in enumerate(
            [(tok_hbm, text.at[pl.ds(3, ROWS)]), (wq_hbm, wq), (wo_hbm, wo), (gm_hbm, gmb), (wm_hbm, wm)]
        )
    ]
    for load in loads:
        load.start()
    at = coordinates()
    greet(at)
    halos = [Halo(sign, hsend.at[n], hrecv.at[n]) for n, sign in enumerate((1, -1, 1, -1))]

    loads[0].wait()
    for m in range(ROWS // 2):
        pk[m] = jnp.concatenate(
            [text[3 + 2 * m + k, 32:48, :].astype(F32)[8:16] for k in range(2)], axis=0
        ).astype(BF)
    halos[0].start(
        [pk, text.at[pl.ds(24, 3)], pk.at[pl.ds(10, 2)]],
        [hw.at[pl.ds(2, 12)], text.at[pl.ds(0, 3)], hw.at[pl.ds(0, 2)]],
    )
    loads[1].wait()
    halos[0].arrived()

    def forward_row(w, carry):
        load_frame(fr, w, text, hw)
        xhat, _ = moments(fr[...])
        fr[...] = xhat * ga_ref[...].reshape(1, 1, C)
        to_windows(fr, s2)
        normed = s2[...].reshape(NWT, C).astype(BF)
        nrm[pl.ds(pl.multiple_of(w * NWT, NWT), NWT), :] = normed
        for t in range(3):
            part = dot(normed, wq[:, C * t : C * (t + 1)], 1, 0).reshape(NW, WIN, C)
            if t == 0:
                qf[...] = part
            qkv[pl.ds(NW * w, NW), :, C * t : C * (t + 1)] = part.astype(BF)
        bias = bias_ref[w]

        def window(v, carry):
            masks = head_masks(0.125)
            n = NW * w + v
            for p in range(PAIRS):
                lanes = slice(128 * p, 128 * (p + 1))
                qs = stacked(qf[v, :, lanes].astype(BF).astype(F32), masks)
                k = qkv[n, :, C + 128 * p : C + 128 * (p + 1)]
                val = qkv[n, :, 2 * C + 128 * p : 2 * C + 128 * (p + 1)]
                s = dot(k, qs, 1, 1) + bias
                e = jnp.exp(s - jnp.max(s, axis=0, keepdims=True))
                pr = (e * (1.0 / jnp.sum(e, axis=0, keepdims=True))).astype(BF)
                prob[n, p] = pr
                s2[v, :, lanes] = merged_heads(dot(pr, val, 0, 0))
            return carry

        lax.fori_loop(0, NW, window, 0)
        to_frame(s2, fr)
        pack_rows(fr, bw, w)
        for r in range(WLAT):
            attx[WLAT * w + r] = fr[r, 8:FR, :].astype(BF)
        return carry

    lax.fori_loop(0, WROWS, forward_row, 0)

    halos[1].start(
        [bw, attx.at[pl.ds(0, 3)], bw.at[pl.ds(0, 2)]],
        [he.at[pl.ds(0, 12)], attx.at[pl.ds(24, 3)], he.at[pl.ds(12, 2)]],
    )
    for load in loads[2:]:
        load.wait()
    halos[1].arrived()
    gain = gmg_ref[...]
    lower = lax.broadcasted_iota(jnp.int32, (8, C), 0) < 2

    def merge_forward(c, carry):
        pieces = []
        for i in range(CH):
            row = attx[CH * c + 3 + i].astype(F32)
            edge = pair_half(he, 2 * c + (3 + i) // 2, (3 + i) % 2)
            pieces.append(jnp.concatenate([row[:40], jnp.where(lower, row[40:], edge)], axis=0))
        att = jnp.concatenate(pieces, axis=0).astype(BF)
        attx[pl.ds(CH * c + 3, CH)] = att.reshape(CH, COLS, C)
        proj = dot(att, wo[...], 1, 0).reshape(CH, COLS, C)
        mixed = (text[pl.ds(CH * c + 3, CH)].astype(F32) + proj).astype(BF).astype(F32)
        for q in range(4):
            s1[q] = mixed[:, :, 128 * q : 128 * (q + 1)]
        parts = []
        for b in range(2):
            for a in range(2):
                for q in range(4):
                    piece = [s1[q, 2 * i + a, pl.ds(b, COLS // 2, stride=2), :] for i in range(CH // 2)]
                    parts.append(jnp.concatenate(piece, axis=0))
        xhat, rstd = moments(jnp.concatenate(parts, axis=1))
        here = pl.ds(pl.multiple_of(c * MT, MT), MT)
        xh[here, :] = xhat
        rs[here, :] = rstd
        mi[here, :] = (xhat * gain).astype(BF)
        return carry

    lax.fori_loop(0, NCH, merge_forward, 0)
    gm = gmb[...].astype(F32).reshape(MALL, C2).astype(BF)

    def merged_tile(n, carry):
        cols = pl.ds(pl.multiple_of(n * 256, 256), 256)
        tile = dot(mi[...], wm[:, cols], 1, 0).reshape(ROWS // 2, COLS // 2, 256)
        merged_ref[:, :, cols] = tile.astype(BF)
        return carry

    lax.fori_loop(0, C2 // 256, merged_tile, 0)

    def wide_tile(n, carry):
        cols = pl.ds(pl.multiple_of(n * 256, 256), 256)
        gwm[cols, :] = dot(mi[:, cols], gm, 0, 0).astype(BF)
        mi[:, cols] = dot(gm, wm[cols, :], 1, 1).astype(BF)
        return carry

    lax.fori_loop(0, C4 // 256, wide_tile, 0)

    def summed(src, out, turn, n):
        order = AXES[turn:] + AXES[:turn]
        return Sum(at, src, out, order, sums[4 * n : 4 * n + 4], send.at[n], recv.at[n])

    wide = [
        summed(gwm.at[:, 0:384], outm_ref.at[:, 0:384], 0, 0),
        summed(gwm.at[:, 384:768], outm_ref.at[:, 384:768], 1, 1),
        summed(gwm.at[:, 768:1024], outm_ref.at[:, 768:1024], 2, 2),
    ]
    early = wide + [summed(qo.at[:, 0:128], outq_ref.at[:, 0:128], 2, 3)]
    late = [
        summed(qo.at[:, 128 * (t + 1) : 128 * (t + 2)], outq_ref.at[:, 128 * (t + 1) : 128 * (t + 2)], t, 4 + t)
        for t in range(3)
    ]

    def advance(group, n):
        for part in group:
            part.step(n)

    advance(wide, 0)
    ggm[...] = jnp.zeros_like(ggm)

    def merge_backward(c, carry):
        here = pl.ds(pl.multiple_of(c * MT, MT), MT)
        xhat = xh[here, :]
        g = mi[here, :].astype(F32)
        ggm[...] += jnp.sum(g * xhat, axis=0, keepdims=True)
        dx = g * gain
        m1 = jnp.mean(dx, axis=-1, keepdims=True)
        m2 = jnp.mean(dx * xhat, axis=-1, keepdims=True)
        dx = rs[here, :] * (dx - m1 - xhat * m2)
        for b in range(2):
            for a in range(2):
                for q in range(4):
                    start = C * (2 * b + a) + 128 * q
                    for i in range(CH // 2):
                        s1[q, 2 * i + a, pl.ds(b, COLS // 2, stride=2), :] = dx[
                            (COLS // 2) * i : (COLS // 2) * (i + 1), start : start + 128
                        ]
        mixed = jnp.concatenate([s1[q] for q in range(4)], axis=-1).astype(BF)
        gmix[pl.ds(c * CH, CH)] = mixed
        gatt = dot(mixed.reshape(CH * COLS, C), wo[...], 1, 1).reshape(CH, COLS, C)
        gext[pl.ds(CH * c + 3, CH)] = gatt.astype(BF)
        for m in range(CH // 2):
            pkg[(CH // 2) * c + m] = jnp.concatenate(
                [gatt[2 * m, 40:48], gatt[2 * m + 1, 40:48]], axis=0
            ).astype(BF)
        return carry

    lax.fori_loop(0, NCH, merge_backward, 0)

    halos[2].start(
        [pkg, gext.at[pl.ds(24, 3)], pkg.at[pl.ds(10, 2)]],
        [gw.at[pl.ds(2, 12)], gext.at[pl.ds(0, 3)], gw.at[pl.ds(0, 2)]],
    )
    flat = gmix[...].reshape(ROWS * COLS, C)
    att = attx[pl.ds(3, ROWS)].reshape(ROWS * COLS, C)
    gwo = dot(att, flat, 0, 0).astype(BF)
    for n in range(4):
        qo[C * n : C * (n + 1), 0:128] = gwo[:, 128 * n : 128 * (n + 1)]
    early[3].step(0)
    halos[2].arrived()
    advance(early, 1)

    def backward_row(w, carry):
        load_frame(fr, w, gext, gw)
        to_windows(fr, s2)

        def window(v, carry):
            masks = head_masks(1.0)
            scaled = head_masks(0.125)
            n = NW * w + v
            for p in range(PAIRS):
                lanes = slice(128 * p, 128 * (p + 1))
                qs = stacked(qkv[n, :, lanes].astype(F32), scaled)
                k = qkv[n, :, C + 128 * p : C + 128 * (p + 1)]
                val = qkv[n, :, 2 * C + 128 * p : 2 * C + 128 * (p + 1)]
                gs = stacked(s2[v, :, lanes], masks)
                pr = prob[n, p]
                pf = pr.astype(F32)
                dp = dot(val, gs, 1, 1)
                delta = jnp.sum(pf * dp, axis=0, keepdims=True)
                ds = (pf * (dp - delta)).astype(BF)
                dq[v, :, lanes] = merged_heads(dot(ds, k, 0, 0)) * 0.125
                dq[v, :, C + 128 * p : C + 128 * (p + 1)] = dot(ds, qs, 1, 0)
                dq[v, :, 2 * C + 128 * p : 2 * C + 128 * (p + 1)] = dot(pr, gs, 1, 0)
            return carry

        lax.fori_loop(0, NW, window, 0)
        dall[pl.ds(pl.multiple_of(w * NWT, NWT), NWT), :] = dq[...].reshape(NWT, 3 * C).astype(BF)
        return carry

    lax.fori_loop(0, 2, backward_row, 0)
    advance(early, 2)
    lax.fori_loop(2, 3, backward_row, 0)
    advance(early, 3)
    lax.fori_loop(3, 4, backward_row, 0)
    advance(early, 4)
    for n in range(6):
        tile = dot(nrm[...], dall[:, 256 * n : 256 * (n + 1)], 0, 0).astype(BF)
        for k in range(2):
            g = 2 * n + k
            qo[C * (g // 3) : C * (g // 3 + 1), 128 * (1 + g % 3) : 128 * (2 + g % 3)] = tile[:, 128 * k : 128 * (k + 1)]
    advance(late, 0)
    advance(early, 5)
    gga[...] = jnp.zeros_like(gga)

    def dgrad_row(w, carry):
        rows = pl.ds(pl.multiple_of(w * NWT, NWT), NWT)
        s2[...] = dot(dall[rows, :], wq[...], 1, 1).astype(BF).astype(F32).reshape(NW, WIN, C)
        load_frame(fr, w, text, hw)
        xhat, rstd = moments(fr[...])
        fr[:, 0:8, :] = jnp.zeros((WLAT, 8, C), F32)
        fr[:, FR - 8 : FR, :] = jnp.zeros((WLAT, 8, C), F32)
        to_frame(s2, fr)
        g = fr[...]
        gga[...] += jnp.sum(g * xhat, axis=(0, 1)).reshape(1, C)
        dx = g * ga_ref[...].reshape(1, 1, C)
        m1 = jnp.mean(dx, axis=-1, keepdims=True)
        m2 = jnp.mean(dx * xhat, axis=-1, keepdims=True)
        fr[...] = rstd * (dx - m1 - xhat * m2)
        pack_rows(fr, bw2, w)
        for r in range(3):
            bn2[WLAT * w + r] = fr[r, 8:FR, :].astype(BF)
        for r in range(3):
            gtok_ref[WLAT * w + r] = fr[3 + r, 8:FR, :] + gmix[WLAT * w + r].astype(F32)

        @pl.when(w > 0)
        def _():
            for r in range(3):
                gtok_ref[WLAT * w - 3 + r] = fr[r, 8:FR, :] + gmix[WLAT * w - 3 + r].astype(F32)

        return carry

    lax.fori_loop(0, 1, dgrad_row, 0)
    advance(late, 1)
    lax.fori_loop(1, 2, dgrad_row, 0)
    advance(early, 6)
    advance(late, 2)
    lax.fori_loop(2, 4, dgrad_row, 0)
    halos[3].start(
        [bw2, bn2.at[pl.ds(0, 3)], bw2.at[pl.ds(0, 2)]],
        [he2.at[pl.ds(0, 12)], hs2, he2.at[pl.ds(12, 2)]],
    )
    small[0] = jnp.zeros_like(small[0])
    small[0, 0:1, :] = gga[...]
    for n in range(4):
        small[0, 1 + n : 2 + n, :] = ggm[:, C * n : C * (n + 1)]
    gains = SmallSum(at, small, slots, ssend, srecv)
    gains.begin(0)
    advance(late, 3)
    gains.end(0)
    gains.begin(1)
    advance(late, 4)
    halos[3].arrived()
    for r in range(3):
        gtok_ref[21 + r] = hs2[r].astype(F32) + gmix[21 + r].astype(F32)
    for r in range(ROWS):
        edge = pair_half(he2, (r + 3) // 2, (r + 3) % 2) + gmix[r, 32:48, :].astype(F32)[8:16]
        gtok_ref[r, 40:48, :] = jnp.where(lower, gtok_ref[r, 40:48, :], edge)
    gains.end(1)
    gains.begin(2)
    advance(late, 5)
    gains.end(2)
    gains.begin(3)
    advance(early, 7)
    advance(late, 6)
    gains.end(3)
    outs_ref[...] = small[4]
    advance(late, 7)
    advance(early, 8)
    advance(late, 8)
    gains.finish()
    for halo in halos:
        halo.left()


def step_kernel(tokens, bias, gain_a, w_qkv, w_out, grad_merged, w_merge, gain_m):
    vmem = pl.BlockSpec(memory_space=pltpu.VMEM)
    hbm = pl.BlockSpec(memory_space=pl.ANY)
    lanes = (384, 384, 256, 128, 128, 128, 128)
    sums = []
    for n in lanes:
        sums += sum_scratch(TALL, n)
    return pl.pallas_call(
        step_body,
        in_specs=[hbm, vmem, vmem, hbm, hbm, hbm, hbm, vmem],
        out_specs=[vmem] * 5,
        out_shape=[
            jax.ShapeDtypeStruct((ROWS // 2, COLS // 2, C2), BF),
            jax.ShapeDtypeStruct((ROWS, COLS, C), F32),
            jax.ShapeDtypeStruct((C4, C2), BF),
            jax.ShapeDtypeStruct((TALL, C), BF),
            jax.ShapeDtypeStruct((8, C), F32),
        ],
        scratch_shapes=[
            pltpu.VMEM((27, COLS, C), BF),
            pltpu.VMEM((14, 16, C), BF),
            pltpu.VMEM((12, 16, C), BF),
            pltpu.VMEM((C, 3 * C), BF),
            pltpu.VMEM((C, C), BF),
            pltpu.VMEM((ROWS // 2, COLS // 2, C2), BF),
            pltpu.VMEM((C4, C2), BF),
            pltpu.VMEM((WROWS * NW, WIN, 3 * C), BF),
            pltpu.VMEM((WROWS * NW, PAIRS, WIN, 2 * WIN), BF),
            pltpu.VMEM((ROWS * COLS, C), BF),
            pltpu.VMEM((NW, WIN, C), F32),
            pltpu.VMEM((NW, WIN, C), F32),
            pltpu.VMEM((WLAT, FR, C), F32),
            pltpu.VMEM((27, COLS, C), BF),
            pltpu.VMEM((14, 16, C), BF),
            pltpu.VMEM((12, 16, C), BF),
            pltpu.VMEM((4, CH, COLS, 128), F32),
            pltpu.VMEM((MALL, C4), F32),
            pltpu.VMEM((MALL, 1), F32),
            pltpu.VMEM((MALL, C4), BF),
            pltpu.VMEM((C4, C2), BF),
            pltpu.VMEM((TALL, C), BF),
            pltpu.VMEM((ROWS, COLS, C), BF),
            pltpu.VMEM((27, COLS, C), BF),
            pltpu.VMEM((14, 16, C), BF),
            pltpu.VMEM((12, 16, C), BF),
            pltpu.VMEM((NW, WIN, 3 * C), F32),
            pltpu.VMEM((ROWS * COLS, 3 * C), BF),
            pltpu.VMEM((21, COLS, C), BF),
            pltpu.VMEM((12, 16, C), BF),
            pltpu.VMEM((3, COLS, C), BF),
            pltpu.VMEM((14, 16, C), BF),
            pltpu.VMEM((5, 8, C), F32),
            pltpu.VMEM((10, 8, C), F32),
            pltpu.VMEM((1, C4), F32),
            pltpu.VMEM((1, C), F32),
            pltpu.SemaphoreType.DMA((5,)),
            pltpu.SemaphoreType.DMA((4, 3)),
            pltpu.SemaphoreType.DMA((4, 3)),
            pltpu.SemaphoreType.DMA((7, SUM_COPIES)),
            pltpu.SemaphoreType.DMA((7, SUM_COPIES)),
            pltpu.SemaphoreType.DMA((10,)),
            pltpu.SemaphoreType.DMA((10,)),
        ]
        + sums,
        compiler_params=pltpu.CompilerParams(
            vmem_limit_bytes=62 * MIB, collective_id=0, has_side_effects=True
        ),
        name="step",
    )(tokens, bias, gain_a, w_qkv, w_out, grad_merged, w_merge, gain_m)


def on_device(tokens, lat_band, gain_attn, w_qkv, w_out, gain_merge, w_merge, grad_merged):
    half_lat = WLAT // 2
    band_count = lat_band.shape[0]
    extended = jnp.concatenate([lat_band[band_count - half_lat :], lat_band])
    band_rows = lax.dynamic_slice_in_dim(extended, lax.axis_index("lat") * ROWS, ROWS)
    labels = jnp.repeat(band_rows.reshape(-1, WLAT), WLON, axis=1)
    bias = jnp.where(labels[:, :, None] == jnp.tile(labels, (1, 2))[:, None, :], 0.0, -1e30).astype(F32)
    merged, grad_tokens, sum_merge, sum_qo, sum_gain = step_kernel(
        tokens, bias, gain_attn.reshape(1, C), w_qkv, w_out, grad_merged, w_merge, gain_merge.reshape(1, C4)
    )
    groups = [sum_qo[C * (g // 3) : C * (g // 3 + 1), 128 * (1 + g % 3) : 128 * (2 + g % 3)] for g in range(12)]
    outs = [sum_qo[C * n : C * (n + 1), 0:128] for n in range(4)]
    return (
        merged,
        grad_tokens,
        sum_gain[0],
        jnp.concatenate(groups, axis=1).astype(F32),
        jnp.concatenate(outs, axis=1).astype(F32),
        sum_gain[1:5].reshape(C4),
        sum_merge.astype(F32),
    )


def solution(mesh):
    return jax.shard_map(
        on_device,
        mesh=mesh,
        in_specs=(P("lat", "lon", None), P(), P(), P(), P(), P(), P(), P("lat", "lon", None)),
        out_specs=(P("lat", "lon", None), P("lat", "lon", None), P(), P(), P(), P(), P()),
        check_vma=False,
    )
```

```python
import functools
import jax
import jax.numpy as jnp
from jax import lax
from jax.experimental import pallas as pl
from jax.experimental.pallas import tpu as pltpu
from jax.sharding import PartitionSpec as P

HEADS = 8
WLAT = 6
WLON = 12
EPSILON = 1e-05
F32 = jnp.float32
BF = jnp.bfloat16
ROWS = 24
COLS = 48
C = 512
WIN = 72
NW = COLS // WLON
PAIRS = HEADS // 2
MIB = 1 << 20


def dot(a, b, ca, cb):
    return lax.dot_general(a, b, (((ca,), (cb,)), ((), ())), preferred_element_type=F32)


def head_masks(scale):
    lane = lax.broadcasted_iota(jnp.int32, (1, 128), 1)
    low = jnp.where(lane < 64, scale, 0.0).astype(F32)
    high = jnp.where(lane < 64, 0.0, scale).astype(F32)
    return low, high


def stacked(value, masks):
    return jnp.concatenate([value * masks[0], value * masks[1]], axis=0).astype(BF)


def merged_heads(value):
    lane = lax.broadcasted_iota(jnp.int32, (WIN, 128), 1)
    return jnp.where(lane < 64, value[:WIN], value[WIN:])


def moments(x):
    mean = jnp.mean(x, axis=-1, keepdims=True)
    centered = x - mean
    var = jnp.mean(centered * centered, axis=-1, keepdims=True)
    rstd = lax.rsqrt(var + EPSILON)
    return centered * rstd, rstd


AXES = ("x", "y", "z")


def coordinates():
    lat = lax.axis_index("lat")
    lon = lax.axis_index("lon")
    return {"x": lon // 4, "y": (lat // 4) * 2 + (lon // 2) % 2, "z": lat % 4, "core": lon % 2}


def device(at):
    return ((at["y"] // 2) * 4 + at["z"], at["x"] * 4 + (at["y"] % 2) * 2 + at["core"])


def peer(at, axis, step):
    size = 2 if axis == "core" else 4
    return device({**at, axis: (at[axis] + step) % size})


def remote(src, dst, send, recv, target):
    return pltpu.make_async_remote_copy(
        src_ref=src, dst_ref=dst, send_sem=send, recv_sem=recv,
        device_id=target, device_id_type=pl.DeviceIdType.MESH,
    )


def neighbour(rows, cols):
    lat = lax.axis_index("lat")
    lon = lax.axis_index("lon")
    return ((lat + rows) % 8, (lon + cols) % 16)


EDGES = ((0, 1), (1, 0), (1, 1))


def greet(at):
    barrier = pltpu.get_barrier_semaphore()
    targets = [
        peer(at, axis, step)
        for axis, count in (("core", 2), ("x", 4), ("y", 4), ("z", 4))
        for step in range(1, count)
    ]
    targets += [neighbour(sign * r, sign * c) for sign in (1, -1) for r, c in EDGES]
    for target in targets:
        pl.semaphore_signal(barrier, inc=1, device_id=target, device_id_type=pl.DeviceIdType.MESH)
    pl.semaphore_wait(barrier, len(targets))


def add_rows(dst, start, terms, rows):
    chunk = min(rows, 64)

    def body(i, carry):
        total = None
        for ref, first in terms:
            piece = ref[pl.ds(pl.multiple_of(first + i * chunk, 16), chunk), :].astype(F32)
            total = piece if total is None else total + piece
        dst[pl.ds(pl.multiple_of(start + i * chunk, 16), chunk), :] = total.astype(dst.dtype)
        return carry

    lax.fori_loop(0, rows // chunk, body, 0)


class Sum:
    def __init__(self, at, src, out, order, recvs, send, recv):
        self.at, self.src, self.out, self.order = at, src, out, order
        self.recvs, self.send, self.recv = recvs, send, recv
        self.rows = src.shape[0]
        self.sent = []

    def start(self, src, dst, index, target):
        copy = remote(src, dst, self.send.at[index], self.recv.at[index], target)
        copy.start()
        self.sent.append(copy)
        return copy

    def block(self, level):
        return self.rows // 2 // 4**level

    def first(self, levels):
        first = self.at["core"] * (self.rows // 2)
        for level in range(levels):
            first = first + self.at[self.order[level]] * self.block(level + 1)
        return pl.multiple_of(first, 16)

    def begin(self):
        half = self.rows // 2
        theirs = pl.ds(pl.multiple_of((1 - self.at["core"]) * half, 16), half)
        self.last = [self.start(self.src.at[theirs, :], self.recvs[0].at[0], 0, peer(self.at, "core", 1))]

    def combine(self, level):
        for copy in self.last:
            copy.wait_recv()
        count = self.block(level)
        first = self.first(level)
        terms = [(self.src, first)] + [(self.recvs[level].at[s], 0) for s in range(1 if level == 0 else 3)]
        if level == 3:
            add_rows(self.out, first, terms, count)
            self.gather(3)
            return
        add_rows(self.src, first, terms, count)
        axis = self.order[level]
        block = self.block(level + 1)
        self.last = []
        for step in range(1, 4):
            there = pl.multiple_of(first + (self.at[axis] + step) % 4 * block, 16)
            self.last.append(
                self.start(
                    self.src.at[pl.ds(there, block), :], self.recvs[level + 1].at[step - 1],
                    3 * level + step, peer(self.at, axis, step),
                )
            )

    def gather(self, level):
        mine = self.out.at[pl.ds(self.first(level), self.block(level)), :]
        if level == 0:
            self.last = [self.start(mine, mine, 19, peer(self.at, "core", 1))]
            return
        axis = self.order[level - 1]
        self.last = [
            self.start(mine, mine, 10 + 3 * (level - 1) + step - 1, peer(self.at, axis, step)) for step in range(1, 4)
        ]

    def gathered(self, level):
        for copy in self.last:
            copy.wait_recv()
        self.gather(level - 1)

    def finish(self):
        self.last[0].wait_recv()
        for copy in self.sent:
            copy.wait_send()

    def step(self, n):
        if n == 0:
            self.begin()
        elif n < 5:
            self.combine(n - 1)
        elif n < 8:
            self.gathered(8 - n)
        else:
            self.finish()


SUM_COPIES = 20


def sum_scratch(rows, lanes):
    half = rows // 2
    return [pltpu.VMEM((1, half, lanes), BF)] + [pltpu.VMEM((3, half // 4**n, lanes), BF) for n in (1, 2, 3)]


class SmallSum:
    def __init__(self, at, block, slots, send, recv):
        self.at, self.block, self.slots, self.send, self.recv = at, block, slots, send, recv
        self.sent = []

    def begin(self, level):
        axis, count = (("core", 2), ("x", 4), ("y", 4), ("z", 4))[level]
        base = 0 if level == 0 else 3 * level - 2
        self.last = []
        for step in range(1, count):
            i = base + step - 1
            copy = remote(self.block.at[level], self.slots.at[i], self.send.at[i], self.recv.at[i],
                          peer(self.at, axis, step))
            copy.start()
            self.last.append((copy, i))
            self.sent.append(copy)

    def end(self, level):
        total = self.block[level]
        for copy, i in self.last:
            copy.wait_recv()
            total = total + self.slots[i]
        self.block[level + 1] = total

    def finish(self):
        for copy in self.sent:
            copy.wait_send()

CH = 4
NCH = ROWS // CH
MT = (CH // 2) * (COLS // 2)
MALL = NCH * MT
C4 = 4 * C
C2 = 1024
WROWS = ROWS // WLAT
NWT = NW * WIN
FR = COLS + 8
TALL = 4 * C


class Halo:
    def __init__(self, send, recv):
        self.send, self.recv, self.copies = send, recv, []

    def start(self, src, dst, rows, cols):
        n = len(self.copies)
        copy = remote(src, dst, self.send.at[n], self.recv.at[n], neighbour(rows, cols))
        copy.start()
        self.copies.append(copy)
        return copy

    def left(self):
        for copy in self.copies:
            copy.wait_send()


def band_bias(band_ref, bias):
    band = band_ref[...].astype(F32)
    total = band.shape[1]

    def grid_row(place, first):
        row = first + jnp.floor((place.astype(F32) + 0.5) * (1.0 / WLON)).astype(jnp.int32)
        return jnp.where(row >= total, row - total, row)

    for w in range(WROWS):
        first = (lax.axis_index("lat") * ROWS + WLAT * w - 3 + total) % total
        key = lax.broadcasted_iota(jnp.int32, (WIN, total), 0)
        hit = grid_row(key, first) == lax.broadcasted_iota(jnp.int32, (WIN, total), 1)
        keys = jnp.sum(jnp.where(hit, band, 0.0), axis=1, keepdims=True)
        query = lax.broadcasted_iota(jnp.int32, (total, 2 * WIN), 1)
        query = jnp.where(query >= WIN, query - WIN, query)
        hit = grid_row(query, first) == lax.broadcasted_iota(jnp.int32, (total, 2 * WIN), 0)
        queries = dot(jnp.broadcast_to(band, (8, total)).astype(BF), jnp.where(hit, 1.0, 0.0).astype(BF), 1, 0)
        bias[w] = jnp.where(keys == queries[0:1], 0.0, -1e30)


def pair_half(ref, pair, half):
    return ref[pair].astype(F32)[8 * half : 8 * half + 8]


def load_frame(fr, w, rows_ref, edge_ref):
    for r in range(WLAT):
        fr[r, 8:FR, :] = rows_ref[WLAT * w + r].astype(F32)
        fr[r, 0:8, :] = pair_half(edge_ref, 3 * w + (r + 1) // 2, (r + 1) % 2)


def to_windows(fr, dst):
    for v in range(NW):
        for r in range(WLAT):
            dst[v, WLON * r : WLON * (r + 1), :] = fr[r, WLON * v + 2 : WLON * v + 14, :]


def to_frame(src, fr):
    for v in range(NW):
        for r in range(WLAT):
            fr[r, WLON * v + 2 : WLON * v + 14, :] = src[v, WLON * r : WLON * (r + 1), :]


def pack_rows(fr, edge_ref, w):
    for r in range(0, WLAT, 2):
        edge_ref[3 * w + r // 2] = jnp.concatenate([fr[r, 0:8, :], fr[r + 1, 0:8, :]], axis=0).astype(BF)


def step_body(tok_hbm, band_ref, ga_ref, wq_hbm, wo_hbm, gm_hbm, wm_hbm, gmg_ref,
              merged_ref, gtok_ref, outm_ref, outq_ref, outs_ref,
              text, hw, pk, wq, wo, gmb, wm, qkv, prob, nrm, qf, s2, fr, attx, he, bw,
              s1, xh, rs, mi, gi, gwm, qo, gmix, gext, gw, pkg, dq, dall, bn2, bw2, hs2, he2,
              small, slots, ggm, gga, bias, lsem, hsend, hrecv, send, recv, ssend, srecv, *sums):
    loads = [
        pltpu.make_async_copy(src, dst, lsem.at[n])
        for n, (src, dst) in enumerate(
            [(tok_hbm, text.at[pl.ds(3, ROWS)]), (wq_hbm, wq), (wo_hbm, wo), (gm_hbm, gmb), (wm_hbm, wm)]
        )
    ]
    for load in loads:
        load.start()
    at = coordinates()
    greet(at)
    halos = [Halo(hsend.at[n], hrecv.at[n]) for n in range(4)]

    loads[0].wait()

    def pack_tokens(first, count):
        for m in range(first, first + count):
            pk[m] = jnp.concatenate(
                [text[3 + 2 * m + k, 32:48, :].astype(F32)[8:16] for k in range(2)], axis=0
            ).astype(BF)
        return halos[0].start(pk.at[pl.ds(first, count)], hw.at[pl.ds(first + 2, count)], 0, 1)

    north = [halos[0].start(text.at[pl.ds(24, 3)], text.at[pl.ds(0, 3)], 1, 0)]
    west = [pack_tokens(1, 4), pack_tokens(5, 7)]
    north.append(pack_tokens(0, 1))
    north.append(halos[0].start(pk.at[pl.ds(10, 2)], hw.at[pl.ds(0, 2)], 1, 1))
    band_bias(band_ref, bias)
    loads[1].wait()

    def forward_row(w, carry):
        load_frame(fr, w, text, hw)
        xhat, _ = moments(fr[...])
        fr[...] = xhat * ga_ref[...].reshape(1, 1, C)
        to_windows(fr, s2)
        normed = s2[...].reshape(NWT, C).astype(BF)
        nrm[pl.ds(pl.multiple_of(w * NWT, NWT), NWT), :] = normed
        for t in range(3):
            part = dot(normed, wq[:, C * t : C * (t + 1)], 1, 0).reshape(NW, WIN, C)
            if t == 0:
                qf[...] = part
            qkv[pl.ds(NW * w, NW), :, C * t : C * (t + 1)] = part.astype(BF)
        mask = bias[w]

        def window(v, carry):
            masks = head_masks(0.125)
            n = NW * w + v
            for p in range(PAIRS):
                lanes = slice(128 * p, 128 * (p + 1))
                qs = stacked(qf[v, :, lanes].astype(BF).astype(F32), masks)
                k = qkv[n, :, C + 128 * p : C + 128 * (p + 1)]
                val = qkv[n, :, 2 * C + 128 * p : 2 * C + 128 * (p + 1)]
                s = dot(k, qs, 1, 1) + mask
                e = jnp.exp(s - jnp.max(s, axis=0, keepdims=True))
                pr = (e * (1.0 / jnp.sum(e, axis=0, keepdims=True))).astype(BF)
                prob[n, p] = pr
                s2[v, :, lanes] = merged_heads(dot(pr, val, 0, 0))
            return carry

        lax.fori_loop(0, NW, window, 0)
        to_frame(s2, fr)
        pack_rows(fr, bw, w)
        for r in range(WLAT):
            attx[WLAT * w + r] = fr[r, 8:FR, :].astype(BF)
        return carry

    def send_back(w):
        return halos[1].start(bw.at[pl.ds(3 * w, 3)], he.at[pl.ds(3 * w, 3)], 0, -1)

    west[0].wait_recv()
    lax.fori_loop(1, 2, forward_row, 0)
    east = [send_back(1)]
    for copy in north + west[1:]:
        copy.wait_recv()
    lax.fori_loop(0, 1, forward_row, 0)
    south = [
        halos[1].start(attx.at[pl.ds(0, 3)], attx.at[pl.ds(24, 3)], -1, 0),
        halos[1].start(bw.at[pl.ds(0, 2)], he.at[pl.ds(12, 2)], -1, -1),
    ]
    east.append(send_back(0))
    lax.fori_loop(2, 3, forward_row, 0)
    east.append(send_back(2))
    lax.fori_loop(3, 4, forward_row, 0)
    south.append(send_back(3))
    for load in loads[2:]:
        load.wait()
    for copy in east:
        copy.wait_recv()
    gain = gmg_ref[...]
    lower = lax.broadcasted_iota(jnp.int32, (8, C), 0) < 2

    def merge_forward(c, carry):
        pieces = []
        for i in range(CH):
            row = attx[CH * c + 3 + i].astype(F32)
            edge = pair_half(he, 2 * c + (3 + i) // 2, (3 + i) % 2)
            pieces.append(jnp.concatenate([row[:40], jnp.where(lower, row[40:], edge)], axis=0))
        att = jnp.concatenate(pieces, axis=0).astype(BF)
        attx[pl.ds(CH * c + 3, CH)] = att.reshape(CH, COLS, C)
        proj = dot(att, wo[...], 1, 0).reshape(CH, COLS, C)
        mixed = (text[pl.ds(CH * c + 3, CH)].astype(F32) + proj).astype(BF).astype(F32)
        for q in range(4):
            s1[q] = mixed[:, :, 128 * q : 128 * (q + 1)]
        parts = []
        for b in range(2):
            for a in range(2):
                for q in range(4):
                    piece = [s1[q, 2 * i + a, pl.ds(b, COLS // 2, stride=2), :] for i in range(CH // 2)]
                    parts.append(jnp.concatenate(piece, axis=0))
        xhat, rstd = moments(jnp.concatenate(parts, axis=1))
        here = pl.ds(pl.multiple_of(c * MT, MT), MT)
        xh[here, :] = xhat
        rs[here, :] = rstd
        mi[here, :] = (xhat * gain).astype(BF)
        return carry

    lax.fori_loop(0, 3, merge_forward, 0)
    for copy in south:
        copy.wait_recv()
    lax.fori_loop(3, NCH, merge_forward, 0)
    gm = gmb[...].astype(F32).reshape(MALL, C2).astype(BF)

    def merged_tile(n, carry):
        cols = pl.ds(pl.multiple_of(n * 256, 256), 256)
        tile = dot(mi[...], wm[:, cols], 1, 0).reshape(ROWS // 2, COLS // 2, 256)
        merged_ref[:, :, cols] = tile.astype(BF)
        return carry


    def wide_tile(n, carry):
        cols = pl.ds(pl.multiple_of(n * 256, 256), 256)
        gwm[cols, :] = dot(mi[:, cols], gm, 0, 0).astype(BF)
        gi[:, cols] = dot(gm, wm[cols, :], 1, 1).astype(BF)
        return carry

    lax.fori_loop(0, C4 // 256, wide_tile, 0)

    def summed(src, out, turn, n):
        order = AXES[turn:] + AXES[:turn]
        return Sum(at, src, out, order, sums[4 * n : 4 * n + 4], send.at[n], recv.at[n])

    wide = [
        summed(gwm.at[:, 0:384], outm_ref.at[:, 0:384], 0, 0),
        summed(gwm.at[:, 384:768], outm_ref.at[:, 384:768], 1, 1),
        summed(gwm.at[:, 768:1024], outm_ref.at[:, 768:1024], 2, 2),
    ]
    early = wide + [summed(qo.at[:, 0:128], outq_ref.at[:, 0:128], 2, 3)]
    late = [
        summed(qo.at[:, 128 * (t + 1) : 128 * (t + 2)], outq_ref.at[:, 128 * (t + 1) : 128 * (t + 2)], t, 4 + t)
        for t in range(3)
    ]

    def advance(group, n):
        for part in group:
            part.step(n)

    advance(wide, 0)
    ggm[...] = jnp.zeros_like(ggm)

    def merge_backward(c, carry):
        here = pl.ds(pl.multiple_of(c * MT, MT), MT)
        xhat = xh[here, :]
        g = gi[here, :].astype(F32)
        ggm[...] += jnp.sum(g * xhat, axis=0, keepdims=True)
        dx = g * gain
        m1 = jnp.mean(dx, axis=-1, keepdims=True)
        m2 = jnp.mean(dx * xhat, axis=-1, keepdims=True)
        dx = rs[here, :] * (dx - m1 - xhat * m2)
        for b in range(2):
            for a in range(2):
                for q in range(4):
                    start = C * (2 * b + a) + 128 * q
                    for i in range(CH // 2):
                        s1[q, 2 * i + a, pl.ds(b, COLS // 2, stride=2), :] = dx[
                            (COLS // 2) * i : (COLS // 2) * (i + 1), start : start + 128
                        ]
        mixed = jnp.concatenate([s1[q] for q in range(4)], axis=-1).astype(BF)
        gmix[pl.ds(c * CH, CH)] = mixed
        gatt = dot(mixed.reshape(CH * COLS, C), wo[...], 1, 1).reshape(CH, COLS, C)
        gext[pl.ds(CH * c + 3, CH)] = gatt.astype(BF)
        for m in range(CH // 2):
            pkg[(CH // 2) * c + m] = jnp.concatenate(
                [gatt[2 * m, 40:48], gatt[2 * m + 1, 40:48]], axis=0
            ).astype(BF)
        return carry

    def send_cotangents(first, count):
        return halos[2].start(pkg.at[pl.ds(first, count)], gw.at[pl.ds(first + 2, count)], 0, 1)

    lax.fori_loop(5, 6, merge_backward, 0)
    halos[2].start(gext.at[pl.ds(24, 3)], gext.at[pl.ds(0, 3)], 1, 0)
    halos[2].start(pkg.at[pl.ds(10, 2)], gw.at[pl.ds(0, 2)], 1, 1)
    send_cotangents(10, 2)
    lax.fori_loop(0, 3, merge_backward, 0)
    send_cotangents(0, 6)
    lax.fori_loop(3, 5, merge_backward, 0)
    send_cotangents(6, 4)
    flat = gmix[...].reshape(ROWS * COLS, C)
    att = attx[pl.ds(3, ROWS)].reshape(ROWS * COLS, C)
    gwo = dot(att, flat, 0, 0).astype(BF)
    for n in range(4):
        qo[C * n : C * (n + 1), 0:128] = gwo[:, 128 * n : 128 * (n + 1)]
    early[3].step(0)
    advance(early, 1)
    for copy in halos[2].copies:
        copy.wait_recv()

    def backward_row(w, carry):
        load_frame(fr, w, gext, gw)
        to_windows(fr, s2)

        def window(v, carry):
            masks = head_masks(1.0)
            scaled = head_masks(0.125)
            n = NW * w + v
            for p in range(PAIRS):
                lanes = slice(128 * p, 128 * (p + 1))
                qs = stacked(qkv[n, :, lanes].astype(F32), scaled)
                k = qkv[n, :, C + 128 * p : C + 128 * (p + 1)]
                val = qkv[n, :, 2 * C + 128 * p : 2 * C + 128 * (p + 1)]
                gs = stacked(s2[v, :, lanes], masks)
                pr = prob[n, p]
                pf = pr.astype(F32)
                dp = dot(val, gs, 1, 1)
                delta = jnp.sum(pf * dp, axis=0, keepdims=True)
                ds = (pf * (dp - delta)).astype(BF)
                dq[v, :, lanes] = merged_heads(dot(ds, k, 0, 0)) * 0.125
                dq[v, :, C + 128 * p : C + 128 * (p + 1)] = dot(ds, qs, 1, 0)
                dq[v, :, 2 * C + 128 * p : 2 * C + 128 * (p + 1)] = dot(pr, gs, 1, 0)
            return carry

        lax.fori_loop(0, NW, window, 0)
        dall[pl.ds(pl.multiple_of(w * NWT, NWT), NWT), :] = dq[...].reshape(NWT, 3 * C).astype(BF)
        return carry

    lax.fori_loop(0, 3, backward_row, 0)
    advance(early, 2)
    lax.fori_loop(3, 4, backward_row, 0)
    advance(early, 3)
    for n in range(6):
        tile = dot(nrm[...], dall[:, 256 * n : 256 * (n + 1)], 0, 0).astype(BF)
        for k in range(2):
            g = 2 * n + k
            qo[C * (g // 3) : C * (g // 3 + 1), 128 * (1 + g % 3) : 128 * (2 + g % 3)] = tile[:, 128 * k : 128 * (k + 1)]
    advance(late, 0)
    advance(early, 4)
    gga[...] = jnp.zeros_like(gga)

    def dgrad_row(w, carry):
        rows = pl.ds(pl.multiple_of(w * NWT, NWT), NWT)
        s2[...] = dot(dall[rows, :], wq[...], 1, 1).astype(BF).astype(F32).reshape(NW, WIN, C)
        load_frame(fr, w, text, hw)
        xhat, rstd = moments(fr[...])
        fr[:, 0:8, :] = jnp.zeros((WLAT, 8, C), F32)
        fr[:, FR - 8 : FR, :] = jnp.zeros((WLAT, 8, C), F32)
        to_frame(s2, fr)
        g = fr[...]
        gga[...] += jnp.sum(g * xhat, axis=(0, 1)).reshape(1, C)
        dx = g * ga_ref[...].reshape(1, 1, C)
        m1 = jnp.mean(dx, axis=-1, keepdims=True)
        m2 = jnp.mean(dx * xhat, axis=-1, keepdims=True)
        fr[...] = rstd * (dx - m1 - xhat * m2)
        pack_rows(fr, bw2, w)
        for r in range(3):
            bn2[WLAT * w + r] = fr[r, 8:FR, :].astype(BF)
        for r in range(3):
            gtok_ref[WLAT * w + r] = fr[3 + r, 8:FR, :] + gmix[WLAT * w + r].astype(F32)

        @pl.when(w > 0)
        def _():
            for r in range(3):
                gtok_ref[WLAT * w - 3 + r] = fr[r, 8:FR, :] + gmix[WLAT * w - 3 + r].astype(F32)

        return carry

    lax.fori_loop(0, 1, dgrad_row, 0)
    halos[3].start(bn2.at[pl.ds(0, 3)], hs2, -1, 0)
    halos[3].start(bw2.at[pl.ds(0, 2)], he2.at[pl.ds(12, 2)], -1, -1)
    advance(late, 1)
    lax.fori_loop(1, 2, dgrad_row, 0)
    halos[3].start(bw2.at[pl.ds(0, 6)], he2.at[pl.ds(0, 6)], 0, -1)
    advance(early, 5)
    lax.fori_loop(2, 4, dgrad_row, 0)
    halos[3].start(bw2.at[pl.ds(6, 6)], he2.at[pl.ds(6, 6)], 0, -1)
    advance(late, 2)
    advance(early, 6)
    lax.fori_loop(0, C2 // 256, merged_tile, 0)
    small[0] = jnp.zeros_like(small[0])
    small[0, 0:1, :] = gga[...]
    for n in range(4):
        small[0, 1 + n : 2 + n, :] = ggm[:, C * n : C * (n + 1)]
    gains = SmallSum(at, small, slots, ssend, srecv)
    gains.begin(0)
    advance(late, 3)
    gains.end(0)
    gains.begin(1)
    advance(late, 4)
    for copy in halos[3].copies:
        copy.wait_recv()
    for r in range(3):
        gtok_ref[21 + r] = hs2[r].astype(F32) + gmix[21 + r].astype(F32)
    for r in range(ROWS):
        edge = pair_half(he2, (r + 3) // 2, (r + 3) % 2) + gmix[r, 32:48, :].astype(F32)[8:16]
        gtok_ref[r, 40:48, :] = jnp.where(lower, gtok_ref[r, 40:48, :], edge)
    gains.end(1)
    gains.begin(2)
    advance(late, 5)
    gains.end(2)
    gains.begin(3)
    advance(early, 7)
    advance(late, 6)
    gains.end(3)
    outs_ref[...] = small[4]
    advance(late, 7)
    advance(early, 8)
    advance(late, 8)
    gains.finish()
    for halo in halos:
        halo.left()


def step_kernel(tokens, band, gain_a, w_qkv, w_out, grad_merged, w_merge, gain_m):
    vmem = pl.BlockSpec(memory_space=pltpu.VMEM)
    hbm = pl.BlockSpec(memory_space=pl.ANY)
    lanes = (384, 384, 256, 128, 128, 128, 128)
    sums = []
    for n in lanes:
        sums += sum_scratch(TALL, n)
    return pl.pallas_call(
        step_body,
        in_specs=[hbm, vmem, vmem, hbm, hbm, hbm, hbm, vmem],
        out_specs=[vmem] * 5,
        out_shape=[
            jax.ShapeDtypeStruct((ROWS // 2, COLS // 2, C2), BF),
            jax.ShapeDtypeStruct((ROWS, COLS, C), F32),
            jax.ShapeDtypeStruct((C4, C2), BF),
            jax.ShapeDtypeStruct((TALL, C), BF),
            jax.ShapeDtypeStruct((8, C), F32),
        ],
        scratch_shapes=[
            pltpu.VMEM((27, COLS, C), BF),
            pltpu.VMEM((14, 16, C), BF),
            pltpu.VMEM((12, 16, C), BF),
            pltpu.VMEM((C, 3 * C), BF),
            pltpu.VMEM((C, C), BF),
            pltpu.VMEM((ROWS // 2, COLS // 2, C2), BF),
            pltpu.VMEM((C4, C2), BF),
            pltpu.VMEM((WROWS * NW, WIN, 3 * C), BF),
            pltpu.VMEM((WROWS * NW, PAIRS, WIN, 2 * WIN), BF),
            pltpu.VMEM((ROWS * COLS, C), BF),
            pltpu.VMEM((NW, WIN, C), F32),
            pltpu.VMEM((NW, WIN, C), F32),
            pltpu.VMEM((WLAT, FR, C), F32),
            pltpu.VMEM((27, COLS, C), BF),
            pltpu.VMEM((14, 16, C), BF),
            pltpu.VMEM((12, 16, C), BF),
            pltpu.VMEM((4, CH, COLS, 128), F32),
            pltpu.VMEM((MALL, C4), F32),
            pltpu.VMEM((MALL, 1), F32),
            pltpu.VMEM((MALL, C4), BF),
            pltpu.VMEM((MALL, C4), BF),
            pltpu.VMEM((C4, C2), BF),
            pltpu.VMEM((TALL, C), BF),
            pltpu.VMEM((ROWS, COLS, C), BF),
            pltpu.VMEM((27, COLS, C), BF),
            pltpu.VMEM((14, 16, C), BF),
            pltpu.VMEM((12, 16, C), BF),
            pltpu.VMEM((NW, WIN, 3 * C), F32),
            pltpu.VMEM((ROWS * COLS, 3 * C), BF),
            pltpu.VMEM((21, COLS, C), BF),
            pltpu.VMEM((12, 16, C), BF),
            pltpu.VMEM((3, COLS, C), BF),
            pltpu.VMEM((14, 16, C), BF),
            pltpu.VMEM((5, 8, C), F32),
            pltpu.VMEM((10, 8, C), F32),
            pltpu.VMEM((1, C4), F32),
            pltpu.VMEM((1, C), F32),
            pltpu.VMEM((WROWS, WIN, 2 * WIN), F32),
            pltpu.SemaphoreType.DMA((5,)),
            pltpu.SemaphoreType.DMA((4, 6)),
            pltpu.SemaphoreType.DMA((4, 6)),
            pltpu.SemaphoreType.DMA((7, SUM_COPIES)),
            pltpu.SemaphoreType.DMA((7, SUM_COPIES)),
            pltpu.SemaphoreType.DMA((10,)),
            pltpu.SemaphoreType.DMA((10,)),
        ]
        + sums,
        compiler_params=pltpu.CompilerParams(
            vmem_limit_bytes=62 * MIB, collective_id=0, has_side_effects=True
        ),
        name="step",
    )(tokens, band, gain_a, w_qkv, w_out, grad_merged, w_merge, gain_m)


def widen_body(m_ref, q_ref, s_ref, gm_ref, gq_ref, go_ref, ga_ref, gg_ref):
    gm_ref[...] = m_ref[...].astype(F32)
    go_ref[...] = q_ref[:, 0:128].astype(F32)
    gq_ref[...] = q_ref[:, 128:].astype(F32)
    ga_ref[...] = s_ref[0:1, :]
    for n in range(4):
        gg_ref[:, C * n : C * (n + 1)] = s_ref[1 + n : 2 + n, :]


def widen(sum_merge, sum_qo, sum_gain):
    return pl.pallas_call(
        widen_body,
        grid=(4,),
        in_specs=[
            pl.BlockSpec((C, C2), lambda i: (i, 0)),
            pl.BlockSpec((C, C), lambda i: (i, 0)),
            pl.BlockSpec((8, C), lambda i: (0, 0)),
        ],
        out_specs=[
            pl.BlockSpec((C, C2), lambda i: (i, 0)),
            pl.BlockSpec((C, 384), lambda i: (0, i)),
            pl.BlockSpec((C, 128), lambda i: (0, i)),
            pl.BlockSpec((1, C), lambda i: (0, 0)),
            pl.BlockSpec((1, C4), lambda i: (0, 0)),
        ],
        out_shape=[
            jax.ShapeDtypeStruct((C4, C2), F32),
            jax.ShapeDtypeStruct((C, 3 * C), F32),
            jax.ShapeDtypeStruct((C, C), F32),
            jax.ShapeDtypeStruct((1, C), F32),
            jax.ShapeDtypeStruct((1, C4), F32),
        ],
        compiler_params=pltpu.CompilerParams(vmem_limit_bytes=32 * MIB),
        name="widen",
    )(sum_merge, sum_qo, sum_gain)


def on_device(tokens, lat_band, gain_attn, w_qkv, w_out, gain_merge, w_merge, grad_merged):
    merged, grad_tokens, sum_merge, sum_qo, sum_gain = step_kernel(
        tokens, lat_band.reshape(1, -1), gain_attn.reshape(1, C), w_qkv, w_out, grad_merged, w_merge,
        gain_merge.reshape(1, C4)
    )
    gw_merge, gw_qkv, gw_out, gg_attn, gg_merge = widen(sum_merge, sum_qo, sum_gain)
    return merged, grad_tokens, gg_attn.reshape(C), gw_qkv, gw_out, gg_merge.reshape(C4), gw_merge


def solution(mesh):
    return jax.shard_map(
        on_device,
        mesh=mesh,
        in_specs=(P("lat", "lon", None), P(), P(), P(), P(), P(), P(), P("lat", "lon", None)),
        out_specs=(P("lat", "lon", None), P("lat", "lon", None), P(), P(), P(), P(), P()),
        check_vma=False,
    )
```

```python
import functools
import jax
import jax.numpy as jnp
from jax import lax
from jax.experimental import pallas as pl
from jax.experimental.pallas import tpu as pltpu
from jax.sharding import PartitionSpec as P

HEADS = 8
WLAT = 6
WLON = 12
EPSILON = 1e-05
F32 = jnp.float32
BF = jnp.bfloat16
ROWS = 24
COLS = 48
C = 512
WIN = 72
NW = COLS // WLON
PAIRS = HEADS // 2
MIB = 1 << 20


def dot(a, b, ca, cb):
    return lax.dot_general(a, b, (((ca,), (cb,)), ((), ())), preferred_element_type=F32)


def head_masks(scale):
    lane = lax.broadcasted_iota(jnp.int32, (1, 128), 1)
    low = jnp.where(lane < 64, scale, 0.0).astype(F32)
    high = jnp.where(lane < 64, 0.0, scale).astype(F32)
    return low, high


def stacked(value, masks):
    return jnp.concatenate([value * masks[0], value * masks[1]], axis=0).astype(BF)


def merged_heads(value):
    lane = lax.broadcasted_iota(jnp.int32, (WIN, 128), 1)
    return jnp.where(lane < 64, value[:WIN], value[WIN:])


def moments(x):
    mean = jnp.mean(x, axis=-1, keepdims=True)
    centered = x - mean
    var = jnp.mean(centered * centered, axis=-1, keepdims=True)
    rstd = lax.rsqrt(var + EPSILON)
    return centered * rstd, rstd


AXES = ("x", "y", "z")


def coordinates():
    lat = lax.axis_index("lat")
    lon = lax.axis_index("lon")
    return {"x": lon // 4, "y": (lat // 4) * 2 + (lon // 2) % 2, "z": lat % 4, "core": lon % 2}


def device(at):
    return ((at["y"] // 2) * 4 + at["z"], at["x"] * 4 + (at["y"] % 2) * 2 + at["core"])


def peer(at, axis, step):
    size = 2 if axis == "core" else 4
    return device({**at, axis: (at[axis] + step) % size})


def remote(src, dst, send, recv, target):
    return pltpu.make_async_remote_copy(
        src_ref=src, dst_ref=dst, send_sem=send, recv_sem=recv,
        device_id=target, device_id_type=pl.DeviceIdType.MESH,
    )


def neighbour(rows, cols):
    lat = lax.axis_index("lat")
    lon = lax.axis_index("lon")
    return ((lat + rows) % 8, (lon + cols) % 16)


EDGES = ((0, 1), (1, 0), (1, 1))


def greet(at):
    barrier = pltpu.get_barrier_semaphore()
    targets = [
        peer(at, axis, step)
        for axis, count in (("core", 2), ("x", 4), ("y", 4), ("z", 4))
        for step in range(1, count)
    ]
    targets += [neighbour(sign * r, sign * c) for sign in (1, -1) for r, c in EDGES]
    for target in targets:
        pl.semaphore_signal(barrier, inc=1, device_id=target, device_id_type=pl.DeviceIdType.MESH)
    pl.semaphore_wait(barrier, len(targets))


def add_rows(dst, start, terms, rows):
    chunk = min(rows, 64)

    def body(i, carry):
        total = None
        for ref, first in terms:
            piece = ref[pl.ds(pl.multiple_of(first + i * chunk, 16), chunk), :].astype(F32)
            total = piece if total is None else total + piece
        dst[pl.ds(pl.multiple_of(start + i * chunk, 16), chunk), :] = total.astype(dst.dtype)
        return carry

    lax.fori_loop(0, rows // chunk, body, 0)


class Sum:
    def __init__(self, at, src, out, order, recvs, send, recv):
        self.at, self.src, self.out, self.order = at, src, out, order
        self.recvs, self.send, self.recv = recvs, send, recv
        self.rows = src.shape[0]
        self.sent = []

    def start(self, src, dst, index, target):
        copy = remote(src, dst, self.send.at[index], self.recv.at[index], target)
        copy.start()
        self.sent.append(copy)
        return copy

    def block(self, level):
        return self.rows // 2 // 4**level

    def first(self, levels):
        first = self.at["core"] * (self.rows // 2)
        for level in range(levels):
            first = first + self.at[self.order[level]] * self.block(level + 1)
        return pl.multiple_of(first, 16)

    def begin(self):
        half = self.rows // 2
        theirs = pl.ds(pl.multiple_of((1 - self.at["core"]) * half, 16), half)
        self.last = [self.start(self.src.at[theirs, :], self.recvs[0].at[0], 0, peer(self.at, "core", 1))]

    def combine(self, level):
        for copy in self.last:
            copy.wait_recv()
        count = self.block(level)
        first = self.first(level)
        terms = [(self.src, first)] + [(self.recvs[level].at[s], 0) for s in range(1 if level == 0 else 3)]
        if level == 3:
            add_rows(self.out, first, terms, count)
            self.gather(3)
            return
        add_rows(self.src, first, terms, count)
        axis = self.order[level]
        block = self.block(level + 1)
        self.last = []
        for step in range(1, 4):
            there = pl.multiple_of(first + (self.at[axis] + step) % 4 * block, 16)
            self.last.append(
                self.start(
                    self.src.at[pl.ds(there, block), :], self.recvs[level + 1].at[step - 1],
                    3 * level + step, peer(self.at, axis, step),
                )
            )

    def gather(self, level):
        mine = self.out.at[pl.ds(self.first(level), self.block(level)), :]
        if level == 0:
            self.last = [self.start(mine, mine, 19, peer(self.at, "core", 1))]
            return
        axis = self.order[level - 1]
        self.last = [
            self.start(mine, mine, 10 + 3 * (level - 1) + step - 1, peer(self.at, axis, step)) for step in range(1, 4)
        ]

    def gathered(self, level):
        for copy in self.last:
            copy.wait_recv()
        self.gather(level - 1)

    def finish(self):
        self.last[0].wait_recv()
        for copy in self.sent:
            copy.wait_send()

    def step(self, n):
        if n == 0:
            self.begin()
        elif n < 5:
            self.combine(n - 1)
        elif n < 8:
            self.gathered(8 - n)
        else:
            self.finish()


SUM_COPIES = 20


def sum_scratch(rows, lanes):
    half = rows // 2
    return [pltpu.VMEM((1, half, lanes), BF)] + [pltpu.VMEM((3, half // 4**n, lanes), BF) for n in (1, 2, 3)]


class SmallSum:
    def __init__(self, at, block, slots, send, recv):
        self.at, self.block, self.slots, self.send, self.recv = at, block, slots, send, recv
        self.sent = []

    def begin(self, level):
        axis, count = (("core", 2), ("x", 4), ("y", 4), ("z", 4))[level]
        base = 0 if level == 0 else 3 * level - 2
        self.last = []
        for step in range(1, count):
            i = base + step - 1
            copy = remote(self.block.at[level], self.slots.at[i], self.send.at[i], self.recv.at[i],
                          peer(self.at, axis, step))
            copy.start()
            self.last.append((copy, i))
            self.sent.append(copy)

    def end(self, level):
        total = self.block[level]
        for copy, i in self.last:
            copy.wait_recv()
            total = total + self.slots[i]
        self.block[level + 1] = total

    def finish(self):
        for copy in self.sent:
            copy.wait_send()

CH = 4
NCH = ROWS // CH
MT = (CH // 2) * (COLS // 2)
MALL = NCH * MT
C4 = 4 * C
C2 = 1024
WROWS = ROWS // WLAT
NWT = NW * WIN
FR = COLS + 8
TALL = 4 * C


class Halo:
    def __init__(self, send, recv):
        self.send, self.recv, self.copies = send, recv, []

    def start(self, src, dst, rows, cols):
        n = len(self.copies)
        copy = remote(src, dst, self.send.at[n], self.recv.at[n], neighbour(rows, cols))
        copy.start()
        self.copies.append(copy)
        return copy

    def left(self):
        for copy in self.copies:
            copy.wait_send()


def band_bias(band_ref, bias):
    band = band_ref[...].astype(F32)
    total = band.shape[1]

    def grid_row(place, first):
        row = first + jnp.floor((place.astype(F32) + 0.5) * (1.0 / WLON)).astype(jnp.int32)
        return jnp.where(row >= total, row - total, row)

    for w in range(WROWS):
        first = (lax.axis_index("lat") * ROWS + WLAT * w - 3 + total) % total
        key = lax.broadcasted_iota(jnp.int32, (WIN, total), 0)
        hit = grid_row(key, first) == lax.broadcasted_iota(jnp.int32, (WIN, total), 1)
        keys = jnp.sum(jnp.where(hit, band, 0.0), axis=1, keepdims=True)
        query = lax.broadcasted_iota(jnp.int32, (total, 2 * WIN), 1)
        query = jnp.where(query >= WIN, query - WIN, query)
        hit = grid_row(query, first) == lax.broadcasted_iota(jnp.int32, (total, 2 * WIN), 0)
        queries = dot(jnp.broadcast_to(band, (8, total)).astype(BF), jnp.where(hit, 1.0, 0.0).astype(BF), 1, 0)
        bias[w] = jnp.where(keys == queries[0:1], 0.0, -1e30)


def pair_half(ref, pair, half):
    return ref[pair].astype(F32)[8 * half : 8 * half + 8]


def load_frame(fr, w, rows_ref, edge_ref):
    for r in range(WLAT):
        fr[r, 8:FR, :] = rows_ref[WLAT * w + r].astype(F32)
        fr[r, 0:8, :] = pair_half(edge_ref, 3 * w + (r + 1) // 2, (r + 1) % 2)


def to_windows(fr, dst):
    for v in range(NW):
        for r in range(WLAT):
            dst[v, WLON * r : WLON * (r + 1), :] = fr[r, WLON * v + 2 : WLON * v + 14, :]


def to_frame(src, fr):
    for v in range(NW):
        for r in range(WLAT):
            fr[r, WLON * v + 2 : WLON * v + 14, :] = src[v, WLON * r : WLON * (r + 1), :]


def pack_rows(fr, edge_ref, w):
    for r in range(0, WLAT, 2):
        edge_ref[3 * w + r // 2] = jnp.concatenate([fr[r, 0:8, :], fr[r + 1, 0:8, :]], axis=0).astype(BF)


def step_body(tok_hbm, band_ref, ga_ref, wq_hbm, wo_hbm, gm_hbm, wm_hbm, gmg_ref,
              merged_out, gtok_out, outm_out, outq_out, outs_ref,
              merged_ref, gtok_ref, outm_ref, outq_ref,
              text, hw, pk, wq, wo, gmb, wm, qkv, prob, qst, nrm, qf, s2, fr, attx, he, bw,
              s1, xh, rs, mi, gi, gwm, qo, gmix, gext, gw, pkg, dq, dall, bn2, bw2, hs2, he2,
              small, slots, ggm, gga, bias, lsem, hsend, hrecv, send, recv, ssend, srecv, *sums):
    loads = [
        pltpu.make_async_copy(src, dst, lsem.at[n])
        for n, (src, dst) in enumerate(
            [(tok_hbm, text.at[pl.ds(3, ROWS)]), (wq_hbm, wq), (wo_hbm, wo), (gm_hbm, gmb), (wm_hbm, wm)]
        )
    ]
    for load in loads:
        load.start()
    at = coordinates()
    greet(at)
    halos = [Halo(hsend.at[n], hrecv.at[n]) for n in range(4)]

    loads[0].wait()

    def pack_tokens(first, count):
        for m in range(first, first + count):
            pk[m] = jnp.concatenate(
                [text[3 + 2 * m + k, 32:48, :].astype(F32)[8:16] for k in range(2)], axis=0
            ).astype(BF)
        return halos[0].start(pk.at[pl.ds(first, count)], hw.at[pl.ds(first + 2, count)], 0, 1)

    north = [halos[0].start(text.at[pl.ds(24, 3)], text.at[pl.ds(0, 3)], 1, 0)]
    west = [pack_tokens(1, 4), pack_tokens(5, 7)]
    north.append(pack_tokens(0, 1))
    north.append(halos[0].start(pk.at[pl.ds(10, 2)], hw.at[pl.ds(0, 2)], 1, 1))
    band_bias(band_ref, bias)
    loads[1].wait()

    def forward_row(w, carry):
        load_frame(fr, w, text, hw)
        xhat, _ = moments(fr[...])
        fr[...] = xhat * ga_ref[...].reshape(1, 1, C)
        to_windows(fr, s2)
        normed = s2[...].reshape(NWT, C).astype(BF)
        nrm[pl.ds(pl.multiple_of(w * NWT, NWT), NWT), :] = normed
        for t in range(3):
            part = dot(normed, wq[:, C * t : C * (t + 1)], 1, 0).reshape(NW, WIN, C)
            if t == 0:
                qf[...] = part
            qkv[pl.ds(NW * w, NW), :, C * t : C * (t + 1)] = part.astype(BF)
        mask = bias[w]

        def window(v, carry):
            masks = head_masks(0.125)
            n = NW * w + v
            scores = []
            for p in range(PAIRS):
                qs = stacked(qf[v, :, 128 * p : 128 * (p + 1)].astype(BF).astype(F32), masks)
                qst[n, p] = qs
                scores.append(dot(qkv[n, :, C + 128 * p : C + 128 * (p + 1)], qs, 1, 1))
            probs = []
            for p in range(PAIRS):
                s = scores[p] + mask
                e = jnp.exp(s - jnp.max(s, axis=0, keepdims=True))
                pr = (e * (1.0 / jnp.sum(e, axis=0, keepdims=True))).astype(BF)
                prob[n, p] = pr
                probs.append(pr)
            for p in range(PAIRS):
                val = qkv[n, :, 2 * C + 128 * p : 2 * C + 128 * (p + 1)]
                s2[v, :, 128 * p : 128 * (p + 1)] = merged_heads(dot(probs[p], val, 0, 0))
            return carry

        lax.fori_loop(0, NW, window, 0)
        to_frame(s2, fr)
        pack_rows(fr, bw, w)
        for r in range(WLAT):
            attx[WLAT * w + r] = fr[r, 8:FR, :].astype(BF)
        return carry

    def send_back(w):
        return halos[1].start(bw.at[pl.ds(3 * w, 3)], he.at[pl.ds(3 * w, 3)], 0, -1)

    west[0].wait_recv()
    lax.fori_loop(1, 2, forward_row, 0)
    east = [send_back(1)]
    for copy in north + west[1:]:
        copy.wait_recv()
    lax.fori_loop(0, 1, forward_row, 0)
    south = [
        halos[1].start(attx.at[pl.ds(0, 3)], attx.at[pl.ds(24, 3)], -1, 0),
        halos[1].start(bw.at[pl.ds(0, 2)], he.at[pl.ds(12, 2)], -1, -1),
    ]
    east.append(send_back(0))
    lax.fori_loop(2, 3, forward_row, 0)
    east.append(send_back(2))
    lax.fori_loop(3, 4, forward_row, 0)
    south.append(send_back(3))
    for load in loads[2:]:
        load.wait()
    for copy in east:
        copy.wait_recv()
    gain = gmg_ref[...]
    lower = lax.broadcasted_iota(jnp.int32, (8, C), 0) < 2

    def merge_forward(c, carry):
        pieces = []
        for i in range(CH):
            row = attx[CH * c + 3 + i].astype(F32)
            edge = pair_half(he, 2 * c + (3 + i) // 2, (3 + i) % 2)
            pieces.append(jnp.concatenate([row[:40], jnp.where(lower, row[40:], edge)], axis=0))
        att = jnp.concatenate(pieces, axis=0).astype(BF)
        attx[pl.ds(CH * c + 3, CH)] = att.reshape(CH, COLS, C)
        proj = dot(att, wo[...], 1, 0).reshape(CH, COLS, C)
        mixed = (text[pl.ds(CH * c + 3, CH)].astype(F32) + proj).astype(BF).astype(F32)
        for q in range(4):
            s1[q] = mixed[:, :, 128 * q : 128 * (q + 1)]
        parts = []
        for b in range(2):
            for a in range(2):
                for q in range(4):
                    piece = [s1[q, 2 * i + a, pl.ds(b, COLS // 2, stride=2), :] for i in range(CH // 2)]
                    parts.append(jnp.concatenate(piece, axis=0))
        xhat, rstd = moments(jnp.concatenate(parts, axis=1))
        here = pl.ds(pl.multiple_of(c * MT, MT), MT)
        xh[here, :] = xhat
        rs[here, :] = rstd
        mi[here, :] = (xhat * gain).astype(BF)
        return carry

    lax.fori_loop(0, 3, merge_forward, 0)
    for copy in south:
        copy.wait_recv()
    lax.fori_loop(3, NCH, merge_forward, 0)
    gm = gmb[...].astype(F32).reshape(MALL, C2).astype(BF)

    def merged_tile(n, carry):
        cols = pl.ds(pl.multiple_of(n * 256, 256), 256)
        tile = dot(mi[...], wm[:, cols], 1, 0).reshape(ROWS // 2, COLS // 2, 256)
        merged_ref[:, :, cols] = tile.astype(BF)
        return carry


    def weight_tile(n, carry):
        cols = pl.ds(pl.multiple_of(n * 256, 256), 256)
        gwm[cols, :] = dot(mi[:, cols], gm, 0, 0).astype(BF)
        return carry

    lax.fori_loop(0, C4 // 256, weight_tile, 0)

    def summed(src, out, turn, n):
        order = AXES[turn:] + AXES[:turn]
        return Sum(at, src, out, order, sums[4 * n : 4 * n + 4], send.at[n], recv.at[n])

    wide = [
        summed(gwm.at[:, 0:384], outm_ref.at[:, 0:384], 0, 0),
        summed(gwm.at[:, 384:768], outm_ref.at[:, 384:768], 1, 1),
        summed(gwm.at[:, 768:1024], outm_ref.at[:, 768:1024], 2, 2),
    ]
    early = wide + [summed(qo.at[:, 0:128], outq_ref.at[:, 0:128], 2, 3)]
    late = [
        summed(qo.at[:, 128 * (t + 1) : 128 * (t + 2)], outq_ref.at[:, 128 * (t + 1) : 128 * (t + 2)], t, 4 + t)
        for t in range(3)
    ]

    def advance(group, n):
        for part in group:
            part.step(n)

    advance(wide, 0)

    def cotangent_tile(n, carry):
        cols = pl.ds(pl.multiple_of(n * 256, 256), 256)
        gi[:, cols] = dot(gm, wm[cols, :], 1, 1).astype(BF)
        return carry

    lax.fori_loop(0, C4 // 256, cotangent_tile, 0)
    ggm[...] = jnp.zeros_like(ggm)

    def merge_backward(c, carry):
        here = pl.ds(pl.multiple_of(c * MT, MT), MT)
        xhat = xh[here, :]
        g = gi[here, :].astype(F32)
        ggm[...] += jnp.sum(g * xhat, axis=0, keepdims=True)
        dx = g * gain
        m1 = jnp.mean(dx, axis=-1, keepdims=True)
        m2 = jnp.mean(dx * xhat, axis=-1, keepdims=True)
        dx = rs[here, :] * (dx - m1 - xhat * m2)
        for b in range(2):
            for a in range(2):
                for q in range(4):
                    start = C * (2 * b + a) + 128 * q
                    for i in range(CH // 2):
                        s1[q, 2 * i + a, pl.ds(b, COLS // 2, stride=2), :] = dx[
                            (COLS // 2) * i : (COLS // 2) * (i + 1), start : start + 128
                        ]
        mixed = jnp.concatenate([s1[q] for q in range(4)], axis=-1).astype(BF)
        gmix[pl.ds(c * CH, CH)] = mixed
        gatt = dot(mixed.reshape(CH * COLS, C), wo[...], 1, 1).reshape(CH, COLS, C)
        gext[pl.ds(CH * c + 3, CH)] = gatt.astype(BF)
        for m in range(CH // 2):
            pkg[(CH // 2) * c + m] = jnp.concatenate(
                [gatt[2 * m, 40:48], gatt[2 * m + 1, 40:48]], axis=0
            ).astype(BF)
        return carry

    def send_cotangents(first, count):
        return halos[2].start(pkg.at[pl.ds(first, count)], gw.at[pl.ds(first + 2, count)], 0, 1)

    lax.fori_loop(5, 6, merge_backward, 0)
    halos[2].start(gext.at[pl.ds(24, 3)], gext.at[pl.ds(0, 3)], 1, 0)
    halos[2].start(pkg.at[pl.ds(10, 2)], gw.at[pl.ds(0, 2)], 1, 1)
    send_cotangents(10, 2)
    lax.fori_loop(0, 3, merge_backward, 0)
    send_cotangents(0, 6)
    lax.fori_loop(3, 5, merge_backward, 0)
    send_cotangents(6, 4)
    flat = gmix[...].reshape(ROWS * COLS, C)
    att = attx[pl.ds(3, ROWS)].reshape(ROWS * COLS, C)
    gwo = dot(att, flat, 0, 0).astype(BF)
    for n in range(4):
        qo[C * n : C * (n + 1), 0:128] = gwo[:, 128 * n : 128 * (n + 1)]
    early[3].step(0)
    advance(early, 1)
    for copy in halos[2].copies:
        copy.wait_recv()

    def backward_row(w, carry):
        load_frame(fr, w, gext, gw)
        to_windows(fr, s2)

        def window(v, carry):
            masks = head_masks(1.0)
            n = NW * w + v
            cots, dps = [], []
            for p in range(PAIRS):
                gs = stacked(s2[v, :, 128 * p : 128 * (p + 1)], masks)
                cots.append(gs)
                dps.append(dot(qkv[n, :, 2 * C + 128 * p : 2 * C + 128 * (p + 1)], gs, 1, 1))
            for p in range(PAIRS):
                dq[v, :, 2 * C + 128 * p : 2 * C + 128 * (p + 1)] = dot(prob[n, p], cots[p], 1, 0)
            dss = []
            for p in range(PAIRS):
                pf = prob[n, p].astype(F32)
                delta = jnp.sum(pf * dps[p], axis=0, keepdims=True)
                dss.append((pf * (dps[p] - delta)).astype(BF))
            for p in range(PAIRS):
                dq[v, :, C + 128 * p : C + 128 * (p + 1)] = dot(dss[p], qst[n, p], 1, 0)
            for p in range(PAIRS):
                k = qkv[n, :, C + 128 * p : C + 128 * (p + 1)]
                dq[v, :, 128 * p : 128 * (p + 1)] = merged_heads(dot(dss[p], k, 0, 0)) * 0.125
            return carry

        lax.fori_loop(0, NW, window, 0)
        dall[pl.ds(pl.multiple_of(w * NWT, NWT), NWT), :] = dq[...].reshape(NWT, 3 * C).astype(BF)
        return carry

    lax.fori_loop(0, 3, backward_row, 0)
    advance(early, 2)
    lax.fori_loop(3, 4, backward_row, 0)
    advance(early, 3)
    for n in range(6):
        tile = dot(nrm[...], dall[:, 256 * n : 256 * (n + 1)], 0, 0).astype(BF)
        for k in range(2):
            g = 2 * n + k
            qo[C * (g // 3) : C * (g // 3 + 1), 128 * (1 + g % 3) : 128 * (2 + g % 3)] = tile[:, 128 * k : 128 * (k + 1)]
    advance(late, 0)
    advance(early, 4)
    gga[...] = jnp.zeros_like(gga)

    def dgrad_row(w, carry):
        rows = pl.ds(pl.multiple_of(w * NWT, NWT), NWT)
        s2[...] = dot(dall[rows, :], wq[...], 1, 1).astype(BF).astype(F32).reshape(NW, WIN, C)
        load_frame(fr, w, text, hw)
        xhat, rstd = moments(fr[...])
        fr[:, 0:8, :] = jnp.zeros((WLAT, 8, C), F32)
        fr[:, FR - 8 : FR, :] = jnp.zeros((WLAT, 8, C), F32)
        to_frame(s2, fr)
        g = fr[...]
        gga[...] += jnp.sum(g * xhat, axis=(0, 1)).reshape(1, C)
        dx = g * ga_ref[...].reshape(1, 1, C)
        m1 = jnp.mean(dx, axis=-1, keepdims=True)
        m2 = jnp.mean(dx * xhat, axis=-1, keepdims=True)
        fr[...] = rstd * (dx - m1 - xhat * m2)
        pack_rows(fr, bw2, w)
        for r in range(3):
            bn2[WLAT * w + r] = fr[r, 8:FR, :].astype(BF)
        for r in range(3):
            gtok_ref[WLAT * w + r] = fr[3 + r, 8:FR, :] + gmix[WLAT * w + r].astype(F32)

        @pl.when(w > 0)
        def _():
            for r in range(3):
                gtok_ref[WLAT * w - 3 + r] = fr[r, 8:FR, :] + gmix[WLAT * w - 3 + r].astype(F32)

        return carry

    lax.fori_loop(0, 1, dgrad_row, 0)
    halos[3].start(bn2.at[pl.ds(0, 3)], hs2, -1, 0)
    halos[3].start(bw2.at[pl.ds(0, 2)], he2.at[pl.ds(12, 2)], -1, -1)
    advance(late, 1)
    lax.fori_loop(1, 2, dgrad_row, 0)
    halos[3].start(bw2.at[pl.ds(0, 6)], he2.at[pl.ds(0, 6)], 0, -1)
    advance(early, 5)
    lax.fori_loop(2, 4, dgrad_row, 0)
    halos[3].start(bw2.at[pl.ds(6, 6)], he2.at[pl.ds(6, 6)], 0, -1)
    advance(late, 2)
    advance(early, 6)
    lax.fori_loop(0, C2 // 256, merged_tile, 0)
    stores = [
        pltpu.make_async_copy(src, dst, lsem.at[5 + n])
        for n, (src, dst) in enumerate(
            [(merged_ref, merged_out), (gtok_ref, gtok_out), (outm_ref, outm_out), (outq_ref, outq_out)]
        )
    ]
    stores[0].start()
    small[0] = jnp.zeros_like(small[0])
    small[0, 0:1, :] = gga[...]
    for n in range(4):
        small[0, 1 + n : 2 + n, :] = ggm[:, C * n : C * (n + 1)]
    gains = SmallSum(at, small, slots, ssend, srecv)
    gains.begin(0)
    advance(late, 3)
    gains.end(0)
    gains.begin(1)
    advance(late, 4)
    for copy in halos[3].copies:
        copy.wait_recv()
    for r in range(3):
        gtok_ref[21 + r] = hs2[r].astype(F32) + gmix[21 + r].astype(F32)
    for r in range(ROWS):
        edge = pair_half(he2, (r + 3) // 2, (r + 3) % 2) + gmix[r, 32:48, :].astype(F32)[8:16]
        gtok_ref[r, 40:48, :] = jnp.where(lower, gtok_ref[r, 40:48, :], edge)
    stores[1].start()
    gains.end(1)
    gains.begin(2)
    advance(late, 5)
    gains.end(2)
    gains.begin(3)
    advance(early, 7)
    advance(late, 6)
    gains.end(3)
    outs_ref[...] = small[4]
    advance(early, 8)
    stores[2].start()
    advance(late, 7)
    advance(late, 8)
    stores[3].start()
    gains.finish()
    for halo in halos:
        halo.left()
    for store in stores:
        store.wait()


def step_kernel(tokens, band, gain_a, w_qkv, w_out, grad_merged, w_merge, gain_m):
    vmem = pl.BlockSpec(memory_space=pltpu.VMEM)
    hbm = pl.BlockSpec(memory_space=pl.ANY)
    lanes = (384, 384, 256, 128, 128, 128, 128)
    sums = []
    for n in lanes:
        sums += sum_scratch(TALL, n)
    return pl.pallas_call(
        step_body,
        in_specs=[hbm, vmem, vmem, hbm, hbm, hbm, hbm, vmem],
        out_specs=[hbm] * 4 + [vmem],
        out_shape=[
            jax.ShapeDtypeStruct((ROWS // 2, COLS // 2, C2), BF),
            jax.ShapeDtypeStruct((ROWS, COLS, C), F32),
            jax.ShapeDtypeStruct((C4, C2), BF),
            jax.ShapeDtypeStruct((TALL, C), BF),
            jax.ShapeDtypeStruct((8, C), F32),
        ],
        scratch_shapes=[
            pltpu.VMEM((ROWS // 2, COLS // 2, C2), BF),
            pltpu.VMEM((ROWS, COLS, C), F32),
            pltpu.VMEM((C4, C2), BF),
            pltpu.VMEM((TALL, C), BF),
            pltpu.VMEM((27, COLS, C), BF),
            pltpu.VMEM((14, 16, C), BF),
            pltpu.VMEM((12, 16, C), BF),
            pltpu.VMEM((C, 3 * C), BF),
            pltpu.VMEM((C, C), BF),
            pltpu.VMEM((ROWS // 2, COLS // 2, C2), BF),
            pltpu.VMEM((C4, C2), BF),
            pltpu.VMEM((WROWS * NW, WIN, 3 * C), BF),
            pltpu.VMEM((WROWS * NW, PAIRS, WIN, 2 * WIN), BF),
            pltpu.VMEM((WROWS * NW, PAIRS, 2 * WIN, 128), BF),
            pltpu.VMEM((ROWS * COLS, C), BF),
            pltpu.VMEM((NW, WIN, C), F32),
            pltpu.VMEM((NW, WIN, C), F32),
            pltpu.VMEM((WLAT, FR, C), F32),
            pltpu.VMEM((27, COLS, C), BF),
            pltpu.VMEM((14, 16, C), BF),
            pltpu.VMEM((12, 16, C), BF),
            pltpu.VMEM((4, CH, COLS, 128), F32),
            pltpu.VMEM((MALL, C4), F32),
            pltpu.VMEM((MALL, 1), F32),
            pltpu.VMEM((MALL, C4), BF),
            pltpu.VMEM((MALL, C4), BF),
            pltpu.VMEM((C4, C2), BF),
            pltpu.VMEM((TALL, C), BF),
            pltpu.VMEM((ROWS, COLS, C), BF),
            pltpu.VMEM((27, COLS, C), BF),
            pltpu.VMEM((14, 16, C), BF),
            pltpu.VMEM((12, 16, C), BF),
            pltpu.VMEM((NW, WIN, 3 * C), F32),
            pltpu.VMEM((ROWS * COLS, 3 * C), BF),
            pltpu.VMEM((21, COLS, C), BF),
            pltpu.VMEM((12, 16, C), BF),
            pltpu.VMEM((3, COLS, C), BF),
            pltpu.VMEM((14, 16, C), BF),
            pltpu.VMEM((5, 8, C), F32),
            pltpu.VMEM((10, 8, C), F32),
            pltpu.VMEM((1, C4), F32),
            pltpu.VMEM((1, C), F32),
            pltpu.VMEM((WROWS, WIN, 2 * WIN), F32),
            pltpu.SemaphoreType.DMA((9,)),
            pltpu.SemaphoreType.DMA((4, 6)),
            pltpu.SemaphoreType.DMA((4, 6)),
            pltpu.SemaphoreType.DMA((7, SUM_COPIES)),
            pltpu.SemaphoreType.DMA((7, SUM_COPIES)),
            pltpu.SemaphoreType.DMA((10,)),
            pltpu.SemaphoreType.DMA((10,)),
        ]
        + sums,
        compiler_params=pltpu.CompilerParams(
            vmem_limit_bytes=62 * MIB, collective_id=0, has_side_effects=True
        ),
        name="step",
    )(tokens, band, gain_a, w_qkv, w_out, grad_merged, w_merge, gain_m)


def widen_body(m_ref, q_ref, s_ref, gm_ref, gq_ref, go_ref, ga_ref, gg_ref):
    gm_ref[...] = m_ref[...].astype(F32)
    go_ref[...] = q_ref[:, 0:128].astype(F32)
    gq_ref[...] = q_ref[:, 128:].astype(F32)
    ga_ref[...] = s_ref[0:1, :]
    for n in range(4):
        gg_ref[:, C * n : C * (n + 1)] = s_ref[1 + n : 2 + n, :]


def widen(sum_merge, sum_qo, sum_gain):
    return pl.pallas_call(
        widen_body,
        grid=(4,),
        in_specs=[
            pl.BlockSpec((C, C2), lambda i: (i, 0)),
            pl.BlockSpec((C, C), lambda i: (i, 0)),
            pl.BlockSpec((8, C), lambda i: (0, 0)),
        ],
        out_specs=[
            pl.BlockSpec((C, C2), lambda i: (i, 0)),
            pl.BlockSpec((C, 384), lambda i: (0, i)),
            pl.BlockSpec((C, 128), lambda i: (0, i)),
            pl.BlockSpec((1, C), lambda i: (0, 0)),
            pl.BlockSpec((1, C4), lambda i: (0, 0)),
        ],
        out_shape=[
            jax.ShapeDtypeStruct((C4, C2), F32),
            jax.ShapeDtypeStruct((C, 3 * C), F32),
            jax.ShapeDtypeStruct((C, C), F32),
            jax.ShapeDtypeStruct((1, C), F32),
            jax.ShapeDtypeStruct((1, C4), F32),
        ],
        compiler_params=pltpu.CompilerParams(vmem_limit_bytes=60 * MIB),
        name="widen",
    )(sum_merge, sum_qo, sum_gain)


def on_device(tokens, lat_band, gain_attn, w_qkv, w_out, gain_merge, w_merge, grad_merged):
    merged, grad_tokens, sum_merge, sum_qo, sum_gain = step_kernel(
        tokens, lat_band.reshape(1, -1), gain_attn.reshape(1, C), w_qkv, w_out, grad_merged, w_merge,
        gain_merge.reshape(1, C4)
    )
    gw_merge, gw_qkv, gw_out, gg_attn, gg_merge = widen(sum_merge, sum_qo, sum_gain)
    return merged, grad_tokens, gg_attn.reshape(C), gw_qkv, gw_out, gg_merge.reshape(C4), gw_merge


def solution(mesh):
    return jax.shard_map(
        on_device,
        mesh=mesh,
        in_specs=(P("lat", "lon", None), P(), P(), P(), P(), P(), P(), P("lat", "lon", None)),
        out_specs=(P("lat", "lon", None), P("lat", "lon", None), P(), P(), P(), P(), P()),
        check_vma=False,
    )
```

```python
import functools
import jax
import jax.numpy as jnp
from jax import lax
from jax.experimental import pallas as pl
from jax.experimental.pallas import tpu as pltpu
from jax.sharding import PartitionSpec as P

HEADS = 8
WLAT = 6
WLON = 12
EPSILON = 1e-05
F32 = jnp.float32
BF = jnp.bfloat16
ROWS = 24
COLS = 48
C = 512
WIN = 72
NW = COLS // WLON
PAIRS = HEADS // 2
MIB = 1 << 20


def dot(a, b, ca, cb):
    return lax.dot_general(a, b, (((ca,), (cb,)), ((), ())), preferred_element_type=F32)


def head_masks(scale):
    lane = lax.broadcasted_iota(jnp.int32, (1, 128), 1)
    low = jnp.where(lane < 64, scale, 0.0).astype(F32)
    high = jnp.where(lane < 64, 0.0, scale).astype(F32)
    return low, high


def stacked(value, masks):
    return jnp.concatenate([value * masks[0], value * masks[1]], axis=0).astype(BF)


def merged_heads(value):
    lane = lax.broadcasted_iota(jnp.int32, (WIN, 128), 1)
    return jnp.where(lane < 64, value[:WIN], value[WIN:])


def moments(x):
    mean = jnp.mean(x, axis=-1, keepdims=True)
    centered = x - mean
    var = jnp.mean(centered * centered, axis=-1, keepdims=True)
    rstd = lax.rsqrt(var + EPSILON)
    return centered * rstd, rstd


AXES = ("x", "y", "z")


def coordinates():
    lat = lax.axis_index("lat")
    lon = lax.axis_index("lon")
    return {"x": lon // 4, "y": (lat // 4) * 2 + (lon // 2) % 2, "z": lat % 4, "core": lon % 2}


def device(at):
    return ((at["y"] // 2) * 4 + at["z"], at["x"] * 4 + (at["y"] % 2) * 2 + at["core"])


def peer(at, axis, step):
    size = 2 if axis == "core" else 4
    return device({**at, axis: (at[axis] + step) % size})


def remote(src, dst, send, recv, target):
    return pltpu.make_async_remote_copy(
        src_ref=src, dst_ref=dst, send_sem=send, recv_sem=recv,
        device_id=target, device_id_type=pl.DeviceIdType.MESH,
    )


def neighbour(rows, cols):
    lat = lax.axis_index("lat")
    lon = lax.axis_index("lon")
    return ((lat + rows) % 8, (lon + cols) % 16)


EDGES = ((0, 1), (1, 0), (1, 1))


def greet(at):
    barrier = pltpu.get_barrier_semaphore()
    targets = [
        peer(at, axis, step)
        for axis, count in (("core", 2), ("x", 4), ("y", 4), ("z", 4))
        for step in range(1, count)
    ]
    targets += [neighbour(sign * r, sign * c) for sign in (1, -1) for r, c in EDGES]
    for target in targets:
        pl.semaphore_signal(barrier, inc=1, device_id=target, device_id_type=pl.DeviceIdType.MESH)
    pl.semaphore_wait(barrier, len(targets))


def add_rows(dst, start, terms, rows):
    chunk = min(rows, 64)

    def body(i, carry):
        total = None
        for ref, first in terms:
            piece = ref[pl.ds(pl.multiple_of(first + i * chunk, 16), chunk), :].astype(F32)
            total = piece if total is None else total + piece
        dst[pl.ds(pl.multiple_of(start + i * chunk, 16), chunk), :] = total.astype(dst.dtype)
        return carry

    lax.fori_loop(0, rows // chunk, body, 0)


class Sum:
    def __init__(self, at, src, out, order, recvs, send, recv, ring):
        self.at, self.src, self.out, self.order = at, src, out, order
        self.recvs, self.send, self.recv = recvs, send, recv
        self.rows, self.ring = src.shape[0], ring
        self.sent = []

    def start(self, src, dst, index, target):
        copy = remote(src, dst, self.send.at[index], self.recv.at[index], target)
        copy.start()
        self.sent.append(copy)
        return copy

    def block(self, level):
        return self.rows // 2 // 4**level

    def first(self, levels):
        first = self.at["core"] * (self.rows // 2)
        for level in range(levels):
            first = first + self.at[self.order[level]] * self.block(level + 1)
        return pl.multiple_of(first, 16)

    def begin(self):
        half = self.rows // 2
        theirs = pl.ds(pl.multiple_of((1 - self.at["core"]) * half, 16), half)
        self.last = [self.start(self.src.at[theirs, :], self.recvs[0].at[0], 0, peer(self.at, "core", 1))]

    def combine(self, level):
        for copy in self.last:
            copy.wait_recv()
        count = self.block(level)
        first = self.first(level)
        terms = [(self.src, first)] + [(self.recvs[level].at[s], 0) for s in range(1 if level == 0 else 3)]
        if level == 3:
            add_rows(self.out, first, terms, count)
            self.gather(3)
            return
        if level == 1 and self.ring:
            terms = [(self.src, first), (self.recvs[1].at[1], 0), (self.recvs[1].at[2], 0)]
        add_rows(self.src, first, terms, count)
        if level == 0 and self.ring:
            self.ring_start()
            return
        axis = self.order[level]
        block = self.block(level + 1)
        self.last = []
        for step in range(1, 4):
            there = pl.multiple_of(first + (self.at[axis] + step) % 4 * block, 16)
            self.last.append(
                self.start(
                    self.src.at[pl.ds(there, block), :], self.recvs[level + 1].at[step - 1],
                    3 * level + step, peer(self.at, axis, step),
                )
            )

    def part(self, step, half):
        block = self.block(1)
        return pl.multiple_of(self.first(0) + (self.at[self.order[0]] + step) % 4 * block + half * (block // 2), 16)

    def ring_send(self, step, half, slot, index, towards):
        size = self.block(1) // 2
        return self.start(
            self.src.at[pl.ds(self.part(step, half), size), :],
            self.recvs[1].at[slot, pl.ds(half * size, size), :],
            index, peer(self.at, self.order[0], towards),
        )

    def ring_start(self):
        self.relayed = [self.ring_send(2, 0, 0, 20, 1), self.ring_send(2, 1, 0, 21, 3)]
        self.last = [self.ring_send(1, 1, 1, 22, 1), self.ring_send(3, 0, 1, 23, 3)]

    def ring_relay(self):
        for copy in self.relayed:
            copy.wait_recv()
        size = self.block(1) // 2
        for step, half, index in ((1, 0, 24), (3, 1, 25)):
            first = self.part(step, half)
            add_rows(self.src, first, [(self.src, first), (self.recvs[1].at[0], half * size)], size)
            self.last.append(self.ring_send(step, half, 2, index, step))

    def ring_forward(self):
        for copy in self.last:
            copy.wait_recv()
        size = self.block(1) // 2
        self.last = []
        for step, half, index in ((3, 0, 28), (1, 1, 29)):
            rows = self.out.at[pl.ds(self.part(step, half), size), :]
            self.last.append(self.start(rows, rows, index, peer(self.at, self.order[0], 4 - step)))

    def gather(self, level):
        mine = self.out.at[pl.ds(self.first(level), self.block(level)), :]
        if level == 0:
            self.last = [self.start(mine, mine, 19, peer(self.at, "core", 1))]
            return
        axis = self.order[level - 1]
        if level == 1 and self.ring:
            self.last = [self.start(mine, mine, 26 + n, peer(self.at, axis, step)) for n, step in enumerate((1, 3))]
            return
        self.last = [
            self.start(mine, mine, 10 + 3 * (level - 1) + step - 1, peer(self.at, axis, step)) for step in range(1, 4)
        ]

    def gathered(self, level):
        for copy in self.last:
            copy.wait_recv()
        self.gather(level - 1)

    def finish(self):
        self.last[0].wait_recv()
        for copy in self.sent:
            copy.wait_send()

    def step(self, n):
        if self.ring:
            if n == 2:
                self.ring_relay()
                return
            if n == 8:
                self.ring_forward()
                return
            n = n - (n > 2) - (n > 8)
        if n == 0:
            self.begin()
        elif n < 5:
            self.combine(n - 1)
        elif n < 8:
            self.gathered(8 - n)
        else:
            self.finish()


SUM_COPIES = 30


def sum_scratch(rows, lanes):
    half = rows // 2
    return [pltpu.VMEM((1, half, lanes), BF)] + [pltpu.VMEM((3, half // 4**n, lanes), BF) for n in (1, 2, 3)]


class SmallSum:
    def __init__(self, at, block, slots, send, recv):
        self.at, self.block, self.slots, self.send, self.recv = at, block, slots, send, recv
        self.sent = []

    def begin(self, level):
        axis, count = (("core", 2), ("x", 4), ("y", 4), ("z", 4))[level]
        base = 0 if level == 0 else 3 * level - 2
        self.last = []
        for step in range(1, count):
            i = base + step - 1
            copy = remote(self.block.at[level], self.slots.at[i], self.send.at[i], self.recv.at[i],
                          peer(self.at, axis, step))
            copy.start()
            self.last.append((copy, i))
            self.sent.append(copy)

    def end(self, level):
        total = self.block[level]
        for copy, i in self.last:
            copy.wait_recv()
            total = total + self.slots[i]
        self.block[level + 1] = total

    def finish(self):
        for copy in self.sent:
            copy.wait_send()

CH = 4
NCH = ROWS // CH
MT = (CH // 2) * (COLS // 2)
MALL = NCH * MT
C4 = 4 * C
C2 = 1024
WROWS = ROWS // WLAT
NWT = NW * WIN
FR = COLS + 8
TALL = 4 * C


class Halo:
    def __init__(self, send, recv):
        self.send, self.recv, self.copies = send, recv, []

    def start(self, src, dst, rows, cols):
        n = len(self.copies)
        copy = remote(src, dst, self.send.at[n], self.recv.at[n], neighbour(rows, cols))
        copy.start()
        self.copies.append(copy)
        return copy

    def left(self):
        for copy in self.copies:
            copy.wait_send()


def band_bias(band_ref, bias):
    band = band_ref[...].astype(F32)
    total = band.shape[1]

    def grid_row(place, first):
        row = first + jnp.floor((place.astype(F32) + 0.5) * (1.0 / WLON)).astype(jnp.int32)
        return jnp.where(row >= total, row - total, row)

    for w in range(WROWS):
        first = (lax.axis_index("lat") * ROWS + WLAT * w - 3 + total) % total
        key = lax.broadcasted_iota(jnp.int32, (WIN, total), 0)
        hit = grid_row(key, first) == lax.broadcasted_iota(jnp.int32, (WIN, total), 1)
        keys = jnp.sum(jnp.where(hit, band, 0.0), axis=1, keepdims=True)
        query = lax.broadcasted_iota(jnp.int32, (total, 2 * WIN), 1)
        query = jnp.where(query >= WIN, query - WIN, query)
        hit = grid_row(query, first) == lax.broadcasted_iota(jnp.int32, (total, 2 * WIN), 0)
        queries = dot(jnp.broadcast_to(band, (8, total)).astype(BF), jnp.where(hit, 1.0, 0.0).astype(BF), 1, 0)
        bias[w] = jnp.where(keys == queries[0:1], 0.0, -1e30)


def pair_half(ref, pair, half):
    return ref[pair].astype(F32)[8 * half : 8 * half + 8]


def load_frame(fr, w, rows_ref, edge_ref):
    for r in range(WLAT):
        fr[r, 8:FR, :] = rows_ref[WLAT * w + r].astype(F32)
        fr[r, 0:8, :] = pair_half(edge_ref, 3 * w + (r + 1) // 2, (r + 1) % 2)


def to_windows(fr, dst):
    for v in range(NW):
        for r in range(WLAT):
            dst[v, WLON * r : WLON * (r + 1), :] = fr[r, WLON * v + 2 : WLON * v + 14, :]


def to_frame(src, fr):
    for v in range(NW):
        for r in range(WLAT):
            fr[r, WLON * v + 2 : WLON * v + 14, :] = src[v, WLON * r : WLON * (r + 1), :]


def pack_rows(fr, edge_ref, w):
    for r in range(0, WLAT, 2):
        edge_ref[3 * w + r // 2] = jnp.concatenate([fr[r, 0:8, :], fr[r + 1, 0:8, :]], axis=0).astype(BF)


def step_body(tok_hbm, band_ref, ga_ref, wq_hbm, wo_hbm, gm_hbm, wm_hbm, gmg_ref,
              merged_out, gtok_out, outm_out, outq_out, outs_ref,
              merged_ref, gtok_ref, outm_ref, outq_ref,
              text, hw, pk, wq, wo, gmb, wm, qkv, prob, qst, nrm, qf, s2, fr, attx, he, bw,
              s1, xh, rs, mi, gi, gwm, qo, gmix, gext, gw, pkg, dq, dall, bn2, bw2, hs2, he2,
              small, slots, ggm, gga, bias, lsem, hsend, hrecv, send, recv, ssend, srecv, *sums):
    loads = [
        pltpu.make_async_copy(src, dst, lsem.at[n])
        for n, (src, dst) in enumerate(
            [(tok_hbm, text.at[pl.ds(3, ROWS)]), (wq_hbm, wq), (wo_hbm, wo), (gm_hbm, gmb), (wm_hbm, wm)]
        )
    ]
    for load in loads:
        load.start()
    at = coordinates()
    greet(at)
    halos = [Halo(hsend.at[n], hrecv.at[n]) for n in range(4)]

    loads[0].wait()

    def pack_tokens(first, count):
        for m in range(first, first + count):
            pk[m] = jnp.concatenate(
                [text[3 + 2 * m + k, 32:48, :].astype(F32)[8:16] for k in range(2)], axis=0
            ).astype(BF)
        return halos[0].start(pk.at[pl.ds(first, count)], hw.at[pl.ds(first + 2, count)], 0, 1)

    north = [halos[0].start(text.at[pl.ds(24, 3)], text.at[pl.ds(0, 3)], 1, 0)]
    west = [pack_tokens(1, 4), pack_tokens(5, 7)]
    north.append(pack_tokens(0, 1))
    north.append(halos[0].start(pk.at[pl.ds(10, 2)], hw.at[pl.ds(0, 2)], 1, 1))
    band_bias(band_ref, bias)
    loads[1].wait()

    def forward_row(w, carry):
        load_frame(fr, w, text, hw)
        xhat, _ = moments(fr[...])
        fr[...] = xhat * ga_ref[...].reshape(1, 1, C)
        to_windows(fr, s2)
        normed = s2[...].reshape(NWT, C).astype(BF)
        nrm[pl.ds(pl.multiple_of(w * NWT, NWT), NWT), :] = normed
        for t in range(3):
            part = dot(normed, wq[:, C * t : C * (t + 1)], 1, 0).reshape(NW, WIN, C)
            if t == 0:
                qf[...] = part
            qkv[pl.ds(NW * w, NW), :, C * t : C * (t + 1)] = part.astype(BF)
        mask = bias[w]

        def window(v, carry):
            masks = head_masks(0.125)
            n = NW * w + v
            scores = []
            for p in range(PAIRS):
                qs = stacked(qf[v, :, 128 * p : 128 * (p + 1)].astype(BF).astype(F32), masks)
                qst[n, p] = qs
                scores.append(dot(qkv[n, :, C + 128 * p : C + 128 * (p + 1)], qs, 1, 1))
            probs = []
            for p in range(PAIRS):
                s = scores[p] + mask
                e = jnp.exp(s - jnp.max(s, axis=0, keepdims=True))
                pr = (e * (1.0 / jnp.sum(e, axis=0, keepdims=True))).astype(BF)
                prob[n, p] = pr
                probs.append(pr)
            for p in range(PAIRS):
                val = qkv[n, :, 2 * C + 128 * p : 2 * C + 128 * (p + 1)]
                s2[v, :, 128 * p : 128 * (p + 1)] = merged_heads(dot(probs[p], val, 0, 0))
            return carry

        lax.fori_loop(0, NW, window, 0)
        to_frame(s2, fr)
        pack_rows(fr, bw, w)
        for r in range(WLAT):
            attx[WLAT * w + r] = fr[r, 8:FR, :].astype(BF)
        return carry

    def send_back(w):
        return halos[1].start(bw.at[pl.ds(3 * w, 3)], he.at[pl.ds(3 * w, 3)], 0, -1)

    west[0].wait_recv()
    lax.fori_loop(1, 2, forward_row, 0)
    east = [send_back(1)]
    for copy in north + west[1:]:
        copy.wait_recv()
    lax.fori_loop(0, 1, forward_row, 0)
    south = [
        halos[1].start(attx.at[pl.ds(0, 3)], attx.at[pl.ds(24, 3)], -1, 0),
        halos[1].start(bw.at[pl.ds(0, 2)], he.at[pl.ds(12, 2)], -1, -1),
    ]
    east.append(send_back(0))
    lax.fori_loop(2, 3, forward_row, 0)
    east.append(send_back(2))
    lax.fori_loop(3, 4, forward_row, 0)
    south.append(send_back(3))
    for load in loads[2:]:
        load.wait()
    for copy in east:
        copy.wait_recv()
    gain = gmg_ref[...]
    lower = lax.broadcasted_iota(jnp.int32, (8, C), 0) < 2

    def merge_forward(c, carry):
        pieces = []
        for i in range(CH):
            row = attx[CH * c + 3 + i].astype(F32)
            edge = pair_half(he, 2 * c + (3 + i) // 2, (3 + i) % 2)
            pieces.append(jnp.concatenate([row[:40], jnp.where(lower, row[40:], edge)], axis=0))
        att = jnp.concatenate(pieces, axis=0).astype(BF)
        attx[pl.ds(CH * c + 3, CH)] = att.reshape(CH, COLS, C)
        proj = dot(att, wo[...], 1, 0).reshape(CH, COLS, C)
        mixed = (text[pl.ds(CH * c + 3, CH)].astype(F32) + proj).astype(BF).astype(F32)
        for q in range(4):
            s1[q] = mixed[:, :, 128 * q : 128 * (q + 1)]
        parts = []
        for b in range(2):
            for a in range(2):
                for q in range(4):
                    piece = [s1[q, 2 * i + a, pl.ds(b, COLS // 2, stride=2), :] for i in range(CH // 2)]
                    parts.append(jnp.concatenate(piece, axis=0))
        xhat, rstd = moments(jnp.concatenate(parts, axis=1))
        here = pl.ds(pl.multiple_of(c * MT, MT), MT)
        xh[here, :] = xhat
        rs[here, :] = rstd
        mi[here, :] = (xhat * gain).astype(BF)
        return carry

    lax.fori_loop(0, 3, merge_forward, 0)
    for copy in south:
        copy.wait_recv()
    lax.fori_loop(3, NCH, merge_forward, 0)
    gm = gmb[...].astype(F32).reshape(MALL, C2).astype(BF)

    def merged_tile(n, carry):
        cols = pl.ds(pl.multiple_of(n * 256, 256), 256)
        tile = dot(mi[...], wm[:, cols], 1, 0).reshape(ROWS // 2, COLS // 2, 256)
        merged_ref[:, :, cols] = tile.astype(BF)
        return carry


    def weight_tile(n, carry):
        cols = pl.ds(pl.multiple_of(n * 256, 256), 256)
        gwm[cols, :] = dot(mi[:, cols], gm, 0, 0).astype(BF)
        return carry

    lax.fori_loop(0, C4 // 256, weight_tile, 0)

    def summed(src, out, turn, n, ring):
        order = AXES[turn:] + AXES[:turn]
        return Sum(at, src, out, order, sums[4 * n : 4 * n + 4], send.at[n], recv.at[n], ring)

    wide = [
        summed(gwm.at[:, 0:384], outm_ref.at[:, 0:384], 0, 0, True),
        summed(gwm.at[:, 384:768], outm_ref.at[:, 384:768], 1, 1, True),
        summed(gwm.at[:, 768:1024], outm_ref.at[:, 768:1024], 2, 2, True),
    ]
    early = wide + [summed(qo.at[:, 0:128], outq_ref.at[:, 0:128], 2, 3, True)]
    late = [
        summed(qo.at[:, 128 * (t + 1) : 128 * (t + 2)], outq_ref.at[:, 128 * (t + 1) : 128 * (t + 2)], t, 4 + t, False)
        for t in range(3)
    ]

    def advance(group, n):
        for part in group:
            part.step(n)

    advance(wide, 0)

    def cotangent_tile(n, carry):
        cols = pl.ds(pl.multiple_of(n * 256, 256), 256)
        gi[:, cols] = dot(gm, wm[cols, :], 1, 1).astype(BF)
        return carry

    lax.fori_loop(0, C4 // 256, cotangent_tile, 0)
    ggm[...] = jnp.zeros_like(ggm)

    def merge_backward(c, carry):
        here = pl.ds(pl.multiple_of(c * MT, MT), MT)
        xhat = xh[here, :]
        g = gi[here, :].astype(F32)
        ggm[...] += jnp.sum(g * xhat, axis=0, keepdims=True)
        dx = g * gain
        m1 = jnp.mean(dx, axis=-1, keepdims=True)
        m2 = jnp.mean(dx * xhat, axis=-1, keepdims=True)
        dx = rs[here, :] * (dx - m1 - xhat * m2)
        for b in range(2):
            for a in range(2):
                for q in range(4):
                    start = C * (2 * b + a) + 128 * q
                    for i in range(CH // 2):
                        s1[q, 2 * i + a, pl.ds(b, COLS // 2, stride=2), :] = dx[
                            (COLS // 2) * i : (COLS // 2) * (i + 1), start : start + 128
                        ]
        mixed = jnp.concatenate([s1[q] for q in range(4)], axis=-1).astype(BF)
        gmix[pl.ds(c * CH, CH)] = mixed
        gatt = dot(mixed.reshape(CH * COLS, C), wo[...], 1, 1).reshape(CH, COLS, C)
        gext[pl.ds(CH * c + 3, CH)] = gatt.astype(BF)
        for m in range(CH // 2):
            pkg[(CH // 2) * c + m] = jnp.concatenate(
                [gatt[2 * m, 40:48], gatt[2 * m + 1, 40:48]], axis=0
            ).astype(BF)
        return carry

    def send_cotangents(first, count):
        return halos[2].start(pkg.at[pl.ds(first, count)], gw.at[pl.ds(first + 2, count)], 0, 1)

    lax.fori_loop(5, 6, merge_backward, 0)
    halos[2].start(gext.at[pl.ds(24, 3)], gext.at[pl.ds(0, 3)], 1, 0)
    halos[2].start(pkg.at[pl.ds(10, 2)], gw.at[pl.ds(0, 2)], 1, 1)
    send_cotangents(10, 2)
    lax.fori_loop(0, 3, merge_backward, 0)
    send_cotangents(0, 6)
    lax.fori_loop(3, 5, merge_backward, 0)
    send_cotangents(6, 4)
    flat = gmix[...].reshape(ROWS * COLS, C)
    att = attx[pl.ds(3, ROWS)].reshape(ROWS * COLS, C)
    gwo = dot(att, flat, 0, 0).astype(BF)
    for n in range(4):
        qo[C * n : C * (n + 1), 0:128] = gwo[:, 128 * n : 128 * (n + 1)]
    early[3].step(0)
    advance(early, 1)
    for copy in halos[2].copies:
        copy.wait_recv()

    def backward_row(w, carry):
        load_frame(fr, w, gext, gw)
        to_windows(fr, s2)

        def window(v, carry):
            masks = head_masks(1.0)
            n = NW * w + v
            cots, dps = [], []
            for p in range(PAIRS):
                gs = stacked(s2[v, :, 128 * p : 128 * (p + 1)], masks)
                cots.append(gs)
                dps.append(dot(qkv[n, :, 2 * C + 128 * p : 2 * C + 128 * (p + 1)], gs, 1, 1))
            for p in range(PAIRS):
                dq[v, :, 2 * C + 128 * p : 2 * C + 128 * (p + 1)] = dot(prob[n, p], cots[p], 1, 0)
            dss = []
            for p in range(PAIRS):
                pf = prob[n, p].astype(F32)
                delta = jnp.sum(pf * dps[p], axis=0, keepdims=True)
                dss.append((pf * (dps[p] - delta)).astype(BF))
            for p in range(PAIRS):
                dq[v, :, C + 128 * p : C + 128 * (p + 1)] = dot(dss[p], qst[n, p], 1, 0)
            for p in range(PAIRS):
                k = qkv[n, :, C + 128 * p : C + 128 * (p + 1)]
                dq[v, :, 128 * p : 128 * (p + 1)] = merged_heads(dot(dss[p], k, 0, 0)) * 0.125
            return carry

        lax.fori_loop(0, NW, window, 0)
        dall[pl.ds(pl.multiple_of(w * NWT, NWT), NWT), :] = dq[...].reshape(NWT, 3 * C).astype(BF)
        return carry

    lax.fori_loop(0, 2, backward_row, 0)
    advance(early, 2)
    lax.fori_loop(2, 4, backward_row, 0)
    advance(early, 3)
    for n in range(6):
        tile = dot(nrm[...], dall[:, 256 * n : 256 * (n + 1)], 0, 0).astype(BF)
        for k in range(2):
            g = 2 * n + k
            qo[C * (g // 3) : C * (g // 3 + 1), 128 * (1 + g % 3) : 128 * (2 + g % 3)] = tile[:, 128 * k : 128 * (k + 1)]
    advance(late, 0)
    gga[...] = jnp.zeros_like(gga)

    def dgrad_row(w, carry):
        rows = pl.ds(pl.multiple_of(w * NWT, NWT), NWT)
        s2[...] = dot(dall[rows, :], wq[...], 1, 1).astype(BF).astype(F32).reshape(NW, WIN, C)
        load_frame(fr, w, text, hw)
        xhat, rstd = moments(fr[...])
        fr[:, 0:8, :] = jnp.zeros((WLAT, 8, C), F32)
        fr[:, FR - 8 : FR, :] = jnp.zeros((WLAT, 8, C), F32)
        to_frame(s2, fr)
        g = fr[...]
        gga[...] += jnp.sum(g * xhat, axis=(0, 1)).reshape(1, C)
        dx = g * ga_ref[...].reshape(1, 1, C)
        m1 = jnp.mean(dx, axis=-1, keepdims=True)
        m2 = jnp.mean(dx * xhat, axis=-1, keepdims=True)
        fr[...] = rstd * (dx - m1 - xhat * m2)
        pack_rows(fr, bw2, w)
        for r in range(3):
            bn2[WLAT * w + r] = fr[r, 8:FR, :].astype(BF)
        for r in range(3):
            gtok_ref[WLAT * w + r] = fr[3 + r, 8:FR, :] + gmix[WLAT * w + r].astype(F32)

        @pl.when(w > 0)
        def _():
            for r in range(3):
                gtok_ref[WLAT * w - 3 + r] = fr[r, 8:FR, :] + gmix[WLAT * w - 3 + r].astype(F32)

        return carry

    lax.fori_loop(0, 1, dgrad_row, 0)
    halos[3].start(bn2.at[pl.ds(0, 3)], hs2, -1, 0)
    halos[3].start(bw2.at[pl.ds(0, 2)], he2.at[pl.ds(12, 2)], -1, -1)
    advance(late, 1)
    advance(early, 4)
    lax.fori_loop(1, 2, dgrad_row, 0)
    halos[3].start(bw2.at[pl.ds(0, 6)], he2.at[pl.ds(0, 6)], 0, -1)
    lax.fori_loop(2, 4, dgrad_row, 0)
    halos[3].start(bw2.at[pl.ds(6, 6)], he2.at[pl.ds(6, 6)], 0, -1)
    advance(early, 5)
    lax.fori_loop(0, C2 // 256, merged_tile, 0)
    stores = [
        pltpu.make_async_copy(src, dst, lsem.at[5 + n])
        for n, (src, dst) in enumerate(
            [(merged_ref, merged_out), (gtok_ref, gtok_out), (outm_ref, outm_out), (outq_ref, outq_out)]
        )
    ]
    stores[0].start()
    small[0] = jnp.zeros_like(small[0])
    small[0, 0:1, :] = gga[...]
    for n in range(4):
        small[0, 1 + n : 2 + n, :] = ggm[:, C * n : C * (n + 1)]
    gains = SmallSum(at, small, slots, ssend, srecv)
    gains.begin(0)
    advance(early, 6)
    for copy in halos[3].copies:
        copy.wait_recv()
    for r in range(3):
        gtok_ref[21 + r] = hs2[r].astype(F32) + gmix[21 + r].astype(F32)
    for r in range(ROWS):
        edge = pair_half(he2, (r + 3) // 2, (r + 3) % 2) + gmix[r, 32:48, :].astype(F32)[8:16]
        gtok_ref[r, 40:48, :] = jnp.where(lower, gtok_ref[r, 40:48, :], edge)
    stores[1].start()
    gains.end(0)
    gains.begin(1)
    advance(late, 2)
    gains.end(1)
    gains.begin(2)
    advance(early, 7)
    advance(late, 3)
    gains.end(2)
    gains.begin(3)
    advance(late, 4)
    gains.end(3)
    outs_ref[...] = small[4]
    advance(late, 5)
    advance(early, 8)
    advance(late, 6)
    advance(early, 9)
    advance(late, 7)
    advance(early, 10)
    stores[2].start()
    advance(late, 8)
    stores[3].start()
    gains.finish()
    for halo in halos:
        halo.left()
    for store in stores:
        store.wait()


def step_kernel(tokens, band, gain_a, w_qkv, w_out, grad_merged, w_merge, gain_m):
    vmem = pl.BlockSpec(memory_space=pltpu.VMEM)
    hbm = pl.BlockSpec(memory_space=pl.ANY)
    lanes = (384, 384, 256, 128, 128, 128, 128)
    sums = []
    for n in lanes:
        sums += sum_scratch(TALL, n)
    return pl.pallas_call(
        step_body,
        in_specs=[hbm, vmem, vmem, hbm, hbm, hbm, hbm, vmem],
        out_specs=[hbm] * 4 + [vmem],
        out_shape=[
            jax.ShapeDtypeStruct((ROWS // 2, COLS // 2, C2), BF),
            jax.ShapeDtypeStruct((ROWS, COLS, C), F32),
            jax.ShapeDtypeStruct((C4, C2), BF),
            jax.ShapeDtypeStruct((TALL, C), BF),
            jax.ShapeDtypeStruct((8, C), F32),
        ],
        scratch_shapes=[
            pltpu.VMEM((ROWS // 2, COLS // 2, C2), BF),
            pltpu.VMEM((ROWS, COLS, C), F32),
            pltpu.VMEM((C4, C2), BF),
            pltpu.VMEM((TALL, C), BF),
            pltpu.VMEM((27, COLS, C), BF),
            pltpu.VMEM((14, 16, C), BF),
            pltpu.VMEM((12, 16, C), BF),
            pltpu.VMEM((C, 3 * C), BF),
            pltpu.VMEM((C, C), BF),
            pltpu.VMEM((ROWS // 2, COLS // 2, C2), BF),
            pltpu.VMEM((C4, C2), BF),
            pltpu.VMEM((WROWS * NW, WIN, 3 * C), BF),
            pltpu.VMEM((WROWS * NW, PAIRS, WIN, 2 * WIN), BF),
            pltpu.VMEM((WROWS * NW, PAIRS, 2 * WIN, 128), BF),
            pltpu.VMEM((ROWS * COLS, C), BF),
            pltpu.VMEM((NW, WIN, C), F32),
            pltpu.VMEM((NW, WIN, C), F32),
            pltpu.VMEM((WLAT, FR, C), F32),
            pltpu.VMEM((27, COLS, C), BF),
            pltpu.VMEM((14, 16, C), BF),
            pltpu.VMEM((12, 16, C), BF),
            pltpu.VMEM((4, CH, COLS, 128), F32),
            pltpu.VMEM((MALL, C4), F32),
            pltpu.VMEM((MALL, 1), F32),
            pltpu.VMEM((MALL, C4), BF),
            pltpu.VMEM((MALL, C4), BF),
            pltpu.VMEM((C4, C2), BF),
            pltpu.VMEM((TALL, C), BF),
            pltpu.VMEM((ROWS, COLS, C), BF),
            pltpu.VMEM((27, COLS, C), BF),
            pltpu.VMEM((14, 16, C), BF),
            pltpu.VMEM((12, 16, C), BF),
            pltpu.VMEM((NW, WIN, 3 * C), F32),
            pltpu.VMEM((ROWS * COLS, 3 * C), BF),
            pltpu.VMEM((21, COLS, C), BF),
            pltpu.VMEM((12, 16, C), BF),
            pltpu.VMEM((3, COLS, C), BF),
            pltpu.VMEM((14, 16, C), BF),
            pltpu.VMEM((5, 8, C), F32),
            pltpu.VMEM((10, 8, C), F32),
            pltpu.VMEM((1, C4), F32),
            pltpu.VMEM((1, C), F32),
            pltpu.VMEM((WROWS, WIN, 2 * WIN), F32),
            pltpu.SemaphoreType.DMA((9,)),
            pltpu.SemaphoreType.DMA((4, 6)),
            pltpu.SemaphoreType.DMA((4, 6)),
            pltpu.SemaphoreType.DMA((7, SUM_COPIES)),
            pltpu.SemaphoreType.DMA((7, SUM_COPIES)),
            pltpu.SemaphoreType.DMA((10,)),
            pltpu.SemaphoreType.DMA((10,)),
        ]
        + sums,
        compiler_params=pltpu.CompilerParams(
            vmem_limit_bytes=62 * MIB, collective_id=0, has_side_effects=True
        ),
        name="step",
    )(tokens, band, gain_a, w_qkv, w_out, grad_merged, w_merge, gain_m)


def widen_body(m_ref, q_ref, s_ref, gm_ref, gq_ref, go_ref, ga_ref, gg_ref):
    gm_ref[...] = m_ref[...].astype(F32)
    go_ref[...] = q_ref[:, 0:128].astype(F32)
    gq_ref[...] = q_ref[:, 128:].astype(F32)
    ga_ref[...] = s_ref[0:1, :]
    for n in range(4):
        gg_ref[:, C * n : C * (n + 1)] = s_ref[1 + n : 2 + n, :]


def widen(sum_merge, sum_qo, sum_gain):
    return pl.pallas_call(
        widen_body,
        grid=(4, 2),
        in_specs=[
            pl.BlockSpec((C // 2, C2), lambda i, j: (2 * i + j, 0)),
            pl.BlockSpec((C // 2, C), lambda i, j: (2 * i + j, 0)),
            pl.BlockSpec((8, C), lambda i, j: (0, 0)),
        ],
        out_specs=[
            pl.BlockSpec((C // 2, C2), lambda i, j: (2 * i + j, 0)),
            pl.BlockSpec((C // 2, 384), lambda i, j: (j, i)),
            pl.BlockSpec((C // 2, 128), lambda i, j: (j, i)),
            pl.BlockSpec((1, C), lambda i, j: (0, 0)),
            pl.BlockSpec((1, C4), lambda i, j: (0, 0)),
        ],
        out_shape=[
            jax.ShapeDtypeStruct((C4, C2), F32),
            jax.ShapeDtypeStruct((C, 3 * C), F32),
            jax.ShapeDtypeStruct((C, C), F32),
            jax.ShapeDtypeStruct((1, C), F32),
            jax.ShapeDtypeStruct((1, C4), F32),
        ],
        compiler_params=pltpu.CompilerParams(vmem_limit_bytes=60 * MIB),
        name="widen",
    )(sum_merge, sum_qo, sum_gain)


def on_device(tokens, lat_band, gain_attn, w_qkv, w_out, gain_merge, w_merge, grad_merged):
    merged, grad_tokens, sum_merge, sum_qo, sum_gain = step_kernel(
        tokens, lat_band.reshape(1, -1), gain_attn.reshape(1, C), w_qkv, w_out, grad_merged, w_merge,
        gain_merge.reshape(1, C4)
    )
    gw_merge, gw_qkv, gw_out, gg_attn, gg_merge = widen(sum_merge, sum_qo, sum_gain)
    return merged, grad_tokens, gg_attn.reshape(C), gw_qkv, gw_out, gg_merge.reshape(C4), gw_merge


def solution(mesh):
    return jax.shard_map(
        on_device,
        mesh=mesh,
        in_specs=(P("lat", "lon", None), P(), P(), P(), P(), P(), P(), P("lat", "lon", None)),
        out_specs=(P("lat", "lon", None), P("lat", "lon", None), P(), P(), P(), P(), P()),
        check_vma=False,
    )
```

```python
import functools
import jax
import jax.numpy as jnp
from jax import lax
from jax.experimental import pallas as pl
from jax.experimental.pallas import tpu as pltpu
from jax.sharding import PartitionSpec as P

HEADS = 8
WLAT = 6
WLON = 12
EPSILON = 1e-05
F32 = jnp.float32
BF = jnp.bfloat16
ROWS = 24
COLS = 48
C = 512
WIN = 72
NW = COLS // WLON
PAIRS = HEADS // 2
MIB = 1 << 20


def dot(a, b, ca, cb):
    return lax.dot_general(a, b, (((ca,), (cb,)), ((), ())), preferred_element_type=F32)


def head_masks(scale):
    lane = lax.broadcasted_iota(jnp.int32, (1, 128), 1)
    low = jnp.where(lane < 64, scale, 0.0).astype(F32)
    high = jnp.where(lane < 64, 0.0, scale).astype(F32)
    return low, high


def stacked(value, masks):
    return jnp.concatenate([value * masks[0], value * masks[1]], axis=0).astype(BF)


def merged_heads(value):
    lane = lax.broadcasted_iota(jnp.int32, (WIN, 128), 1)
    return jnp.where(lane < 64, value[:WIN], value[WIN:])


def moments(x):
    mean = jnp.mean(x, axis=-1, keepdims=True)
    centered = x - mean
    var = jnp.mean(centered * centered, axis=-1, keepdims=True)
    rstd = lax.rsqrt(var + EPSILON)
    return centered * rstd, rstd


AXES = ("x", "y", "z")


def coordinates():
    lat = lax.axis_index("lat")
    lon = lax.axis_index("lon")
    return {"x": lon // 4, "y": (lat // 4) * 2 + (lon // 2) % 2, "z": lat % 4, "core": lon % 2}


def device(at):
    return ((at["y"] // 2) * 4 + at["z"], at["x"] * 4 + (at["y"] % 2) * 2 + at["core"])


def peer(at, axis, step):
    size = 2 if axis == "core" else 4
    return device({**at, axis: (at[axis] + step) % size})


def remote(src, dst, send, recv, target):
    return pltpu.make_async_remote_copy(
        src_ref=src, dst_ref=dst, send_sem=send, recv_sem=recv,
        device_id=target, device_id_type=pl.DeviceIdType.MESH,
    )


def neighbour(rows, cols):
    lat = lax.axis_index("lat")
    lon = lax.axis_index("lon")
    return ((lat + rows) % 8, (lon + cols) % 16)


EDGES = ((0, 1), (1, 0), (1, 1))


def greet(at):
    barrier = pltpu.get_barrier_semaphore()
    targets = [
        peer(at, axis, step)
        for axis, count in (("core", 2), ("x", 4), ("y", 4), ("z", 4))
        for step in range(1, count)
    ]
    targets += [neighbour(sign * r, sign * c) for sign in (1, -1) for r, c in EDGES]
    for target in targets:
        pl.semaphore_signal(barrier, inc=1, device_id=target, device_id_type=pl.DeviceIdType.MESH)
    pl.semaphore_wait(barrier, len(targets))


def add_rows(dst, start, terms, rows):
    chunk = min(rows, 64)

    def body(i, carry):
        total = None
        for ref, first in terms:
            piece = ref[pl.ds(pl.multiple_of(first + i * chunk, 16), chunk), :].astype(F32)
            total = piece if total is None else total + piece
        dst[pl.ds(pl.multiple_of(start + i * chunk, 16), chunk), :] = total.astype(dst.dtype)
        return carry

    lax.fori_loop(0, rows // chunk, body, 0)


class Sum:
    def __init__(self, at, src, out, order, recvs, send, recv, ring):
        self.at, self.src, self.out, self.order = at, src, out, order
        self.recvs, self.send, self.recv = recvs, send, recv
        self.rows, self.ring = src.shape[0], ring
        self.sent = []

    def start(self, src, dst, index, target):
        copy = remote(src, dst, self.send.at[index], self.recv.at[index], target)
        copy.start()
        self.sent.append(copy)
        return copy

    def block(self, level):
        return self.rows // 2 // 4**level

    def first(self, levels):
        first = self.at["core"] * (self.rows // 2)
        for level in range(levels):
            first = first + self.at[self.order[level]] * self.block(level + 1)
        return pl.multiple_of(first, 16)

    def begin(self):
        half = self.rows // 2
        theirs = pl.ds(pl.multiple_of((1 - self.at["core"]) * half, 16), half)
        self.last = [self.start(self.src.at[theirs, :], self.recvs[0].at[0], 0, peer(self.at, "core", 1))]

    def combine(self, level):
        for copy in self.last:
            copy.wait_recv()
        count = self.block(level)
        first = self.first(level)
        terms = [(self.src, first)] + [(self.recvs[level].at[s], 0) for s in range(1 if level == 0 else 3)]
        if level == 3:
            add_rows(self.out, first, terms, count)
            self.gather(3)
            return
        if level == 1 and self.ring:
            terms = [(self.src, first), (self.recvs[1].at[1], 0), (self.recvs[1].at[2], 0)]
        add_rows(self.src, first, terms, count)
        if level == 0 and self.ring:
            self.ring_start()
            return
        axis = self.order[level]
        block = self.block(level + 1)
        self.last = []
        for step in range(1, 4):
            there = pl.multiple_of(first + (self.at[axis] + step) % 4 * block, 16)
            self.last.append(
                self.start(
                    self.src.at[pl.ds(there, block), :], self.recvs[level + 1].at[step - 1],
                    3 * level + step, peer(self.at, axis, step),
                )
            )

    def part(self, step, half):
        block = self.block(1)
        return pl.multiple_of(self.first(0) + (self.at[self.order[0]] + step) % 4 * block + half * (block // 2), 16)

    def ring_send(self, step, half, slot, index, towards):
        size = self.block(1) // 2
        return self.start(
            self.src.at[pl.ds(self.part(step, half), size), :],
            self.recvs[1].at[slot, pl.ds(half * size, size), :],
            index, peer(self.at, self.order[0], towards),
        )

    def ring_start(self):
        self.relayed = [self.ring_send(2, 0, 0, 20, 1), self.ring_send(2, 1, 0, 21, 3)]
        self.last = [self.ring_send(1, 1, 1, 22, 1), self.ring_send(3, 0, 1, 23, 3)]

    def ring_relay(self):
        for copy in self.relayed:
            copy.wait_recv()
        size = self.block(1) // 2
        for step, half, index in ((1, 0, 24), (3, 1, 25)):
            first = self.part(step, half)
            add_rows(self.src, first, [(self.src, first), (self.recvs[1].at[0], half * size)], size)
            self.last.append(self.ring_send(step, half, 2, index, step))

    def ring_forward(self):
        for copy in self.last:
            copy.wait_recv()
        size = self.block(1) // 2
        self.last = []
        for step, half, index in ((3, 0, 28), (1, 1, 29)):
            rows = self.out.at[pl.ds(self.part(step, half), size), :]
            self.last.append(self.start(rows, rows, index, peer(self.at, self.order[0], 4 - step)))

    def gather(self, level):
        mine = self.out.at[pl.ds(self.first(level), self.block(level)), :]
        if level == 0:
            self.last = [self.start(mine, mine, 19, peer(self.at, "core", 1))]
            return
        axis = self.order[level - 1]
        if level == 1 and self.ring:
            self.last = [self.start(mine, mine, 26 + n, peer(self.at, axis, step)) for n, step in enumerate((1, 3))]
            return
        self.last = [
            self.start(mine, mine, 10 + 3 * (level - 1) + step - 1, peer(self.at, axis, step)) for step in range(1, 4)
        ]

    def gathered(self, level):
        for copy in self.last:
            copy.wait_recv()
        self.gather(level - 1)

    def finish(self):
        self.last[0].wait_recv()
        for copy in self.sent:
            copy.wait_send()

    def step(self, n):
        if self.ring:
            if n == 2:
                self.ring_relay()
                return
            if n == 8:
                self.ring_forward()
                return
            n = n - (n > 2) - (n > 8)
        if n == 0:
            self.begin()
        elif n < 5:
            self.combine(n - 1)
        elif n < 8:
            self.gathered(8 - n)
        else:
            self.finish()


SUM_COPIES = 30


def sum_scratch(rows, lanes):
    half = rows // 2
    return [pltpu.VMEM((1, half, lanes), BF)] + [pltpu.VMEM((3, half // 4**n, lanes), BF) for n in (1, 2, 3)]


class SmallSum:
    def __init__(self, at, block, slots, send, recv):
        self.at, self.block, self.slots, self.send, self.recv = at, block, slots, send, recv
        self.sent = []

    def begin(self, level):
        axis, count = (("core", 2), ("x", 4), ("y", 4), ("z", 4))[level]
        base = 0 if level == 0 else 3 * level - 2
        self.last = []
        for step in range(1, count):
            i = base + step - 1
            copy = remote(self.block.at[level], self.slots.at[i], self.send.at[i], self.recv.at[i],
                          peer(self.at, axis, step))
            copy.start()
            self.last.append((copy, i))
            self.sent.append(copy)

    def end(self, level):
        total = self.block[level]
        for copy, i in self.last:
            copy.wait_recv()
            total = total + self.slots[i]
        self.block[level + 1] = total

    def finish(self):
        for copy in self.sent:
            copy.wait_send()

CH = 4
NCH = ROWS // CH
MT = (CH // 2) * (COLS // 2)
MALL = NCH * MT
C4 = 4 * C
C2 = 1024
WROWS = ROWS // WLAT
NWT = NW * WIN
FR = COLS + 8
TALL = 4 * C


class Halo:
    def __init__(self, send, recv):
        self.send, self.recv, self.copies = send, recv, []

    def start(self, src, dst, rows, cols):
        n = len(self.copies)
        copy = remote(src, dst, self.send.at[n], self.recv.at[n], neighbour(rows, cols))
        copy.start()
        self.copies.append(copy)
        return copy

    def left(self):
        for copy in self.copies:
            copy.wait_send()


def band_bias(band_ref, bias):
    band = band_ref[...].astype(F32)
    total = band.shape[1]

    def grid_row(place, first):
        row = first + jnp.floor((place.astype(F32) + 0.5) * (1.0 / WLON)).astype(jnp.int32)
        return jnp.where(row >= total, row - total, row)

    for w in range(WROWS):
        first = (lax.axis_index("lat") * ROWS + WLAT * w - 3 + total) % total
        key = lax.broadcasted_iota(jnp.int32, (WIN, total), 0)
        hit = grid_row(key, first) == lax.broadcasted_iota(jnp.int32, (WIN, total), 1)
        keys = jnp.sum(jnp.where(hit, band, 0.0), axis=1, keepdims=True)
        query = lax.broadcasted_iota(jnp.int32, (total, 2 * WIN), 1)
        query = jnp.where(query >= WIN, query - WIN, query)
        hit = grid_row(query, first) == lax.broadcasted_iota(jnp.int32, (total, 2 * WIN), 0)
        queries = dot(jnp.broadcast_to(band, (8, total)).astype(BF), jnp.where(hit, 1.0, 0.0).astype(BF), 1, 0)
        bias[w] = jnp.where(keys == queries[0:1], 0.0, -1e30)


def pair_half(ref, pair, half):
    return ref[pair].astype(F32)[8 * half : 8 * half + 8]


def load_frame(fr, w, rows_ref, edge_ref):
    for r in range(WLAT):
        fr[r, 8:FR, :] = rows_ref[WLAT * w + r].astype(F32)
        fr[r, 0:8, :] = pair_half(edge_ref, 3 * w + (r + 1) // 2, (r + 1) % 2)


def to_windows(fr, dst):
    for v in range(NW):
        for r in range(WLAT):
            dst[v, WLON * r : WLON * (r + 1), :] = fr[r, WLON * v + 2 : WLON * v + 14, :]


def to_frame(src, fr):
    for v in range(NW):
        for r in range(WLAT):
            fr[r, WLON * v + 2 : WLON * v + 14, :] = src[v, WLON * r : WLON * (r + 1), :]


def pack_rows(fr, edge_ref, w):
    for r in range(0, WLAT, 2):
        edge_ref[3 * w + r // 2] = jnp.concatenate([fr[r, 0:8, :], fr[r + 1, 0:8, :]], axis=0).astype(BF)


def step_body(tok_hbm, band_ref, ga_ref, wq_hbm, wo_hbm, gm_hbm, wm_hbm, gmg_ref,
              merged_out, gtok_out, outm_out, outq_out, outs_ref,
              merged_ref, gtok_ref, om0, om1, om2, oq0, oq1, oq2, oq3,
              text, hw, pk, wq, wo, gmb, wm, qkv, prob, qst, nrm, qf, s2, fr, attx, he, bw,
              s1, xh, rs, mi, gi, gw0, gw1, gw2, qo0, qo1, qo2, qo3, gmix, gext, gw, pkg, dq, dall, bn2, bw2, hs2, he2,
              small, slots, ggm, gga, bias, lsem, hsend, hrecv, send, recv, ssend, srecv, *sums):
    loads = [
        pltpu.make_async_copy(src, dst, lsem.at[n])
        for n, (src, dst) in enumerate(
            [(tok_hbm, text.at[pl.ds(3, ROWS)]), (wq_hbm, wq), (wo_hbm, wo), (gm_hbm, gmb), (wm_hbm, wm)]
        )
    ]
    for load in loads:
        load.start()
    at = coordinates()
    greet(at)
    halos = [Halo(hsend.at[n], hrecv.at[n]) for n in range(4)]

    loads[0].wait()

    def pack_tokens(first, count):
        for m in range(first, first + count):
            pk[m] = jnp.concatenate(
                [text[3 + 2 * m + k, 32:48, :].astype(F32)[8:16] for k in range(2)], axis=0
            ).astype(BF)
        return halos[0].start(pk.at[pl.ds(first, count)], hw.at[pl.ds(first + 2, count)], 0, 1)

    north = [halos[0].start(text.at[pl.ds(24, 3)], text.at[pl.ds(0, 3)], 1, 0)]
    west = [pack_tokens(1, 4), pack_tokens(5, 7)]
    north.append(pack_tokens(0, 1))
    north.append(halos[0].start(pk.at[pl.ds(10, 2)], hw.at[pl.ds(0, 2)], 1, 1))
    band_bias(band_ref, bias)
    loads[1].wait()

    def forward_row(w, carry):
        load_frame(fr, w, text, hw)
        xhat, _ = moments(fr[...])
        fr[...] = xhat * ga_ref[...].reshape(1, 1, C)
        to_windows(fr, s2)
        normed = s2[...].reshape(NWT, C).astype(BF)
        nrm[pl.ds(pl.multiple_of(w * NWT, NWT), NWT), :] = normed
        for t in range(3):
            part = dot(normed, wq[:, C * t : C * (t + 1)], 1, 0).reshape(NW, WIN, C)
            if t == 0:
                qf[...] = part
            qkv[pl.ds(NW * w, NW), :, C * t : C * (t + 1)] = part.astype(BF)
        mask = bias[w]

        def window(v, carry):
            masks = head_masks(0.125)
            n = NW * w + v
            scores = []
            for p in range(PAIRS):
                qs = stacked(qf[v, :, 128 * p : 128 * (p + 1)].astype(BF).astype(F32), masks)
                qst[n, p] = qs
                scores.append(dot(qkv[n, :, C + 128 * p : C + 128 * (p + 1)], qs, 1, 1))
            probs = []
            for p in range(PAIRS):
                s = scores[p] + mask
                e = jnp.exp(s - jnp.max(s, axis=0, keepdims=True))
                pr = (e * (1.0 / jnp.sum(e, axis=0, keepdims=True))).astype(BF)
                prob[n, p] = pr
                probs.append(pr)
            for p in range(PAIRS):
                val = qkv[n, :, 2 * C + 128 * p : 2 * C + 128 * (p + 1)]
                s2[v, :, 128 * p : 128 * (p + 1)] = merged_heads(dot(probs[p], val, 0, 0))
            return carry

        lax.fori_loop(0, NW, window, 0)
        to_frame(s2, fr)
        pack_rows(fr, bw, w)
        for r in range(WLAT):
            attx[WLAT * w + r] = fr[r, 8:FR, :].astype(BF)
        return carry

    def send_back(w):
        return halos[1].start(bw.at[pl.ds(3 * w, 3)], he.at[pl.ds(3 * w, 3)], 0, -1)

    west[0].wait_recv()
    lax.fori_loop(1, 2, forward_row, 0)
    east = [send_back(1)]
    for copy in north + west[1:]:
        copy.wait_recv()
    lax.fori_loop(0, 1, forward_row, 0)
    south = [
        halos[1].start(attx.at[pl.ds(0, 3)], attx.at[pl.ds(24, 3)], -1, 0),
        halos[1].start(bw.at[pl.ds(0, 2)], he.at[pl.ds(12, 2)], -1, -1),
    ]
    east.append(send_back(0))
    lax.fori_loop(2, 3, forward_row, 0)
    east.append(send_back(2))
    lax.fori_loop(3, 4, forward_row, 0)
    south.append(send_back(3))
    for load in loads[2:]:
        load.wait()
    for copy in east:
        copy.wait_recv()
    gain = gmg_ref[...]
    lower = lax.broadcasted_iota(jnp.int32, (8, C), 0) < 2

    def merge_forward(c, carry):
        pieces = []
        for i in range(CH):
            row = attx[CH * c + 3 + i].astype(F32)
            edge = pair_half(he, 2 * c + (3 + i) // 2, (3 + i) % 2)
            pieces.append(jnp.concatenate([row[:40], jnp.where(lower, row[40:], edge)], axis=0))
        att = jnp.concatenate(pieces, axis=0).astype(BF)
        attx[pl.ds(CH * c + 3, CH)] = att.reshape(CH, COLS, C)
        proj = dot(att, wo[...], 1, 0).reshape(CH, COLS, C)
        mixed = (text[pl.ds(CH * c + 3, CH)].astype(F32) + proj).astype(BF).astype(F32)
        for q in range(4):
            s1[q] = mixed[:, :, 128 * q : 128 * (q + 1)]
        parts = []
        for b in range(2):
            for a in range(2):
                for q in range(4):
                    piece = [s1[q, 2 * i + a, pl.ds(b, COLS // 2, stride=2), :] for i in range(CH // 2)]
                    parts.append(jnp.concatenate(piece, axis=0))
        xhat, rstd = moments(jnp.concatenate(parts, axis=1))
        here = pl.ds(pl.multiple_of(c * MT, MT), MT)
        xh[here, :] = xhat
        rs[here, :] = rstd
        mi[here, :] = (xhat * gain).astype(BF)
        return carry

    lax.fori_loop(0, 3, merge_forward, 0)
    for copy in south:
        copy.wait_recv()
    lax.fori_loop(3, NCH, merge_forward, 0)
    gm = gmb[...].astype(F32).reshape(MALL, C2).astype(BF)

    def merged_tile(n, carry):
        cols = pl.ds(pl.multiple_of(n * 256, 256), 256)
        tile = dot(mi[...], wm[:, cols], 1, 0).reshape(ROWS // 2, COLS // 2, 256)
        merged_ref[:, :, cols] = tile.astype(BF)
        return carry


    def weight_tile(n, carry):
        cols = pl.ds(pl.multiple_of(n * 256, 256), 256)
        tile = dot(mi[:, cols], gm, 0, 0).astype(BF)
        gw0[cols, :] = tile[:, 0:384]
        gw1[cols, :] = tile[:, 384:768]
        gw2[cols, :] = tile[:, 768:1024]
        return carry

    lax.fori_loop(0, C4 // 256, weight_tile, 0)

    def summed(src, out, turn, n, ring):
        order = AXES[turn:] + AXES[:turn]
        return Sum(at, src, out, order, sums[4 * n : 4 * n + 4], send.at[n], recv.at[n], ring)

    wide = [
        summed(gw0, om0, 0, 0, True),
        summed(gw1, om1, 1, 1, True),
        summed(gw2, om2, 2, 2, True),
    ]
    early = wide + [summed(qo0, oq0, 2, 3, True)]
    late = [
        summed((qo1, qo2, qo3)[t], (oq1, oq2, oq3)[t], t, 4 + t, False)
        for t in range(3)
    ]

    def advance(group, n):
        for part in group:
            part.step(n)

    advance(wide, 0)

    def cotangent_tile(n, carry):
        cols = pl.ds(pl.multiple_of(n * 256, 256), 256)
        gi[:, cols] = dot(gm, wm[cols, :], 1, 1).astype(BF)
        return carry

    lax.fori_loop(0, C4 // 256, cotangent_tile, 0)
    ggm[...] = jnp.zeros_like(ggm)

    def merge_backward(c, carry):
        here = pl.ds(pl.multiple_of(c * MT, MT), MT)
        xhat = xh[here, :]
        g = gi[here, :].astype(F32)
        ggm[...] += jnp.sum(g * xhat, axis=0, keepdims=True)
        dx = g * gain
        m1 = jnp.mean(dx, axis=-1, keepdims=True)
        m2 = jnp.mean(dx * xhat, axis=-1, keepdims=True)
        dx = rs[here, :] * (dx - m1 - xhat * m2)
        for b in range(2):
            for a in range(2):
                for q in range(4):
                    start = C * (2 * b + a) + 128 * q
                    for i in range(CH // 2):
                        s1[q, 2 * i + a, pl.ds(b, COLS // 2, stride=2), :] = dx[
                            (COLS // 2) * i : (COLS // 2) * (i + 1), start : start + 128
                        ]
        mixed = jnp.concatenate([s1[q] for q in range(4)], axis=-1).astype(BF)
        gmix[pl.ds(c * CH, CH)] = mixed
        gatt = dot(mixed.reshape(CH * COLS, C), wo[...], 1, 1).reshape(CH, COLS, C)
        gext[pl.ds(CH * c + 3, CH)] = gatt.astype(BF)
        for m in range(CH // 2):
            pkg[(CH // 2) * c + m] = jnp.concatenate(
                [gatt[2 * m, 40:48], gatt[2 * m + 1, 40:48]], axis=0
            ).astype(BF)
        return carry

    def send_cotangents(first, count):
        return halos[2].start(pkg.at[pl.ds(first, count)], gw.at[pl.ds(first + 2, count)], 0, 1)

    lax.fori_loop(5, 6, merge_backward, 0)
    halos[2].start(gext.at[pl.ds(24, 3)], gext.at[pl.ds(0, 3)], 1, 0)
    halos[2].start(pkg.at[pl.ds(10, 2)], gw.at[pl.ds(0, 2)], 1, 1)
    send_cotangents(10, 2)
    lax.fori_loop(0, 3, merge_backward, 0)
    send_cotangents(0, 6)
    lax.fori_loop(3, 5, merge_backward, 0)
    send_cotangents(6, 4)
    flat = gmix[...].reshape(ROWS * COLS, C)
    att = attx[pl.ds(3, ROWS)].reshape(ROWS * COLS, C)
    gwo = dot(att, flat, 0, 0).astype(BF)
    for n in range(4):
        qo0[C * n : C * (n + 1), :] = gwo[:, 128 * n : 128 * (n + 1)]
    early[3].step(0)
    advance(early, 1)
    for copy in halos[2].copies:
        copy.wait_recv()

    def backward_row(w, carry):
        load_frame(fr, w, gext, gw)
        to_windows(fr, s2)

        def window(v, carry):
            masks = head_masks(1.0)
            n = NW * w + v
            cots, dps = [], []
            for p in range(PAIRS):
                gs = stacked(s2[v, :, 128 * p : 128 * (p + 1)], masks)
                cots.append(gs)
                dps.append(dot(qkv[n, :, 2 * C + 128 * p : 2 * C + 128 * (p + 1)], gs, 1, 1))
            for p in range(PAIRS):
                dq[v, :, 2 * C + 128 * p : 2 * C + 128 * (p + 1)] = dot(prob[n, p], cots[p], 1, 0)
            dss = []
            for p in range(PAIRS):
                pf = prob[n, p].astype(F32)
                delta = jnp.sum(pf * dps[p], axis=0, keepdims=True)
                dss.append((pf * (dps[p] - delta)).astype(BF))
            for p in range(PAIRS):
                dq[v, :, C + 128 * p : C + 128 * (p + 1)] = dot(dss[p], qst[n, p], 1, 0)
            for p in range(PAIRS):
                k = qkv[n, :, C + 128 * p : C + 128 * (p + 1)]
                dq[v, :, 128 * p : 128 * (p + 1)] = merged_heads(dot(dss[p], k, 0, 0)) * 0.125
            return carry

        lax.fori_loop(0, NW, window, 0)
        dall[pl.ds(pl.multiple_of(w * NWT, NWT), NWT), :] = dq[...].reshape(NWT, 3 * C).astype(BF)
        return carry

    lax.fori_loop(0, 2, backward_row, 0)
    advance(early, 2)
    lax.fori_loop(2, 4, backward_row, 0)
    advance(early, 3)
    for n in range(6):
        tile = dot(nrm[...], dall[:, 256 * n : 256 * (n + 1)], 0, 0).astype(BF)
        for k in range(2):
            g = 2 * n + k
            (qo1, qo2, qo3)[g % 3][C * (g // 3) : C * (g // 3 + 1), :] = tile[:, 128 * k : 128 * (k + 1)]
    advance(late, 0)
    gga[...] = jnp.zeros_like(gga)

    def dgrad_row(w, carry):
        rows = pl.ds(pl.multiple_of(w * NWT, NWT), NWT)
        s2[...] = dot(dall[rows, :], wq[...], 1, 1).astype(BF).astype(F32).reshape(NW, WIN, C)
        load_frame(fr, w, text, hw)
        xhat, rstd = moments(fr[...])
        fr[:, 0:8, :] = jnp.zeros((WLAT, 8, C), F32)
        fr[:, FR - 8 : FR, :] = jnp.zeros((WLAT, 8, C), F32)
        to_frame(s2, fr)
        g = fr[...]
        gga[...] += jnp.sum(g * xhat, axis=(0, 1)).reshape(1, C)
        dx = g * ga_ref[...].reshape(1, 1, C)
        m1 = jnp.mean(dx, axis=-1, keepdims=True)
        m2 = jnp.mean(dx * xhat, axis=-1, keepdims=True)
        fr[...] = rstd * (dx - m1 - xhat * m2)
        pack_rows(fr, bw2, w)
        for r in range(3):
            bn2[WLAT * w + r] = fr[r, 8:FR, :].astype(BF)
        for r in range(3):
            gtok_ref[WLAT * w + r] = fr[3 + r, 8:FR, :] + gmix[WLAT * w + r].astype(F32)

        @pl.when(w > 0)
        def _():
            for r in range(3):
                gtok_ref[WLAT * w - 3 + r] = fr[r, 8:FR, :] + gmix[WLAT * w - 3 + r].astype(F32)

        return carry

    lax.fori_loop(0, 1, dgrad_row, 0)
    halos[3].start(bn2.at[pl.ds(0, 3)], hs2, -1, 0)
    halos[3].start(bw2.at[pl.ds(0, 2)], he2.at[pl.ds(12, 2)], -1, -1)
    advance(late, 1)
    advance(early, 4)
    lax.fori_loop(1, 2, dgrad_row, 0)
    halos[3].start(bw2.at[pl.ds(0, 6)], he2.at[pl.ds(0, 6)], 0, -1)
    lax.fori_loop(2, 4, dgrad_row, 0)
    halos[3].start(bw2.at[pl.ds(6, 6)], he2.at[pl.ds(6, 6)], 0, -1)
    advance(early, 5)
    lax.fori_loop(0, C2 // 256, merged_tile, 0)
    stores = [
        pltpu.make_async_copy(src, dst, lsem.at[5 + n])
        for n, (src, dst) in enumerate(
            [(merged_ref, merged_out), (gtok_ref, gtok_out)]
            + [(om, outm_out.at[:, 384 * k : 384 * k + om.shape[1]]) for k, om in enumerate((om0, om1, om2))]
            + [(oq, outq_out.at[:, 128 * k : 128 * (k + 1)]) for k, oq in enumerate((oq0, oq1, oq2, oq3))]
        )
    ]
    stores[0].start()
    small[0] = jnp.zeros_like(small[0])
    small[0, 0:1, :] = gga[...]
    for n in range(4):
        small[0, 1 + n : 2 + n, :] = ggm[:, C * n : C * (n + 1)]
    gains = SmallSum(at, small, slots, ssend, srecv)
    gains.begin(0)
    advance(early, 6)
    for copy in halos[3].copies:
        copy.wait_recv()
    for r in range(3):
        gtok_ref[21 + r] = hs2[r].astype(F32) + gmix[21 + r].astype(F32)
    for r in range(ROWS):
        edge = pair_half(he2, (r + 3) // 2, (r + 3) % 2) + gmix[r, 32:48, :].astype(F32)[8:16]
        gtok_ref[r, 40:48, :] = jnp.where(lower, gtok_ref[r, 40:48, :], edge)
    stores[1].start()
    gains.end(0)
    gains.begin(1)
    advance(late, 2)
    gains.end(1)
    gains.begin(2)
    advance(early, 7)
    advance(late, 3)
    gains.end(2)
    gains.begin(3)
    advance(late, 4)
    gains.end(3)
    outs_ref[...] = small[4]
    advance(late, 5)
    advance(early, 8)
    advance(late, 6)
    advance(early, 9)
    advance(late, 7)
    advance(early, 10)
    for store in stores[2:6]:
        store.start()
    advance(late, 8)
    for store in stores[6:]:
        store.start()
    gains.finish()
    for halo in halos:
        halo.left()
    for store in stores:
        store.wait()


def step_kernel(tokens, band, gain_a, w_qkv, w_out, grad_merged, w_merge, gain_m):
    vmem = pl.BlockSpec(memory_space=pltpu.VMEM)
    hbm = pl.BlockSpec(memory_space=pl.ANY)
    lanes = (384, 384, 256, 128, 128, 128, 128)
    sums = []
    for n in lanes:
        sums += sum_scratch(TALL, n)
    wide = [pltpu.VMEM((TALL, n), BF) for n in lanes]
    return pl.pallas_call(
        step_body,
        in_specs=[hbm, vmem, vmem, hbm, hbm, hbm, hbm, vmem],
        out_specs=[hbm] * 4 + [vmem],
        out_shape=[
            jax.ShapeDtypeStruct((ROWS // 2, COLS // 2, C2), BF),
            jax.ShapeDtypeStruct((ROWS, COLS, C), F32),
            jax.ShapeDtypeStruct((C4, C2), BF),
            jax.ShapeDtypeStruct((TALL, C), BF),
            jax.ShapeDtypeStruct((8, C), F32),
        ],
        scratch_shapes=[
            pltpu.VMEM((ROWS // 2, COLS // 2, C2), BF),
            pltpu.VMEM((ROWS, COLS, C), F32),
            *wide,
            pltpu.VMEM((27, COLS, C), BF),
            pltpu.VMEM((14, 16, C), BF),
            pltpu.VMEM((12, 16, C), BF),
            pltpu.VMEM((C, 3 * C), BF),
            pltpu.VMEM((C, C), BF),
            pltpu.VMEM((ROWS // 2, COLS // 2, C2), BF),
            pltpu.VMEM((C4, C2), BF),
            pltpu.VMEM((WROWS * NW, WIN, 3 * C), BF),
            pltpu.VMEM((WROWS * NW, PAIRS, WIN, 2 * WIN), BF),
            pltpu.VMEM((WROWS * NW, PAIRS, 2 * WIN, 128), BF),
            pltpu.VMEM((ROWS * COLS, C), BF),
            pltpu.VMEM((NW, WIN, C), F32),
            pltpu.VMEM((NW, WIN, C), F32),
            pltpu.VMEM((WLAT, FR, C), F32),
            pltpu.VMEM((27, COLS, C), BF),
            pltpu.VMEM((14, 16, C), BF),
            pltpu.VMEM((12, 16, C), BF),
            pltpu.VMEM((4, CH, COLS, 128), F32),
            pltpu.VMEM((MALL, C4), F32),
            pltpu.VMEM((MALL, 1), F32),
            pltpu.VMEM((MALL, C4), BF),
            pltpu.VMEM((MALL, C4), BF),
            *wide,
            pltpu.VMEM((ROWS, COLS, C), BF),
            pltpu.VMEM((27, COLS, C), BF),
            pltpu.VMEM((14, 16, C), BF),
            pltpu.VMEM((12, 16, C), BF),
            pltpu.VMEM((NW, WIN, 3 * C), F32),
            pltpu.VMEM((ROWS * COLS, 3 * C), BF),
            pltpu.VMEM((21, COLS, C), BF),
            pltpu.VMEM((12, 16, C), BF),
            pltpu.VMEM((3, COLS, C), BF),
            pltpu.VMEM((14, 16, C), BF),
            pltpu.VMEM((5, 8, C), F32),
            pltpu.VMEM((10, 8, C), F32),
            pltpu.VMEM((1, C4), F32),
            pltpu.VMEM((1, C), F32),
            pltpu.VMEM((WROWS, WIN, 2 * WIN), F32),
            pltpu.SemaphoreType.DMA((14,)),
            pltpu.SemaphoreType.DMA((4, 6)),
            pltpu.SemaphoreType.DMA((4, 6)),
            pltpu.SemaphoreType.DMA((7, SUM_COPIES)),
            pltpu.SemaphoreType.DMA((7, SUM_COPIES)),
            pltpu.SemaphoreType.DMA((10,)),
            pltpu.SemaphoreType.DMA((10,)),
        ]
        + sums,
        compiler_params=pltpu.CompilerParams(
            vmem_limit_bytes=62 * MIB, collective_id=0, has_side_effects=True
        ),
        name="step",
    )(tokens, band, gain_a, w_qkv, w_out, grad_merged, w_merge, gain_m)


def widen_body(m_ref, q_ref, s_ref, gm_ref, gq_ref, go_ref, ga_ref, gg_ref):
    gm_ref[...] = m_ref[...].astype(F32)
    go_ref[...] = q_ref[:, 0:128].astype(F32)
    gq_ref[...] = q_ref[:, 128:].astype(F32)
    ga_ref[...] = s_ref[0:1, :]
    for n in range(4):
        gg_ref[:, C * n : C * (n + 1)] = s_ref[1 + n : 2 + n, :]


def widen(sum_merge, sum_qo, sum_gain):
    return pl.pallas_call(
        widen_body,
        grid=(4,),
        in_specs=[
            pl.BlockSpec((C, C2), lambda i: (i, 0)),
            pl.BlockSpec((C, C), lambda i: (i, 0)),
            pl.BlockSpec((8, C), lambda i: (0, 0)),
        ],
        out_specs=[
            pl.BlockSpec((C, C2), lambda i: (i, 0)),
            pl.BlockSpec((C, 384), lambda i: (0, i)),
            pl.BlockSpec((C, 128), lambda i: (0, i)),
            pl.BlockSpec((1, C), lambda i: (0, 0)),
            pl.BlockSpec((1, C4), lambda i: (0, 0)),
        ],
        out_shape=[
            jax.ShapeDtypeStruct((C4, C2), F32),
            jax.ShapeDtypeStruct((C, 3 * C), F32),
            jax.ShapeDtypeStruct((C, C), F32),
            jax.ShapeDtypeStruct((1, C), F32),
            jax.ShapeDtypeStruct((1, C4), F32),
        ],
        compiler_params=pltpu.CompilerParams(vmem_limit_bytes=60 * MIB),
        name="widen",
    )(sum_merge, sum_qo, sum_gain)


def on_device(tokens, lat_band, gain_attn, w_qkv, w_out, gain_merge, w_merge, grad_merged):
    merged, grad_tokens, sum_merge, sum_qo, sum_gain = step_kernel(
        tokens, lat_band.reshape(1, -1), gain_attn.reshape(1, C), w_qkv, w_out, grad_merged, w_merge,
        gain_merge.reshape(1, C4)
    )
    gw_merge, gw_qkv, gw_out, gg_attn, gg_merge = widen(sum_merge, sum_qo, sum_gain)
    return merged, grad_tokens, gg_attn.reshape(C), gw_qkv, gw_out, gg_merge.reshape(C4), gw_merge


def solution(mesh):
    return jax.shard_map(
        on_device,
        mesh=mesh,
        in_specs=(P("lat", "lon", None), P(), P(), P(), P(), P(), P(), P("lat", "lon", None)),
        out_specs=(P("lat", "lon", None), P("lat", "lon", None), P(), P(), P(), P(), P()),
        check_vma=False,
    )
```

```python
import functools
import jax
import jax.numpy as jnp
from jax import lax
from jax.experimental import pallas as pl
from jax.experimental.pallas import tpu as pltpu
from jax.sharding import PartitionSpec as P

HEADS = 8
WLAT = 6
WLON = 12
EPSILON = 1e-05
F32 = jnp.float32
BF = jnp.bfloat16
ROWS = 24
COLS = 48
C = 512
WIN = 72
NW = COLS // WLON
PAIRS = HEADS // 2
MIB = 1 << 20


def dot(a, b, ca, cb):
    return lax.dot_general(a, b, (((ca,), (cb,)), ((), ())), preferred_element_type=F32)


def head_masks(scale):
    lane = lax.broadcasted_iota(jnp.int32, (1, 128), 1)
    low = jnp.where(lane < 64, scale, 0.0).astype(F32)
    high = jnp.where(lane < 64, 0.0, scale).astype(F32)
    return low, high


def stacked(value, masks):
    return jnp.concatenate([value * masks[0], value * masks[1]], axis=0).astype(BF)


def merged_heads(value):
    lane = lax.broadcasted_iota(jnp.int32, (WIN, 128), 1)
    return jnp.where(lane < 64, value[:WIN], value[WIN:])


def moments(x):
    mean = jnp.mean(x, axis=-1, keepdims=True)
    centered = x - mean
    var = jnp.mean(centered * centered, axis=-1, keepdims=True)
    rstd = lax.rsqrt(var + EPSILON)
    return centered * rstd, rstd


AXES = ("x", "y", "z")


def coordinates():
    lat = lax.axis_index("lat")
    lon = lax.axis_index("lon")
    return {"x": lon // 4, "y": (lat // 4) * 2 + (lon // 2) % 2, "z": lat % 4, "core": lon % 2}


def device(at):
    return ((at["y"] // 2) * 4 + at["z"], at["x"] * 4 + (at["y"] % 2) * 2 + at["core"])


def peer(at, axis, step):
    size = 2 if axis == "core" else 4
    return device({**at, axis: (at[axis] + step) % size})


def remote(src, dst, send, recv, target):
    return pltpu.make_async_remote_copy(
        src_ref=src, dst_ref=dst, send_sem=send, recv_sem=recv,
        device_id=target, device_id_type=pl.DeviceIdType.MESH,
    )


def neighbour(rows, cols):
    lat = lax.axis_index("lat")
    lon = lax.axis_index("lon")
    return ((lat + rows) % 8, (lon + cols) % 16)


EDGES = ((0, 1), (1, 0), (1, 1))


def greet(at):
    barrier = pltpu.get_barrier_semaphore()
    targets = [
        peer(at, axis, step)
        for axis, count in (("core", 2), ("x", 4), ("y", 4), ("z", 4))
        for step in range(1, count)
    ]
    targets += [neighbour(sign * r, sign * c) for sign in (1, -1) for r, c in EDGES]
    for target in targets:
        pl.semaphore_signal(barrier, inc=1, device_id=target, device_id_type=pl.DeviceIdType.MESH)
    pl.semaphore_wait(barrier, len(targets))


def add_rows(dst, start, terms, rows):
    chunk = min(rows, 64)

    def body(i, carry):
        total = None
        for ref, first in terms:
            piece = ref[pl.ds(pl.multiple_of(first + i * chunk, 16), chunk), :].astype(F32)
            total = piece if total is None else total + piece
        dst[pl.ds(pl.multiple_of(start + i * chunk, 16), chunk), :] = total.astype(dst.dtype)
        return carry

    lax.fori_loop(0, rows // chunk, body, 0)


class Sum:
    def __init__(self, at, src, out, order, recvs, send, recv):
        self.at, self.src, self.out, self.order = at, src, out, order
        self.recvs, self.send, self.recv = recvs, send, recv
        self.rows = src.shape[0]
        self.sent = []

    def start(self, src, dst, index, target):
        copy = remote(src, dst, self.send.at[index], self.recv.at[index], target)
        copy.start()
        self.sent.append(copy)
        return copy

    def block(self, level):
        return self.rows // 2 // 4**level

    def first(self, levels):
        first = self.at["core"] * (self.rows // 2)
        for level in range(levels):
            first = first + self.at[self.order[level]] * self.block(level + 1)
        return pl.multiple_of(first, 16)

    def begin(self):
        block = self.block(1)
        self.last = []
        for n, step in enumerate((1, 2, 3, 0)):
            place = (self.at[self.order[0]] + step) % 4 * block
            theirs = pl.multiple_of((1 - self.at["core"]) * (self.rows // 2) + place, 16)
            self.last.append(
                self.start(
                    self.src.at[pl.ds(theirs, block), :],
                    self.recvs[0].at[0, pl.ds(pl.multiple_of(place, 16), block), :],
                    (0, 23, 24, 25)[n], peer(self.at, "core", 1),
                )
            )

    def pass_on(self):
        block = self.block(1)
        arriving, self.last = self.last, []
        for copy, step in zip(arriving, (1, 2, 3, 0)):
            copy.wait_recv()
            place = (self.at[self.order[0]] + step) % 4 * block
            first = pl.multiple_of(self.first(0) + place, 16)
            add_rows(self.src, first, [(self.src, first), (self.recvs[0].at[0], place)], block)
            if step:
                self.last.append(
                    self.start(
                        self.src.at[pl.ds(first, block), :], self.recvs[1].at[step - 1],
                        step, peer(self.at, self.order[0], step),
                    )
                )

    def to_partner(self, step, index):
        block = self.block(1)
        place = (self.at[self.order[0]] + step) % 4 * block
        rows = self.out.at[pl.ds(pl.multiple_of(self.first(0) + place, 16), block), :]
        self.crossed.append(self.start(rows, rows, index, peer(self.at, "core", 1)))

    def cross(self):
        for copy, step in zip(self.last, (3, 2, 1)):
            copy.wait_recv()
            self.to_partner(step, 19 + step)

    def combine(self, level):
        for copy in self.last:
            copy.wait_recv()
        count = self.block(level)
        first = self.first(level)
        terms = [(self.src, first)] + [(self.recvs[level].at[s], 0) for s in range(1 if level == 0 else 3)]
        if level == 3:
            add_rows(self.out, first, terms, count)
            self.gather(3)
            return
        add_rows(self.src, first, terms, count)
        axis = self.order[level]
        block = self.block(level + 1)
        self.last = []
        for step in range(1, 4):
            there = pl.multiple_of(first + (self.at[axis] + step) % 4 * block, 16)
            self.last.append(
                self.start(
                    self.src.at[pl.ds(there, block), :], self.recvs[level + 1].at[step - 1],
                    3 * level + step, peer(self.at, axis, step),
                )
            )

    def gather(self, level):
        mine = self.out.at[pl.ds(self.first(level), self.block(level)), :]
        axis = self.order[level - 1]
        self.last = [
            self.start(mine, mine, 10 + 3 * (level - 1) + step - 1, peer(self.at, axis, step)) for step in range(1, 4)
        ]
        if level == 1:
            self.crossed = []
            self.to_partner(0, 19)

    def gathered(self, level):
        for copy in self.last:
            copy.wait_recv()
        self.gather(level - 1)

    def finish(self):
        for copy in self.crossed:
            copy.wait_recv()
        for copy in self.sent:
            copy.wait_send()

    def step(self, n):
        if n == 0:
            self.begin()
        elif n == 1:
            self.pass_on()
        elif n < 5:
            self.combine(n - 1)
        elif n < 7:
            self.gathered(8 - n)
        elif n == 7:
            self.cross()
        else:
            self.finish()


SUM_COPIES = 30


def sum_scratch(rows, lanes):
    half = rows // 2
    return [pltpu.VMEM((1, half, lanes), BF)] + [pltpu.VMEM((3, half // 4**n, lanes), BF) for n in (1, 2, 3)]


class SmallSum:
    def __init__(self, at, block, slots, send, recv):
        self.at, self.block, self.slots, self.send, self.recv = at, block, slots, send, recv
        self.sent = []

    def begin(self, level):
        axis, count = (("core", 2), ("x", 4), ("y", 4), ("z", 4))[level]
        base = 0 if level == 0 else 3 * level - 2
        self.last = []
        for step in range(1, count):
            i = base + step - 1
            copy = remote(self.block.at[level], self.slots.at[i], self.send.at[i], self.recv.at[i],
                          peer(self.at, axis, step))
            copy.start()
            self.last.append((copy, i))
            self.sent.append(copy)

    def end(self, level):
        total = self.block[level]
        for copy, i in self.last:
            copy.wait_recv()
            total = total + self.slots[i]
        self.block[level + 1] = total

    def finish(self):
        for copy in self.sent:
            copy.wait_send()

CH = 4
NCH = ROWS // CH
MT = (CH // 2) * (COLS // 2)
MALL = NCH * MT
C4 = 4 * C
C2 = 1024
WROWS = ROWS // WLAT
NWT = NW * WIN
FR = COLS + 8
TALL = 4 * C


class Halo:
    def __init__(self, send, recv):
        self.send, self.recv, self.copies = send, recv, []

    def start(self, src, dst, rows, cols):
        n = len(self.copies)
        copy = remote(src, dst, self.send.at[n], self.recv.at[n], neighbour(rows, cols))
        copy.start()
        self.copies.append(copy)
        return copy

    def left(self):
        for copy in self.copies:
            copy.wait_send()


def band_bias(band_ref, bias):
    band = band_ref[...].astype(F32)
    total = band.shape[1]

    def grid_row(place, first):
        row = first + jnp.floor((place.astype(F32) + 0.5) * (1.0 / WLON)).astype(jnp.int32)
        return jnp.where(row >= total, row - total, row)

    for w in range(WROWS):
        first = (lax.axis_index("lat") * ROWS + WLAT * w - 3 + total) % total
        key = lax.broadcasted_iota(jnp.int32, (WIN, total), 0)
        hit = grid_row(key, first) == lax.broadcasted_iota(jnp.int32, (WIN, total), 1)
        keys = jnp.sum(jnp.where(hit, band, 0.0), axis=1, keepdims=True)
        query = lax.broadcasted_iota(jnp.int32, (total, 2 * WIN), 1)
        query = jnp.where(query >= WIN, query - WIN, query)
        hit = grid_row(query, first) == lax.broadcasted_iota(jnp.int32, (total, 2 * WIN), 0)
        queries = dot(jnp.broadcast_to(band, (8, total)).astype(BF), jnp.where(hit, 1.0, 0.0).astype(BF), 1, 0)
        bias[w] = jnp.where(keys == queries[0:1], 0.0, -1e30)


def pair_half(ref, pair, half):
    return ref[pair].astype(F32)[8 * half : 8 * half + 8]


def load_frame(fr, w, rows_ref, edge_ref):
    for r in range(WLAT):
        fr[r, 8:FR, :] = rows_ref[WLAT * w + r].astype(F32)
        fr[r, 0:8, :] = pair_half(edge_ref, 3 * w + (r + 1) // 2, (r + 1) % 2)


def to_windows(fr, dst):
    for v in range(NW):
        for r in range(WLAT):
            dst[v, WLON * r : WLON * (r + 1), :] = fr[r, WLON * v + 2 : WLON * v + 14, :]


def to_frame(src, fr):
    for v in range(NW):
        for r in range(WLAT):
            fr[r, WLON * v + 2 : WLON * v + 14, :] = src[v, WLON * r : WLON * (r + 1), :]


def pack_rows(fr, edge_ref, w):
    for r in range(0, WLAT, 2):
        edge_ref[3 * w + r // 2] = jnp.concatenate([fr[r, 0:8, :], fr[r + 1, 0:8, :]], axis=0).astype(BF)


def step_body(tok_hbm, band_ref, ga_ref, wq_hbm, wo_hbm, gm_hbm, wm_hbm, gmg_ref,
              merged_out, gtok_out, outm_out, outq_out, outs_ref,
              merged_ref, gtok_ref, om0, om1, om2, oq0, oq1, oq2, oq3,
              text, hw, pk, wq, wo, gmb, wm, qkv, prob, qst, nrm, qf, s2, fr, attx, he, bw,
              s1, xh, rs, mi, gi, gw0, gw1, gw2, qo0, qo1, qo2, qo3, gmix, gext, gw, pkg, dq, dall, bn2, bw2, hs2, he2,
              small, slots, ggm, gga, bias, lsem, hsend, hrecv, send, recv, ssend, srecv, *sums):
    loads = [
        pltpu.make_async_copy(src, dst, lsem.at[n])
        for n, (src, dst) in enumerate(
            [(tok_hbm, text.at[pl.ds(3, ROWS)]), (wq_hbm, wq), (wo_hbm, wo), (gm_hbm, gmb), (wm_hbm, wm)]
        )
    ]
    for load in loads:
        load.start()
    at = coordinates()
    greet(at)
    halos = [Halo(hsend.at[n], hrecv.at[n]) for n in range(4)]

    loads[0].wait()

    def pack_tokens(first, count):
        for m in range(first, first + count):
            pk[m] = jnp.concatenate(
                [text[3 + 2 * m + k, 32:48, :].astype(F32)[8:16] for k in range(2)], axis=0
            ).astype(BF)
        return halos[0].start(pk.at[pl.ds(first, count)], hw.at[pl.ds(first + 2, count)], 0, 1)

    north = [halos[0].start(text.at[pl.ds(24, 3)], text.at[pl.ds(0, 3)], 1, 0)]
    west = [pack_tokens(1, 4), pack_tokens(5, 7)]
    north.append(pack_tokens(0, 1))
    north.append(halos[0].start(pk.at[pl.ds(10, 2)], hw.at[pl.ds(0, 2)], 1, 1))
    band_bias(band_ref, bias)
    loads[1].wait()

    def forward_row(w, carry):
        load_frame(fr, w, text, hw)
        xhat, _ = moments(fr[...])
        fr[...] = xhat * ga_ref[...].reshape(1, 1, C)
        to_windows(fr, s2)
        normed = s2[...].reshape(NWT, C).astype(BF)
        nrm[pl.ds(pl.multiple_of(w * NWT, NWT), NWT), :] = normed
        for t in range(3):
            part = dot(normed, wq[:, C * t : C * (t + 1)], 1, 0).reshape(NW, WIN, C)
            if t == 0:
                qf[...] = part
            qkv[pl.ds(NW * w, NW), :, C * t : C * (t + 1)] = part.astype(BF)
        mask = bias[w]

        def window(v, carry):
            masks = head_masks(0.125)
            n = NW * w + v
            scores = []
            for p in range(PAIRS):
                qs = stacked(qf[v, :, 128 * p : 128 * (p + 1)].astype(BF).astype(F32), masks)
                qst[n, p] = qs
                scores.append(dot(qkv[n, :, C + 128 * p : C + 128 * (p + 1)], qs, 1, 1))
            probs = []
            for p in range(PAIRS):
                s = scores[p] + mask
                e = jnp.exp(s - jnp.max(s, axis=0, keepdims=True))
                pr = (e * (1.0 / jnp.sum(e, axis=0, keepdims=True))).astype(BF)
                prob[n, p] = pr
                probs.append(pr)
            for p in range(PAIRS):
                val = qkv[n, :, 2 * C + 128 * p : 2 * C + 128 * (p + 1)]
                s2[v, :, 128 * p : 128 * (p + 1)] = merged_heads(dot(probs[p], val, 0, 0))
            return carry

        lax.fori_loop(0, NW, window, 0)
        to_frame(s2, fr)
        pack_rows(fr, bw, w)
        for r in range(WLAT):
            attx[WLAT * w + r] = fr[r, 8:FR, :].astype(BF)
        return carry

    def send_back(w):
        return halos[1].start(bw.at[pl.ds(3 * w, 3)], he.at[pl.ds(3 * w, 3)], 0, -1)

    west[0].wait_recv()
    lax.fori_loop(1, 2, forward_row, 0)
    east = [send_back(1)]
    for copy in north + west[1:]:
        copy.wait_recv()
    lax.fori_loop(0, 1, forward_row, 0)
    south = [
        halos[1].start(attx.at[pl.ds(0, 3)], attx.at[pl.ds(24, 3)], -1, 0),
        halos[1].start(bw.at[pl.ds(0, 2)], he.at[pl.ds(12, 2)], -1, -1),
    ]
    east.append(send_back(0))
    lax.fori_loop(2, 3, forward_row, 0)
    east.append(send_back(2))
    lax.fori_loop(3, 4, forward_row, 0)
    south.append(send_back(3))
    for load in loads[2:]:
        load.wait()
    for copy in east:
        copy.wait_recv()
    gain = gmg_ref[...]
    lower = lax.broadcasted_iota(jnp.int32, (8, C), 0) < 2

    def merge_forward(c, carry):
        pieces = []
        for i in range(CH):
            row = attx[CH * c + 3 + i].astype(F32)
            edge = pair_half(he, 2 * c + (3 + i) // 2, (3 + i) % 2)
            pieces.append(jnp.concatenate([row[:40], jnp.where(lower, row[40:], edge)], axis=0))
        att = jnp.concatenate(pieces, axis=0).astype(BF)
        attx[pl.ds(CH * c + 3, CH)] = att.reshape(CH, COLS, C)
        proj = dot(att, wo[...], 1, 0).reshape(CH, COLS, C)
        mixed = (text[pl.ds(CH * c + 3, CH)].astype(F32) + proj).astype(BF).astype(F32)
        for q in range(4):
            s1[q] = mixed[:, :, 128 * q : 128 * (q + 1)]
        parts = []
        for b in range(2):
            for a in range(2):
                for q in range(4):
                    piece = [s1[q, 2 * i + a, pl.ds(b, COLS // 2, stride=2), :] for i in range(CH // 2)]
                    parts.append(jnp.concatenate(piece, axis=0))
        xhat, rstd = moments(jnp.concatenate(parts, axis=1))
        here = pl.ds(pl.multiple_of(c * MT, MT), MT)
        xh[here, :] = xhat
        rs[here, :] = rstd
        mi[here, :] = (xhat * gain).astype(BF)
        return carry

    lax.fori_loop(0, 3, merge_forward, 0)
    for copy in south:
        copy.wait_recv()
    lax.fori_loop(3, NCH, merge_forward, 0)
    gm = gmb[...].astype(F32).reshape(MALL, C2).astype(BF)

    def merged_tile(n, carry):
        cols = pl.ds(pl.multiple_of(n * 256, 256), 256)
        tile = dot(mi[...], wm[:, cols], 1, 0).reshape(ROWS // 2, COLS // 2, 256)
        merged_ref[:, :, cols] = tile.astype(BF)
        return carry


    def weight_tile(n, carry):
        cols = pl.ds(pl.multiple_of(n * 256, 256), 256)
        tile = dot(mi[:, cols], gm, 0, 0).astype(BF)
        gw0[cols, :] = tile[:, 0:384]
        gw1[cols, :] = tile[:, 384:768]
        gw2[cols, :] = tile[:, 768:1024]
        return carry

    lax.fori_loop(0, C4 // 256, weight_tile, 0)

    def summed(src, out, turn, n):
        order = AXES[turn:] + AXES[:turn]
        return Sum(at, src, out, order, sums[4 * n : 4 * n + 4], send.at[n], recv.at[n])

    wide = [
        summed(gw0, om0, 0, 0),
        summed(gw1, om1, 1, 1),
        summed(gw2, om2, 2, 2),
    ]
    early = wide + [summed(qo0, oq0, 2, 3)]
    late = [
        summed((qo1, qo2, qo3)[t], (oq1, oq2, oq3)[t], t, 4 + t)
        for t in range(3)
    ]

    def advance(group, n):
        for part in group:
            part.step(n)

    advance(wide, 0)

    def cotangent_tile(n, carry):
        cols = pl.ds(pl.multiple_of(n * 256, 256), 256)
        gi[:, cols] = dot(gm, wm[cols, :], 1, 1).astype(BF)
        return carry

    lax.fori_loop(0, C4 // 256, cotangent_tile, 0)
    ggm[...] = jnp.zeros_like(ggm)

    def merge_backward(c, carry):
        here = pl.ds(pl.multiple_of(c * MT, MT), MT)
        xhat = xh[here, :]
        g = gi[here, :].astype(F32)
        ggm[...] += jnp.sum(g * xhat, axis=0, keepdims=True)
        dx = g * gain
        m1 = jnp.mean(dx, axis=-1, keepdims=True)
        m2 = jnp.mean(dx * xhat, axis=-1, keepdims=True)
        dx = rs[here, :] * (dx - m1 - xhat * m2)
        for b in range(2):
            for a in range(2):
                for q in range(4):
                    start = C * (2 * b + a) + 128 * q
                    for i in range(CH // 2):
                        s1[q, 2 * i + a, pl.ds(b, COLS // 2, stride=2), :] = dx[
                            (COLS // 2) * i : (COLS // 2) * (i + 1), start : start + 128
                        ]
        mixed = jnp.concatenate([s1[q] for q in range(4)], axis=-1).astype(BF)
        gmix[pl.ds(c * CH, CH)] = mixed
        gatt = dot(mixed.reshape(CH * COLS, C), wo[...], 1, 1).reshape(CH, COLS, C)
        gext[pl.ds(CH * c + 3, CH)] = gatt.astype(BF)
        for m in range(CH // 2):
            pkg[(CH // 2) * c + m] = jnp.concatenate(
                [gatt[2 * m, 40:48], gatt[2 * m + 1, 40:48]], axis=0
            ).astype(BF)
        return carry

    def send_cotangents(first, count):
        return halos[2].start(pkg.at[pl.ds(first, count)], gw.at[pl.ds(first + 2, count)], 0, 1)

    lax.fori_loop(5, 6, merge_backward, 0)
    halos[2].start(gext.at[pl.ds(24, 3)], gext.at[pl.ds(0, 3)], 1, 0)
    halos[2].start(pkg.at[pl.ds(10, 2)], gw.at[pl.ds(0, 2)], 1, 1)
    send_cotangents(10, 2)
    lax.fori_loop(0, 3, merge_backward, 0)
    send_cotangents(0, 6)
    lax.fori_loop(3, 5, merge_backward, 0)
    send_cotangents(6, 4)
    flat = gmix[...].reshape(ROWS * COLS, C)
    att = attx[pl.ds(3, ROWS)].reshape(ROWS * COLS, C)
    gwo = dot(att, flat, 0, 0).astype(BF)
    for n in range(4):
        qo0[C * n : C * (n + 1), :] = gwo[:, 128 * n : 128 * (n + 1)]
    early[3].step(0)
    advance(early, 1)
    for copy in halos[2].copies:
        copy.wait_recv()

    def backward_row(w, carry):
        load_frame(fr, w, gext, gw)
        to_windows(fr, s2)

        def window(v, carry):
            masks = head_masks(1.0)
            n = NW * w + v
            cots, dps = [], []
            for p in range(PAIRS):
                gs = stacked(s2[v, :, 128 * p : 128 * (p + 1)], masks)
                cots.append(gs)
                dps.append(dot(qkv[n, :, 2 * C + 128 * p : 2 * C + 128 * (p + 1)], gs, 1, 1))
            for p in range(PAIRS):
                dq[v, :, 2 * C + 128 * p : 2 * C + 128 * (p + 1)] = dot(prob[n, p], cots[p], 1, 0)
            dss = []
            for p in range(PAIRS):
                pf = prob[n, p].astype(F32)
                delta = jnp.sum(pf * dps[p], axis=0, keepdims=True)
                dss.append((pf * (dps[p] - delta)).astype(BF))
            for p in range(PAIRS):
                dq[v, :, C + 128 * p : C + 128 * (p + 1)] = dot(dss[p], qst[n, p], 1, 0)
            for p in range(PAIRS):
                k = qkv[n, :, C + 128 * p : C + 128 * (p + 1)]
                dq[v, :, 128 * p : 128 * (p + 1)] = merged_heads(dot(dss[p], k, 0, 0)) * 0.125
            return carry

        lax.fori_loop(0, NW, window, 0)
        dall[pl.ds(pl.multiple_of(w * NWT, NWT), NWT), :] = dq[...].reshape(NWT, 3 * C).astype(BF)
        return carry

    lax.fori_loop(0, 2, backward_row, 0)
    advance(early, 2)
    lax.fori_loop(2, 4, backward_row, 0)
    advance(early, 3)
    for n in range(6):
        tile = dot(nrm[...], dall[:, 256 * n : 256 * (n + 1)], 0, 0).astype(BF)
        for k in range(2):
            g = 2 * n + k
            (qo1, qo2, qo3)[g % 3][C * (g // 3) : C * (g // 3 + 1), :] = tile[:, 128 * k : 128 * (k + 1)]
    advance(late, 0)
    advance(early, 4)
    gga[...] = jnp.zeros_like(gga)

    def dgrad_row(w, carry):
        rows = pl.ds(pl.multiple_of(w * NWT, NWT), NWT)
        s2[...] = dot(dall[rows, :], wq[...], 1, 1).astype(BF).astype(F32).reshape(NW, WIN, C)
        load_frame(fr, w, text, hw)
        xhat, rstd = moments(fr[...])
        fr[:, 0:8, :] = jnp.zeros((WLAT, 8, C), F32)
        fr[:, FR - 8 : FR, :] = jnp.zeros((WLAT, 8, C), F32)
        to_frame(s2, fr)
        g = fr[...]
        gga[...] += jnp.sum(g * xhat, axis=(0, 1)).reshape(1, C)
        dx = g * ga_ref[...].reshape(1, 1, C)
        m1 = jnp.mean(dx, axis=-1, keepdims=True)
        m2 = jnp.mean(dx * xhat, axis=-1, keepdims=True)
        fr[...] = rstd * (dx - m1 - xhat * m2)
        pack_rows(fr, bw2, w)
        for r in range(3):
            bn2[WLAT * w + r] = fr[r, 8:FR, :].astype(BF)
        for r in range(3):
            gtok_ref[WLAT * w + r] = fr[3 + r, 8:FR, :] + gmix[WLAT * w + r].astype(F32)

        @pl.when(w > 0)
        def _():
            for r in range(3):
                gtok_ref[WLAT * w - 3 + r] = fr[r, 8:FR, :] + gmix[WLAT * w - 3 + r].astype(F32)

        return carry

    lax.fori_loop(0, 1, dgrad_row, 0)
    halos[3].start(bn2.at[pl.ds(0, 3)], hs2, -1, 0)
    halos[3].start(bw2.at[pl.ds(0, 2)], he2.at[pl.ds(12, 2)], -1, -1)
    advance(late, 1)
    lax.fori_loop(1, 2, dgrad_row, 0)
    halos[3].start(bw2.at[pl.ds(0, 6)], he2.at[pl.ds(0, 6)], 0, -1)
    lax.fori_loop(2, 4, dgrad_row, 0)
    halos[3].start(bw2.at[pl.ds(6, 6)], he2.at[pl.ds(6, 6)], 0, -1)
    advance(early, 5)
    lax.fori_loop(0, C2 // 256, merged_tile, 0)
    stores = [
        pltpu.make_async_copy(src, dst, lsem.at[5 + n])
        for n, (src, dst) in enumerate(
            [(merged_ref, merged_out), (gtok_ref, gtok_out)]
            + [(om, outm_out.at[:, 384 * k : 384 * k + om.shape[1]]) for k, om in enumerate((om0, om1, om2))]
            + [(oq, outq_out.at[:, 128 * k : 128 * (k + 1)]) for k, oq in enumerate((oq0, oq1, oq2, oq3))]
        )
    ]
    stores[0].start()
    small[0] = jnp.zeros_like(small[0])
    small[0, 0:1, :] = gga[...]
    for n in range(4):
        small[0, 1 + n : 2 + n, :] = ggm[:, C * n : C * (n + 1)]
    gains = SmallSum(at, small, slots, ssend, srecv)
    gains.begin(0)
    advance(early, 6)
    for copy in halos[3].copies:
        copy.wait_recv()
    for r in range(3):
        gtok_ref[21 + r] = hs2[r].astype(F32) + gmix[21 + r].astype(F32)
    for r in range(ROWS):
        edge = pair_half(he2, (r + 3) // 2, (r + 3) % 2) + gmix[r, 32:48, :].astype(F32)[8:16]
        gtok_ref[r, 40:48, :] = jnp.where(lower, gtok_ref[r, 40:48, :], edge)
    stores[1].start()
    gains.end(0)
    gains.begin(1)
    advance(late, 2)
    gains.end(1)
    gains.begin(2)
    advance(late, 3)
    gains.end(2)
    gains.begin(3)
    advance(late, 4)
    gains.end(3)
    outs_ref[...] = small[4]
    advance(late, 5)
    advance(early, 7)
    advance(late, 6)
    advance(late, 7)
    advance(early, 8)
    for store in stores[2:6]:
        store.start()
    advance(late, 8)
    for store in stores[6:]:
        store.start()
    gains.finish()
    for halo in halos:
        halo.left()
    for store in stores:
        store.wait()


def step_kernel(tokens, band, gain_a, w_qkv, w_out, grad_merged, w_merge, gain_m):
    vmem = pl.BlockSpec(memory_space=pltpu.VMEM)
    hbm = pl.BlockSpec(memory_space=pl.ANY)
    lanes = (384, 384, 256, 128, 128, 128, 128)
    sums = []
    for n in lanes:
        sums += sum_scratch(TALL, n)
    wide = [pltpu.VMEM((TALL, n), BF) for n in lanes]
    return pl.pallas_call(
        step_body,
        in_specs=[hbm, vmem, vmem, hbm, hbm, hbm, hbm, vmem],
        out_specs=[hbm] * 4 + [vmem],
        out_shape=[
            jax.ShapeDtypeStruct((ROWS // 2, COLS // 2, C2), BF),
            jax.ShapeDtypeStruct((ROWS, COLS, C), F32),
            jax.ShapeDtypeStruct((C4, C2), BF),
            jax.ShapeDtypeStruct((TALL, C), BF),
            jax.ShapeDtypeStruct((8, C), F32),
        ],
        scratch_shapes=[
            pltpu.VMEM((ROWS // 2, COLS // 2, C2), BF),
            pltpu.VMEM((ROWS, COLS, C), F32),
            *wide,
            pltpu.VMEM((27, COLS, C), BF),
            pltpu.VMEM((14, 16, C), BF),
            pltpu.VMEM((12, 16, C), BF),
            pltpu.VMEM((C, 3 * C), BF),
            pltpu.VMEM((C, C), BF),
            pltpu.VMEM((ROWS // 2, COLS // 2, C2), BF),
            pltpu.VMEM((C4, C2), BF),
            pltpu.VMEM((WROWS * NW, WIN, 3 * C), BF),
            pltpu.VMEM((WROWS * NW, PAIRS, WIN, 2 * WIN), BF),
            pltpu.VMEM((WROWS * NW, PAIRS, 2 * WIN, 128), BF),
            pltpu.VMEM((ROWS * COLS, C), BF),
            pltpu.VMEM((NW, WIN, C), F32),
            pltpu.VMEM((NW, WIN, C), F32),
            pltpu.VMEM((WLAT, FR, C), F32),
            pltpu.VMEM((27, COLS, C), BF),
            pltpu.VMEM((14, 16, C), BF),
            pltpu.VMEM((12, 16, C), BF),
            pltpu.VMEM((4, CH, COLS, 128), F32),
            pltpu.VMEM((MALL, C4), F32),
            pltpu.VMEM((MALL, 1), F32),
            pltpu.VMEM((MALL, C4), BF),
            pltpu.VMEM((MALL, C4), BF),
            *wide,
            pltpu.VMEM((ROWS, COLS, C), BF),
            pltpu.VMEM((27, COLS, C), BF),
            pltpu.VMEM((14, 16, C), BF),
            pltpu.VMEM((12, 16, C), BF),
            pltpu.VMEM((NW, WIN, 3 * C), F32),
            pltpu.VMEM((ROWS * COLS, 3 * C), BF),
            pltpu.VMEM((21, COLS, C), BF),
            pltpu.VMEM((12, 16, C), BF),
            pltpu.VMEM((3, COLS, C), BF),
            pltpu.VMEM((14, 16, C), BF),
            pltpu.VMEM((5, 8, C), F32),
            pltpu.VMEM((10, 8, C), F32),
            pltpu.VMEM((1, C4), F32),
            pltpu.VMEM((1, C), F32),
            pltpu.VMEM((WROWS, WIN, 2 * WIN), F32),
            pltpu.SemaphoreType.DMA((14,)),
            pltpu.SemaphoreType.DMA((4, 6)),
            pltpu.SemaphoreType.DMA((4, 6)),
            pltpu.SemaphoreType.DMA((7, SUM_COPIES)),
            pltpu.SemaphoreType.DMA((7, SUM_COPIES)),
            pltpu.SemaphoreType.DMA((10,)),
            pltpu.SemaphoreType.DMA((10,)),
        ]
        + sums,
        compiler_params=pltpu.CompilerParams(
            vmem_limit_bytes=62 * MIB, collective_id=0, has_side_effects=True
        ),
        name="step",
    )(tokens, band, gain_a, w_qkv, w_out, grad_merged, w_merge, gain_m)


def widen_body(m_ref, q_ref, s_ref, gm_ref, gq_ref, go_ref, ga_ref, gg_ref):
    gm_ref[...] = m_ref[...].astype(F32)
    go_ref[...] = q_ref[:, 0:128].astype(F32)
    gq_ref[...] = q_ref[:, 128:].astype(F32)
    ga_ref[...] = s_ref[0:1, :]
    for n in range(4):
        gg_ref[:, C * n : C * (n + 1)] = s_ref[1 + n : 2 + n, :]


def widen(sum_merge, sum_qo, sum_gain):
    return pl.pallas_call(
        widen_body,
        grid=(4,),
        in_specs=[
            pl.BlockSpec((C, C2), lambda i: (i, 0)),
            pl.BlockSpec((C, C), lambda i: (i, 0)),
            pl.BlockSpec((8, C), lambda i: (0, 0)),
        ],
        out_specs=[
            pl.BlockSpec((C, C2), lambda i: (i, 0)),
            pl.BlockSpec((C, 384), lambda i: (0, i)),
            pl.BlockSpec((C, 128), lambda i: (0, i)),
            pl.BlockSpec((1, C), lambda i: (0, 0)),
            pl.BlockSpec((1, C4), lambda i: (0, 0)),
        ],
        out_shape=[
            jax.ShapeDtypeStruct((C4, C2), F32),
            jax.ShapeDtypeStruct((C, 3 * C), F32),
            jax.ShapeDtypeStruct((C, C), F32),
            jax.ShapeDtypeStruct((1, C), F32),
            jax.ShapeDtypeStruct((1, C4), F32),
        ],
        compiler_params=pltpu.CompilerParams(vmem_limit_bytes=60 * MIB),
        name="widen",
    )(sum_merge, sum_qo, sum_gain)


def on_device(tokens, lat_band, gain_attn, w_qkv, w_out, gain_merge, w_merge, grad_merged):
    merged, grad_tokens, sum_merge, sum_qo, sum_gain = step_kernel(
        tokens, lat_band.reshape(1, -1), gain_attn.reshape(1, C), w_qkv, w_out, grad_merged, w_merge,
        gain_merge.reshape(1, C4)
    )
    gw_merge, gw_qkv, gw_out, gg_attn, gg_merge = widen(sum_merge, sum_qo, sum_gain)
    return merged, grad_tokens, gg_attn.reshape(C), gw_qkv, gw_out, gg_merge.reshape(C4), gw_merge


def solution(mesh):
    return jax.shard_map(
        on_device,
        mesh=mesh,
        in_specs=(P("lat", "lon", None), P(), P(), P(), P(), P(), P(), P("lat", "lon", None)),
        out_specs=(P("lat", "lon", None), P("lat", "lon", None), P(), P(), P(), P(), P()),
        check_vma=False,
    )
```
